32 devices in a mesh: dp: 8 (over y, x, core), mp: 4 (over z).
Axes of the slice: x: 2, y: 2, z: 4, core: 2. Of those that a mesh axis runs over, the one named last changes fastest.
Arguments:
- tokens: bfloat16 [8, 2048, 768], P('dp', 'mp'), may hold values from -6 to 6
- gain_first: float32 [768], replicated, may hold values from 0.5 to 1.5
- input_weight: bfloat16 [768, 3, 768], P(None, None, 'mp'), may hold values from -0.21875 to 0.21875
- kernel: float32 [768, 2048], P('mp'), may hold values from -0.25 to 0.25
- pad_len: int32 [768], P('mp'), may hold values from 0 to 1023
- output_weight: bfloat16 [768, 768], P('mp'), may hold values from -0.21875 to 0.21875
- gain_second: float32 [768], replicated, may hold values from 0.5 to 1.5
- up_weight: bfloat16 [768, 3072], P(None, 'mp'), may hold values from -0.21875 to 0.21875
- down_weight: bfloat16 [3072, 768], P('mp'), may hold values from -0.109375 to 0.109375
- cotangent: bfloat16 [8, 2048, 768], P('dp', 'mp'), may hold values from -6 to 6
Outputs:
- block_out: bfloat16 [8, 2048, 768], P('dp', 'mp')
- grad_tokens: float32 [8, 2048, 768], P('dp', 'mp')
- grad_gain_first: float32 [768], replicated
- grad_w_in: float32 [768, 3, 768], P(None, None, 'mp')
- grad_kernel: float32 [768, 2048], P('mp')
- grad_w_out: float32 [768, 768], P('mp')
- grad_gain_second: float32 [768], replicated
- grad_w_up: float32 [768, 3072], P(None, 'mp')
- grad_w_down: float32 [3072, 768], P('mp')
The draws below stay inside these ranges and needn't reach their ends.
All inputs are finite; a program needn't handle non-finite values.
Results may differ from the reference program's by a relative error of at most 0.008.
Values may be sent and summed in bfloat16 or wider, within the bound.
No kernel may reach another device: no remote copies, remote signals or barrier semaphores. Data moves between devices by JAX's collectives and lax.ppermute only.
A program may use at most 640 MiB of HBM per device.

```python
import jax
import jax.numpy as jnp
from jax import lax

D = 768
FF = 3072
KLEN = 2048
LEN = 2048
BATCH = 8


def set_ends(drawn, own_key, smallest, top_value):
    dims = drawn.shape
    index_at = [jax.random.randint(jax.random.fold_in(own_key, axis), (), 0, dims[axis]) for axis in range(len(dims))]
    drawn = drawn.at[tuple(index_at)].set(smallest)
    longest = dims.index(max(dims))
    index_at[longest] = (index_at[longest] + 1) % dims[longest]
    return drawn.at[tuple(index_at)].set(top_value)


def shard_levels(key, shape, cuts, low, top_value):
    gain = 1.0
    for axis_at, blocks in cuts:
        steps = jax.random.uniform(jax.random.fold_in(jax.random.fold_in(key, 6), axis_at), (blocks,), jnp.float32, low / len(cuts), top_value / len(cuts))
        gain = gain * jnp.repeat(jnp.exp(steps), shape[axis_at] // blocks).reshape((-1,) + (1,) * (len(shape) - 1 - axis_at))
    return gain


def noise(stream_key, extent, width, bound, cuts=(), dtype=jnp.bfloat16):
    factor_of = shard_levels(stream_key, extent, cuts, -0.22, 0.18) if cuts else 1.0
    array = jax.random.normal(stream_key, extent, jnp.float32) * width * factor_of
    return jnp.minimum(jnp.maximum(array, -bound), bound).astype(dtype)


def setup_inputs(seed: int = 0) -> dict:
    arg_keys = jax.random.split(jax.random.key(seed), 11)
    tokens = noise(arg_keys[0], (BATCH, LEN, D), 1.0, 6.0, ((0, 8), (1, 4)))
    gain_first = jnp.clip(1.0 + 0.1 * jax.random.normal(arg_keys[1], (D,), jnp.float32), 0.5, 1.5)
    input_weight = noise(arg_keys[2], (D, 3, D), D ** -0.5, 0.21875, ((2, 4),))
    kernel = noise(arg_keys[3], (D, KLEN), 0.035, 0.25, ((0, 4),), jnp.float32)
    pad_len = set_ends(jax.random.randint(arg_keys[4], (D,), 0, KLEN // 2), jax.random.fold_in(arg_keys[4], 1), 0, (KLEN // 2) - 1).astype(jnp.int32)
    output_weight = noise(arg_keys[5], (D, D), D ** -0.5, 0.21875, ((0, 4),))
    gain_second = jnp.clip(1.0 + 0.1 * jax.random.normal(arg_keys[6], (D,), jnp.float32), 0.5, 1.5)
    up_weight = noise(arg_keys[7], (D, FF), D ** -0.5, 0.21875, ((1, 4),))
    down_weight = noise(arg_keys[8], (FF, D), FF ** -0.5, 0.109375, ((0, 4),))
    cotangent = noise(arg_keys[9], (BATCH, LEN, D), 1.0, 6.0, ((0, 8), (1, 4)))
    return dict(tokens=tokens, gain_first=gain_first, input_weight=input_weight, kernel=kernel, pad_len=pad_len, output_weight=output_weight, gain_second=gain_second, up_weight=up_weight, down_weight=down_weight, cotangent=cotangent)


@jax.custom_vjp
def low(v):
    return lax.optimization_barrier(v.astype(jnp.bfloat16)).astype(jnp.float32)

@jax.custom_vjp
def low_back(v):
    return v

def low_keep(v):
    return (low(v), None)

def low_pass(kept, grad):
    return (grad,)

def back_keep(v):
    return (v, None)

def back_low(kept, grad):
    return (low(grad),)
low.defvjp(low_keep, low_pass)
low_back.defvjp(back_keep, back_low)
thresh = 0.003
epsilon = 1e-05

def layer_norm(values, scale_vec):
    centered = values - lax.optimization_barrier(jnp.mean(values, axis=-1, keepdims=True))
    spread = lax.optimization_barrier(jnp.mean(centered * centered, axis=-1, keepdims=True))
    return centered * lax.rsqrt(spread + epsilon) * scale_vec

def shrink_pool(kernel, pad_len):
    shrunk = jax.nn.relu(kernel - thresh) - jax.nn.relu(-kernel - thresh)
    padded = jnp.pad(shrunk, ((0, 0), (1, 1)))
    pooled = (padded[:, :-2] + padded[:, 1:-1] + padded[:, 2:]) / 3.0
    positions = lax.broadcasted_iota(jnp.int32, pooled.shape, 1)
    return jnp.where(positions < (pooled.shape[1] - pad_len)[:, None], pooled, 0.0)

def long_conv(mixed_in, filt):
    length = mixed_in.shape[0]
    total_len = length + filt.shape[1]
    spec_in = jnp.fft.rfft(mixed_in, n=total_len, axis=0)
    spec_filt = jnp.fft.rfft(filt.T, n=total_len, axis=0)
    return jnp.fft.irfft(spec_in * spec_filt, n=total_len, axis=0)[:length]

def forward_seq(sequence, gain_first, input_weight, kernel, output_weight, gain_second, up_weight, down_weight, pad_len):
    highest = lax.Precision.HIGHEST
    normed_one = low(layer_norm(sequence, gain_first))
    projected_input = low_back(jnp.einsum('ld,dkc->lkc', normed_one, input_weight, precision=highest))
    filt = shrink_pool(kernel, pad_len)
    conv = long_conv(projected_input[:, 1] * projected_input[:, 0], filt)
    mixer_out = low(projected_input[:, 2] * conv)
    branch_out = low_back(jnp.dot(mixer_out, output_weight, precision=highest))
    residual_one = sequence + branch_out
    normed_two = low(layer_norm(residual_one, gain_second))
    hidden_preactivation = low_back(jnp.dot(normed_two, up_weight, precision=highest))
    hidden_act = low(jax.nn.gelu(hidden_preactivation, approximate=True))
    return residual_one + jnp.dot(hidden_act, down_weight, precision=highest)

def reference(tokens, gain_first, input_weight, kernel, pad_len, output_weight, gain_second, up_weight, down_weight, cotangent):
    weights = (gain_first.astype(jnp.float32), input_weight.astype(jnp.float32), kernel.astype(jnp.float32), output_weight.astype(jnp.float32), gain_second.astype(jnp.float32), up_weight.astype(jnp.float32), down_weight.astype(jnp.float32))

    def per_sequence(running, inputs_pair):
        sequence, grad_seq = inputs_pair

        def forward_one(seq_in, g_one, w_a, k_raw, w_b, g_two, w_c, w_d):
            return forward_seq(seq_in, g_one, w_a, k_raw, w_b, g_two, w_c, w_d, pad_len)
        seq_out, pullback = jax.vjp(forward_one, sequence.astype(jnp.float32), *weights)
        grad_all = pullback(grad_seq.astype(jnp.float32))
        updated = tuple((acc_item + grad_item for acc_item, grad_item in zip(running, grad_all[1:])))
        return (updated, (seq_out.astype(jnp.bfloat16), grad_all[0]))
    zeros_all = tuple((jnp.zeros_like(weight_item) for weight_item in weights))
    totals, (block_out, grad_tokens) = lax.scan(per_sequence, zeros_all, (tokens, cotangent))
    return (block_out, grad_tokens, totals[0], totals[1], totals[2], totals[3], totals[4], totals[5], totals[6])
```

```python
import math
from functools import partial

import jax
import jax.numpy as jnp
import numpy as np
from jax import lax
from jax.experimental import pallas as pl
from jax.experimental.pallas import tpu as pltpu
from jax.sharding import PartitionSpec as P

LANES = 128
ROWS = 16
BASE = 256
f32 = jnp.float32
bf16 = jnp.bfloat16


def dft_tables(length):
    radix = length // BASE
    spot = np.arange(BASE)
    angle = 2 * np.pi * (np.outer(spot, spot) % BASE) / BASE
    cos, sin = np.cos(angle), np.sin(angle)
    matrix = np.block([[cos, -sin], [sin, cos]]).astype(np.float32)
    high = matrix.astype(jnp.bfloat16)
    low = (matrix - high.astype(np.float32)).astype(jnp.bfloat16)
    turn = 2 * np.pi * np.outer(np.arange(radix) + 0.25, spot) / length
    twiddle = np.stack([np.cos(turn), np.sin(turn)]).astype(np.float32)
    return high, low, twiddle


def times(re, im, angle):
    c, s = math.cos(angle), math.sin(angle)
    if abs(s) < 1e-12:
        return (re, im) if c > 0 else (-re, -im)
    if abs(c) < 1e-12:
        return (-im, re) if s > 0 else (im, -re)
    if abs(abs(c) - abs(s)) < 1e-12:
        a = abs(c)
        sc, ss = (a if c > 0 else -a), (1.0 if (s > 0) == (c > 0) else -1.0)
        if ss > 0:
            return (re - im) * sc, (re + im) * sc
        return (re + im) * sc, (im - re) * sc
    return re * c - im * s, re * s + im * c


def radix_dft(re, im, sign):
    n = len(re)
    if n == 1:
        return re, im
    er, ei = radix_dft(re[0::2], im[0::2], sign)
    odr, odi = radix_dft(re[1::2], im[1::2], sign)
    lo_r, lo_i, hi_r, hi_i = [], [], [], []
    for k in range(n // 2):
        tr, ti = times(odr[k], odi[k], sign * 2 * math.pi * k / n)
        lo_r.append(er[k] + tr)
        lo_i.append(ei[k] + ti)
        hi_r.append(er[k] - tr)
        hi_i.append(ei[k] - ti)
    return lo_r + hi_r, lo_i + hi_i


def split_in(load, twiddle_ref, store, radix, channels):
    def step(tile, carry):
        rows = pl.ds(pl.multiple_of(tile * ROWS, ROWS), ROWS)
        for half in range(BASE // LANES):
            lanes = slice(half * LANES, (half + 1) * LANES)
            re, im = [], []
            for block in range(radix):
                x = load(rows, block, half)
                angle = -2 * math.pi * block * 0.25 / radix
                re.append(x * math.cos(angle))
                im.append(x * math.sin(angle))
            re, im = radix_dft(re, im, -1)
            for k in range(radix):
                c = twiddle_ref[0, k : k + 1, lanes]
                s = twiddle_ref[1, k : k + 1, lanes]
                store(rows, k, half, re[k] * c + im[k] * s, im[k] * c - re[k] * s)
        return carry

    lax.fori_loop(0, channels // ROWS, step, 0)


def split_out(load, twiddle_ref, store, radix, channels, length):
    def step(tile, carry):
        rows = pl.ds(pl.multiple_of(tile * ROWS, ROWS), ROWS)
        for half in range(BASE // LANES):
            lanes = slice(half * LANES, (half + 1) * LANES)
            re, im = [], []
            for k in range(radix):
                vr, vi = load(rows, k, half)
                c = twiddle_ref[0, k : k + 1, lanes]
                s = twiddle_ref[1, k : k + 1, lanes]
                re.append(vr * c - vi * s)
                im.append(vr * s + vi * c)
            re, im = radix_dft(re, im, 1)
            for block in range(radix):
                angle = 2 * math.pi * block * 0.25 / radix
                store(
                    rows,
                    block,
                    half,
                    re[block] * (math.cos(angle) / length) - im[block] * (math.sin(angle) / length),
                )
        return carry

    lax.fori_loop(0, channels // ROWS, step, 0)


def forward_dot(z, matrix):
    return jnp.dot(z, matrix, preferred_element_type=f32)


def inverse_dot(y, matrix):
    return lax.dot_general(y, matrix, (((1,), (1,)), ((), ())), preferred_element_type=f32)


def product_loop(a_load, b_load, store, total_rows, conj):
    def step(tile, carry):
        rows = pl.ds(pl.multiple_of(tile * ROWS, ROWS), ROWS)
        for half in range(BASE // LANES):
            cr = slice(half * LANES, (half + 1) * LANES)
            ci = slice(BASE + half * LANES, BASE + (half + 1) * LANES)
            ar, ai = a_load(rows, cr), a_load(rows, ci)
            br, bi = b_load(rows, cr), b_load(rows, ci)
            if conj:
                store(rows, cr, ar * br + ai * bi)
                store(rows, ci, ai * br - ar * bi)
            else:
                store(rows, cr, ar * br - ai * bi)
                store(rows, ci, ai * br + ar * bi)
        return carry

    lax.fori_loop(0, total_rows // ROWS, step, 0)


def cut(ref, rows, block, half):
    width = ref.shape[-1]
    start = block * BASE + half * LANES
    return ref[start // width, rows, start % width : start % width + LANES]


def put(ref, rows, block, half, value):
    width = ref.shape[-1]
    start = block * BASE + half * LANES
    ref[start // width, rows, start % width : start % width + LANES] = value.astype(ref.dtype)


def rowshift(rows, k, channels):
    return pl.ds(pl.multiple_of(rows.start + k * channels, ROWS), ROWS)


def into_scratch(ref, channels):
    def store(rows, k, half, re, im):
        at = rowshift(rows, k, channels)
        ref[at, half * LANES : (half + 1) * LANES] = re.astype(ref.dtype)
        ref[at, BASE + half * LANES : BASE + (half + 1) * LANES] = im.astype(ref.dtype)

    return store


def from_scratch(ref, channels):
    def load(rows, k, half):
        at = rowshift(rows, k, channels)
        return (
            ref[at, half * LANES : (half + 1) * LANES].astype(f32),
            ref[at, BASE + half * LANES : BASE + (half + 1) * LANES].astype(f32),
        )

    return load


def filter_kernel(f_ref, high_ref, low_ref, twiddle_ref, spec_ref, zh, zl, *, radix, channels):
    def store(rows, k, half, re, im):
        at = rowshift(rows, k, channels)
        for value, base in ((re, 0), (im, BASE)):
            lanes = slice(base + half * LANES, base + (half + 1) * LANES)
            top = value.astype(bf16)
            zh[at, lanes] = top
            zl[at, lanes] = (value - top.astype(f32)).astype(bf16)

    split_in(partial(cut, f_ref), twiddle_ref, store, radix, channels)
    spec_ref[...] = (
        forward_dot(zh[...], high_ref[...])
        + forward_dot(zl[...], high_ref[...])
        + forward_dot(zh[...], low_ref[...])
    )


def tile_load(ref):
    return lambda rows, lanes: ref[rows, lanes].astype(f32)


def tile_store(ref):
    def store(rows, lanes, value):
        ref[rows, lanes] = value.astype(ref.dtype)

    return store


def conv_kernel(
    u_ref, fspec_ref, high_ref, twiddle_ref, out_ref, uspec_ref, z, y, big, *, radix, channels, length
):
    load = lambda rows, block, half: cut(u_ref, rows, block, half).astype(f32)
    split_in(load, twiddle_ref, into_scratch(z, channels), radix, channels)
    big[...] = forward_dot(z[...], high_ref[...])
    uspec_ref[...] = big[...].astype(uspec_ref.dtype)
    product_loop(tile_load(big), tile_load(fspec_ref), tile_store(y), radix * channels, False)
    big[...] = inverse_dot(y[...], high_ref[...])
    split_out(from_scratch(big, channels), twiddle_ref, partial(put, out_ref), radix, channels, length)


def conv_back_kernel(
    g_ref, fspec_ref, uspec_ref, high_ref, twiddle_ref, mixed_ref, filt_ref, z, y, big, spec, *, radix, channels, length
):
    load = lambda rows, block, half: cut(g_ref, rows, block, half).astype(f32)
    split_in(load, twiddle_ref, into_scratch(z, channels), radix, channels)
    spec[...] = forward_dot(z[...], high_ref[...])
    product_loop(tile_load(spec), tile_load(fspec_ref), tile_store(y), radix * channels, True)
    big[...] = inverse_dot(y[...], high_ref[...])
    split_out(from_scratch(big, channels), twiddle_ref, partial(put, mixed_ref), radix, channels, length)
    product_loop(tile_load(spec), tile_load(uspec_ref), tile_store(y), radix * channels, True)
    big[...] = inverse_dot(y[...], high_ref[...])
    split_out(from_scratch(big, channels), twiddle_ref, partial(put, filt_ref), radix, channels, length)


VM = pl.BlockSpec(memory_space=pltpu.VMEM)


def filter_spectrum(filt, tables):
    high, low, twiddle = tables
    channels, length = filt.shape[1], filt.shape[0] * filt.shape[2]
    radix = length // BASE
    rows = radix * channels
    return pl.pallas_call(
        partial(filter_kernel, radix=radix, channels=channels),
        out_shape=jax.ShapeDtypeStruct((rows, 2 * BASE), f32),
        in_specs=[VM] * 4,
        out_specs=VM,
        scratch_shapes=[pltpu.VMEM((rows, 2 * BASE), bf16)] * 2,
        name="filter_spectrum",
    )(filt, high, low, twiddle)


def conv_forward(u, fspec, tables, out_dtype):
    high, _, twiddle = tables
    parts, channels, width = u.shape
    length = parts * width
    radix = length // BASE
    rows = radix * channels
    return pl.pallas_call(
        partial(conv_kernel, radix=radix, channels=channels, length=length),
        out_shape=(
            jax.ShapeDtypeStruct((parts, channels, width), out_dtype),
            jax.ShapeDtypeStruct((rows, 2 * BASE), bf16),
        ),
        in_specs=[VM] * 4,
        out_specs=(VM, VM),
        scratch_shapes=[pltpu.VMEM((rows, 2 * BASE), bf16)] * 2 + [pltpu.VMEM((rows, 2 * BASE), f32)],
        name="conv_forward",
    )(u, fspec, high, twiddle)


def conv_backward(g, fspec, uspec, tables, out_dtype, filt_dtype):
    high, _, twiddle = tables
    parts, channels, width = g.shape
    length = parts * width
    radix = length // BASE
    rows = radix * channels
    return pl.pallas_call(
        partial(conv_back_kernel, radix=radix, channels=channels, length=length),
        out_shape=(
            jax.ShapeDtypeStruct((parts, channels, width), out_dtype),
            jax.ShapeDtypeStruct((1, channels, length), filt_dtype),
        ),
        in_specs=[VM] * 5,
        out_specs=(VM, VM),
        scratch_shapes=[pltpu.VMEM((rows, 2 * BASE), bf16)] * 2 + [pltpu.VMEM((rows, 2 * BASE), f32)] * 2,
        name="conv_backward",
    )(g, fspec, uspec, high, twiddle)


thresh = 0.003
epsilon = 1e-05


def layer_norm(values, scale_vec):
    centered = values - jnp.mean(values, axis=-1, keepdims=True)
    spread = jnp.mean(centered * centered, axis=-1, keepdims=True)
    return centered * lax.rsqrt(spread + epsilon) * scale_vec


def gelu_tanh(values):
    return jax.nn.gelu(values, approximate=True)


def shrink_pool(kernel, pad_len):
    shrunk = jax.nn.relu(kernel - thresh) - jax.nn.relu(-kernel - thresh)
    padded = jnp.pad(shrunk, ((0, 0), (1, 1)))
    pooled = (padded[:, :-2] + padded[:, 1:-1] + padded[:, 2:]) / 3.0
    positions = lax.broadcasted_iota(jnp.int32, pooled.shape, 1)
    return jnp.where(positions < (pooled.shape[1] - pad_len)[:, None], pooled, 0.0)


def body(
    tables,
    tokens,
    gain_first,
    input_weight,
    kernel,
    pad_len,
    output_weight,
    gain_second,
    up_weight,
    down_weight,
    cotangent,
):
    start_rows = tokens.astype(f32)
    filt, filter_back = jax.vjp(partial(shrink_pool, pad_len=pad_len), kernel)
    seqs = tokens.shape[0]
    length = tokens.shape[1] * lax.axis_size("mp")
    fspec = filter_spectrum(jnp.pad(filt, ((0, 0), (0, length - filt.shape[1])))[None], tables)
    normed_one, first_back = jax.vjp(layer_norm, start_rows, gain_first)
    normed_low = normed_one.astype(bf16)
    whole = lax.all_gather(normed_low, "mp", axis=1, tiled=True)
    proj = jnp.einsum("spd,dkc->skcp", whole, input_weight, preferred_element_type=f32)
    value, gate_one, gate_two = proj[:, 0], proj[:, 1], proj[:, 2]
    mixed_in = (value * gate_one).astype(bf16)
    conv_runs = [conv_forward(mixed_in[s][None], fspec, tables, f32) for s in range(seqs)]
    conv = jnp.stack([run[0][0] for run in conv_runs])
    mixer_low = (gate_two * conv).astype(bf16)
    partial_rows = jnp.einsum("scp,cd->spd", mixer_low, output_weight, preferred_element_type=f32)
    mixer_sum = lax.psum_scatter(partial_rows.astype(bf16), "mp", scatter_dimension=1, tiled=True)
    residual_one = start_rows + mixer_sum.astype(f32)
    normed_two, second_back = jax.vjp(layer_norm, residual_one, gain_second)
    second_low = normed_two.astype(bf16)
    second_whole = lax.all_gather(second_low, "mp", axis=1, tiled=True)
    grad_whole = lax.all_gather(cotangent, "mp", axis=1, tiled=True)
    hidden_pre = jnp.einsum("spd,df->spf", second_whole, up_weight, preferred_element_type=f32)
    hidden_act, act_back = jax.vjp(gelu_tanh, hidden_pre)
    act_low = hidden_act.astype(bf16)
    down_terms = jnp.einsum("spf,fd->spd", act_low, down_weight, preferred_element_type=f32)
    block_out = residual_one + lax.psum_scatter(
        down_terms.astype(bf16), "mp", scatter_dimension=1, tiled=True
    ).astype(f32)
    grad_act = jnp.einsum("spd,fd->spf", grad_whole, down_weight, preferred_element_type=f32)
    grad_pre = act_back(grad_act)[0].astype(bf16)
    norm_terms = jnp.einsum("spf,df->spd", grad_pre, up_weight, preferred_element_type=f32)
    grad_norm_two = lax.psum_scatter(
        norm_terms.astype(bf16), "mp", scatter_dimension=1, tiled=True
    ).astype(f32)
    up_grad = jnp.einsum("spd,spf->df", second_whole, grad_pre, preferred_element_type=f32)
    down_grad = jnp.einsum("spf,spd->fd", act_low, grad_whole, preferred_element_type=f32)
    grad_mid_norm, gain_second_grad = second_back(grad_norm_two)
    grad_mid = cotangent.astype(f32) + grad_mid_norm
    mid_whole = lax.all_gather(grad_mid.astype(bf16), "mp", axis=1, tiled=True)
    w_out_grad = jnp.einsum("scp,spd->cd", mixer_low, mid_whole, preferred_element_type=f32)
    grad_mixer = jnp.einsum("spd,cd->scp", mid_whole, output_weight, preferred_element_type=f32)
    grad_conv = (grad_mixer * gate_two).astype(bf16)
    back_runs = [
        conv_backward(grad_conv[s][None], fspec, conv_runs[s][1], tables, f32, f32) for s in range(seqs)
    ]
    grad_mixed = jnp.stack([run[0][0] for run in back_runs])
    filt_grad = sum(run[1][0] for run in back_runs)[:, : kernel.shape[1]]
    (kernel_grad,) = filter_back(filt_grad)
    proj_grad = jnp.stack(
        [grad_mixed * gate_one, grad_mixed * value, grad_mixer * conv], axis=1
    ).astype(bf16)
    w_in_grad = jnp.einsum("spd,skcp->dkc", whole, proj_grad, preferred_element_type=f32)
    first_terms = jnp.einsum("skcp,dkc->spd", proj_grad, input_weight, preferred_element_type=f32)
    grad_norm_one = lax.psum_scatter(
        first_terms.astype(bf16), "mp", scatter_dimension=1, tiled=True
    ).astype(f32)
    grad_start, gain_first_grad = first_back(grad_norm_one)
    grad_tokens = grad_mid + grad_start
    weight_sums = lax.psum((w_in_grad, kernel_grad, w_out_grad, up_grad, down_grad), "dp")
    gain_sums = lax.psum((gain_first_grad, gain_second_grad), ("dp", "mp"))
    return (
        block_out.astype(bf16),
        grad_tokens,
        gain_sums[0],
        weight_sums[0],
        weight_sums[1],
        weight_sums[2],
        gain_sums[1],
        weight_sums[3],
        weight_sums[4],
    )


def solution(mesh):
    in_specs = (
        P("dp", "mp", None),
        P(),
        P(None, None, "mp"),
        P("mp", None),
        P("mp"),
        P("mp", None),
        P(),
        P(None, "mp"),
        P("mp", None),
        P("dp", "mp", None),
    )
    out_specs = (
        P("dp", "mp", None),
        P("dp", "mp", None),
        P(),
        P(None, None, "mp"),
        P("mp", None),
        P("mp", None),
        P(),
        P(None, "mp"),
        P("mp", None),
    )

    def program(tokens, *rest):
        tables = tuple(jnp.asarray(t) for t in dft_tables(tokens.shape[1]))
        inner = jax.shard_map(
            body, mesh=mesh, in_specs=((P(), P(), P()),) + in_specs, out_specs=out_specs, check_vma=False
        )
        return inner(tables, tokens, *rest)

    return program
```

```python
import math
from functools import partial

import jax
import jax.numpy as jnp
import numpy as np
from jax import lax
from jax.experimental import pallas as pl
from jax.experimental.pallas import tpu as pltpu
from jax.sharding import PartitionSpec as P

LANES = 128
ROWS = 16
BASE = 256
f32 = jnp.float32
bf16 = jnp.bfloat16


def dft_tables(length):
    radix = length // BASE
    spot = np.arange(BASE)
    angle = 2 * np.pi * (np.outer(spot, spot) % BASE) / BASE
    cos, sin = np.cos(angle), np.sin(angle)
    matrix = np.block([[cos, -sin], [sin, cos]]).astype(np.float32)
    high = matrix.astype(jnp.bfloat16)
    low = (matrix - high.astype(np.float32)).astype(jnp.bfloat16)
    turn = 2 * np.pi * np.outer(np.arange(radix) + 0.25, spot) / length
    twiddle = np.stack([np.cos(turn), np.sin(turn)]).astype(np.float32)
    return high, low, twiddle


def times(re, im, angle):
    c, s = math.cos(angle), math.sin(angle)
    if abs(s) < 1e-12:
        return (re, im) if c > 0 else (-re, -im)
    if abs(c) < 1e-12:
        return (-im, re) if s > 0 else (im, -re)
    if abs(abs(c) - abs(s)) < 1e-12:
        a = abs(c)
        sc, ss = (a if c > 0 else -a), (1.0 if (s > 0) == (c > 0) else -1.0)
        if ss > 0:
            return (re - im) * sc, (re + im) * sc
        return (re + im) * sc, (im - re) * sc
    return re * c - im * s, re * s + im * c


def radix_dft(re, im, sign):
    n = len(re)
    if n == 1:
        return re, im
    er, ei = radix_dft(re[0::2], im[0::2], sign)
    odr, odi = radix_dft(re[1::2], im[1::2], sign)
    lo_r, lo_i, hi_r, hi_i = [], [], [], []
    for k in range(n // 2):
        tr, ti = times(odr[k], odi[k], sign * 2 * math.pi * k / n)
        lo_r.append(er[k] + tr)
        lo_i.append(ei[k] + ti)
        hi_r.append(er[k] - tr)
        hi_i.append(ei[k] - ti)
    return lo_r + hi_r, lo_i + hi_i


def split_in(load, twiddle_ref, store, radix, channels):
    def step(tile, carry):
        rows = pl.ds(pl.multiple_of(tile * ROWS, ROWS), ROWS)
        for half in range(BASE // LANES):
            lanes = slice(half * LANES, (half + 1) * LANES)
            re, im = [], []
            for block in range(radix):
                x = load(rows, block, half)
                angle = -2 * math.pi * block * 0.25 / radix
                re.append(x * math.cos(angle))
                im.append(x * math.sin(angle))
            re, im = radix_dft(re, im, -1)
            for k in range(radix):
                c = twiddle_ref[0, k : k + 1, lanes]
                s = twiddle_ref[1, k : k + 1, lanes]
                store(rows, k, half, re[k] * c + im[k] * s, im[k] * c - re[k] * s)
        return carry

    lax.fori_loop(0, channels // ROWS, step, 0)


def split_out(load, twiddle_ref, store, radix, channels, length):
    def step(tile, carry):
        rows = pl.ds(pl.multiple_of(tile * ROWS, ROWS), ROWS)
        for half in range(BASE // LANES):
            lanes = slice(half * LANES, (half + 1) * LANES)
            re, im = [], []
            for k in range(radix):
                vr, vi = load(rows, k, half)
                c = twiddle_ref[0, k : k + 1, lanes]
                s = twiddle_ref[1, k : k + 1, lanes]
                re.append(vr * c - vi * s)
                im.append(vr * s + vi * c)
            re, im = radix_dft(re, im, 1)
            for block in range(radix):
                angle = 2 * math.pi * block * 0.25 / radix
                store(
                    rows,
                    block,
                    half,
                    re[block] * (math.cos(angle) / length) - im[block] * (math.sin(angle) / length),
                )
        return carry

    lax.fori_loop(0, channels // ROWS, step, 0)


def forward_dot(z, matrix):
    return jnp.dot(z, matrix, preferred_element_type=f32)


def inverse_dot(y, matrix):
    return lax.dot_general(y, matrix, (((1,), (1,)), ((), ())), preferred_element_type=f32)


def product_loop(a_load, b_load, store, total_rows, conj):
    def step(tile, carry):
        rows = pl.ds(pl.multiple_of(tile * ROWS, ROWS), ROWS)
        for half in range(BASE // LANES):
            cr = slice(half * LANES, (half + 1) * LANES)
            ci = slice(BASE + half * LANES, BASE + (half + 1) * LANES)
            ar, ai = a_load(rows, cr), a_load(rows, ci)
            br, bi = b_load(rows, cr), b_load(rows, ci)
            if conj:
                store(rows, cr, ar * br + ai * bi)
                store(rows, ci, ai * br - ar * bi)
            else:
                store(rows, cr, ar * br - ai * bi)
                store(rows, ci, ai * br + ar * bi)
        return carry

    lax.fori_loop(0, total_rows // ROWS, step, 0)


def cut(ref, here, rows, block, half):
    width = ref.shape[-1]
    start = block * BASE + half * LANES
    return ref[(start // width) ^ here, rows, start % width : start % width + LANES].astype(f32)


def put(ref, here, rows, block, half, value):
    width = ref.shape[-1]
    start = block * BASE + half * LANES
    ref[(start // width) ^ here, rows, start % width : start % width + LANES] = value.astype(ref.dtype)


def rowshift(rows, k, channels):
    return pl.ds(pl.multiple_of(rows.start + k * channels, ROWS), ROWS)


def into_scratch(ref, channels):
    def store(rows, k, half, re, im):
        at = rowshift(rows, k, channels)
        ref[at, half * LANES : (half + 1) * LANES] = re.astype(ref.dtype)
        ref[at, BASE + half * LANES : BASE + (half + 1) * LANES] = im.astype(ref.dtype)

    return store


def from_scratch(ref, channels):
    def load(rows, k, half):
        at = rowshift(rows, k, channels)
        return (
            ref[at, half * LANES : (half + 1) * LANES].astype(f32),
            ref[at, BASE + half * LANES : BASE + (half + 1) * LANES].astype(f32),
        )

    return load


def filter_kernel(f_ref, high_ref, low_ref, twiddle_ref, spec_ref, zh, zl, *, radix, channels):
    def store(rows, k, half, re, im):
        at = rowshift(rows, k, channels)
        for value, base in ((re, 0), (im, BASE)):
            lanes = slice(base + half * LANES, base + (half + 1) * LANES)
            top = value.astype(bf16)
            zh[at, lanes] = top
            zl[at, lanes] = (value - top.astype(f32)).astype(bf16)

    split_in(partial(cut, f_ref, 0), twiddle_ref, store, radix, channels)
    spec_ref[...] = (
        forward_dot(zh[...], high_ref[...])
        + forward_dot(zl[...], high_ref[...])
        + forward_dot(zh[...], low_ref[...])
    )


def tile_load(ref):
    return lambda rows, lanes: ref[rows, lanes].astype(f32)


def tile_store(ref):
    def store(rows, lanes, value):
        ref[rows, lanes] = value.astype(ref.dtype)

    return store


def conv_kernel(
    here_ref, u_ref, fspec_ref, high_ref, twiddle_ref, out_ref, uspec_ref, z, y, big, *, radix, channels, length
):
    here = here_ref[0]
    split_in(partial(cut, u_ref, here), twiddle_ref, into_scratch(z, channels), radix, channels)
    big[...] = forward_dot(z[...], high_ref[...])
    uspec_ref[...] = big[...].astype(uspec_ref.dtype)
    product_loop(tile_load(big), tile_load(fspec_ref), tile_store(y), radix * channels, False)
    big[...] = inverse_dot(y[...], high_ref[...])
    split_out(from_scratch(big, channels), twiddle_ref, partial(put, out_ref, here), radix, channels, length)


def conv_mixed_kernel(
    here_ref, g_ref, fspec_ref, high_ref, twiddle_ref, mixed_ref, spec_ref, z, y, big, *, radix, channels, length
):
    here = here_ref[0]
    split_in(partial(cut, g_ref, here), twiddle_ref, into_scratch(z, channels), radix, channels)
    spec_ref[...] = forward_dot(z[...], high_ref[...])
    product_loop(tile_load(spec_ref), tile_load(fspec_ref), tile_store(y), radix * channels, True)
    big[...] = inverse_dot(y[...], high_ref[...])
    split_out(from_scratch(big, channels), twiddle_ref, partial(put, mixed_ref, here), radix, channels, length)


def conv_filt_kernel(
    gspec_ref, uspec_ref, high_ref, twiddle_ref, filt_ref, y, big, *, radix, channels, length, taps
):
    product_loop(tile_load(gspec_ref), tile_load(uspec_ref), tile_store(y), radix * channels, True)
    big[...] = inverse_dot(y[...], high_ref[...])
    filt_ref[filt_ref.shape[0] - 1] = jnp.zeros(filt_ref.shape[1:], filt_ref.dtype)

    def store(rows, block, half, value):
        if block * BASE + half * LANES < taps:
            put(filt_ref, 0, rows, block, half, value)

    split_out(from_scratch(big, channels), twiddle_ref, store, radix, channels, length)


VM = pl.BlockSpec(memory_space=pltpu.VMEM)
SM = pl.BlockSpec(memory_space=pltpu.SMEM)


def filter_spectrum(filt, tables):
    high, low, twiddle = tables
    channels, length = filt.shape[1], filt.shape[0] * filt.shape[2]
    radix = length // BASE
    rows = radix * channels
    return pl.pallas_call(
        partial(filter_kernel, radix=radix, channels=channels),
        out_shape=jax.ShapeDtypeStruct((rows, 2 * BASE), f32),
        in_specs=[VM] * 4,
        out_specs=VM,
        scratch_shapes=[pltpu.VMEM((rows, 2 * BASE), bf16)] * 2,
        name="filter_spectrum",
    )(filt, high, low, twiddle)


def conv_forward(here, u, fspec, tables, out_dtype):
    high, _, twiddle = tables
    parts, channels, width = u.shape
    length = parts * width
    radix = length // BASE
    rows = radix * channels
    return pl.pallas_call(
        partial(conv_kernel, radix=radix, channels=channels, length=length),
        out_shape=(
            jax.ShapeDtypeStruct((parts, channels, width), out_dtype),
            jax.ShapeDtypeStruct((rows, 2 * BASE), bf16),
        ),
        in_specs=[SM] + [VM] * 4,
        out_specs=(VM, VM),
        scratch_shapes=[pltpu.VMEM((rows, 2 * BASE), bf16)] * 2 + [pltpu.VMEM((rows, 2 * BASE), f32)],
        name="conv_forward",
    )(here, u, fspec, high, twiddle)


def conv_mixed(here, g, fspec, tables):
    high, _, twiddle = tables
    parts, channels, width = g.shape
    length = parts * width
    radix = length // BASE
    rows = radix * channels
    return pl.pallas_call(
        partial(conv_mixed_kernel, radix=radix, channels=channels, length=length),
        out_shape=(
            jax.ShapeDtypeStruct((parts, channels, width), bf16),
            jax.ShapeDtypeStruct((rows, 2 * BASE), f32),
        ),
        in_specs=[SM] + [VM] * 4,
        out_specs=(VM, VM),
        scratch_shapes=[pltpu.VMEM((rows, 2 * BASE), bf16)] * 2 + [pltpu.VMEM((rows, 2 * BASE), f32)],
        name="conv_mixed",
    )(here, g, fspec, high, twiddle)


def conv_filt(gspec, uspec, tables, taps, width, length):
    high, _, twiddle = tables
    rows = gspec.shape[0]
    radix = length // BASE
    channels = rows // radix
    return pl.pallas_call(
        partial(conv_filt_kernel, radix=radix, channels=channels, length=length, taps=taps),
        out_shape=jax.ShapeDtypeStruct((-(-taps // width), channels, width), f32),
        in_specs=[VM] * 4,
        out_specs=VM,
        scratch_shapes=[pltpu.VMEM((rows, 2 * BASE), bf16), pltpu.VMEM((rows, 2 * BASE), f32)],
        name="conv_filt",
    )(gspec, uspec, high, twiddle)


thresh = 0.003
epsilon = 1e-05
gelu_scale = math.sqrt(2 / math.pi)
gelu_cube = 0.044715


def norm(values):
    centered = values - jnp.mean(values, axis=-1, keepdims=True)
    inverse = lax.rsqrt(jnp.mean(centered * centered, axis=-1, keepdims=True) + epsilon)
    return centered * inverse, inverse


def norm_back(unit, inverse, gain, grad):
    scaled = grad * gain
    mean = jnp.mean(scaled, axis=-1, keepdims=True)
    along = jnp.mean(scaled * unit, axis=-1, keepdims=True)
    return inverse * (scaled - mean - unit * along), jnp.sum(grad * unit, axis=0)


def shrink_pool(kernel, pad_len):
    shrunk = jax.nn.relu(kernel - thresh) - jax.nn.relu(-kernel - thresh)
    padded = jnp.pad(shrunk, ((0, 0), (1, 1)))
    pooled = (padded[:, :-2] + padded[:, 1:-1] + padded[:, 2:]) / 3.0
    positions = lax.broadcasted_iota(jnp.int32, pooled.shape, 1)
    return jnp.where(positions < (pooled.shape[1] - pad_len)[:, None], pooled, 0.0)


def gelu_both(values):
    cubic = gelu_cube * values * values
    turn = jnp.tanh(gelu_scale * (values + cubic * values))
    half = 0.5 * (1 + turn)
    slope = half + 0.5 * values * (1 - turn * turn) * (gelu_scale * (1 + 3 * cubic))
    return values * half, slope


def dot(a, b, over_a, over_b):
    return lax.dot_general(a, b, (((over_a,), (over_b,)), ((), ())), preferred_element_type=f32)


def after(x, *waits):
    return lax.optimization_barrier((x, waits))[0] if waits else x


def swap(x, axis, bit, done=()):
    return after(lax.ppermute(x, axis, [(i, i ^ bit) for i in range(lax.axis_size(axis))]), *done)


def gather(x, axis, stride=1, done=()):
    return jnp.stack([x] + [swap(x, axis, i, done) for i in range(stride, lax.axis_size(axis), stride)])


def scatter(x, axis, stride=1, done=()):
    terms = [x[0]] + [swap(x[i], axis, i * stride, done) for i in range(1, x.shape[0])]
    return sum(term.astype(f32) for term in terms)


class Gather:
    def __init__(self, x, bits):
        self.x, self.held, self.left = x, [], list(bits)

    def step(self, count=1, done=()):
        for bit in self.left[:count]:
            place = sum(other > bit for other in self.held)
            self.x = jnp.stack([self.x, swap(self.x, "dp", 1 << bit, done)], axis=place)
            self.held.append(bit)
        self.left = self.left[count:]
        return self

    def finish(self, done=()):
        self.step(len(self.left), done)
        return self.x.reshape((-1,) + self.x.shape[len(self.held) :])


def narrow_sum(*terms):
    return sum(term.astype(f32) for term in terms).astype(bf16)


class Reduction:
    def __init__(self, x, bits):
        self.x = x.reshape((2,) * len(bits) + x.shape[1:])
        self.held, self.left = sorted(bits, reverse=True), list(bits)

    def step(self, count=1, done=()):
        for bit in self.left[:count]:
            place = self.held.index(bit)
            self.held.remove(bit)
            keep, send = (lax.index_in_dim(self.x, side, place, keepdims=False) for side in (0, 1))
            self.x = narrow_sum(keep, swap(send, "dp", 1 << bit, done))
        self.left = self.left[count:]
        return self

    def finish(self, done=()):
        return self.step(len(self.left), done).x


def sum_all(x):
    for axis in ("dp", "mp"):
        bit = 1
        while bit < lax.axis_size(axis):
            x = x + swap(x, axis, bit)
            bit *= 2
    return x


def parts_of(x, axis, stride=1):
    return [x] + [swap(x, axis, i) for i in range(stride, lax.axis_size(axis), stride)]


def parts_for(x, axis):
    return [x[0]] + [swap(x[i], axis, i) for i in range(1, x.shape[0])]


def turn(x):
    return lax.all_to_all(x, "mp", 0, 0)


def exchange(x, done=()):
    return jnp.stack([x[0]] + [swap(x[i], "mp", i, done) for i in range(1, x.shape[0])])


def spread(x, *orders):
    x = x.astype(bf16)
    if orders:
        half = x.shape[0] // 16 * 8
        x = [Gather(part, bits).finish() for part, bits in zip((x[:half], x[half:]), orders)]
        x = jnp.concatenate(x, axis=1)
    else:
        x = gather(x, "dp", 2)
    return jnp.concatenate([x, swap(x, "dp", 1)])


class Spread:
    def __init__(self, x, *orders):
        half = x.shape[0] // 16 * 8
        self.parts = [Gather(part, bits) for part, bits in zip((x[:half], x[half:]), orders)]

    @property
    def x(self):
        return [part.x for part in self.parts]

    def step(self, done=()):
        for part in self.parts:
            part.step(done=done)

    def finish(self, done=()):
        x = jnp.concatenate([part.finish(done=done) for part in self.parts], axis=1)
        return jnp.concatenate([x, swap(x, "dp", 1)])


class Doubling:
    def __init__(self, x):
        self.x = x
        self.left = [
            (axis, 1 << bit) for axis in ("dp", "mp") for bit in range(lax.axis_size(axis).bit_length() - 1)
        ]

    def step(self):
        if self.left:
            self.x = self.x + swap(self.x, *self.left.pop(0))

    def finish(self):
        while self.left:
            self.step()


def absolute(x, start, rows):
    here = lax.axis_index("dp")
    count = x.shape[0]
    picks = []
    for index in range(count):
        relative = here ^ index
        at = (relative & 1) * (count // 2) + (relative >> 1)
        picks.append(lax.dynamic_slice(x, (at, start, 0), (1, rows, x.shape[2]))[0])
    return jnp.concatenate(picks).astype(f32)


def plain_body(
    tables,
    tokens,
    gain_first,
    input_weight,
    kernel,
    pad_len,
    output_weight,
    gain_second,
    up_weight,
    down_weight,
    cotangent,
):
    ways, rows_mp = lax.axis_size("dp"), lax.axis_size("mp")
    here_dp, here_mp = lax.axis_index("dp"), lax.axis_index("mp")
    chips = list(range(1, ways.bit_length() - 1))
    first_bits, second_bits = chips, chips[::-1]
    here = here_mp.astype(jnp.int32)[None]
    spots, width = tokens.shape[1:]
    length = spots * rows_mp
    own_channels = kernel.shape[0]
    slice_channels = own_channels // ways
    slice_hidden = up_weight.shape[1] // ways
    channels = own_channels * rows_mp

    own_in = lax.dynamic_slice_in_dim(input_weight, here_dp * slice_channels, slice_channels, 2)
    own_out = lax.dynamic_slice_in_dim(output_weight, here_dp * slice_channels, slice_channels, 0)
    mixer_rows = gather(jnp.concatenate([own_in.transpose(1, 2, 0), own_out[None]]), "mp")
    start_rows = tokens[0].astype(f32)
    unit_one, inverse_one = norm(start_rows)
    normed_low = (unit_one * gain_first).astype(bf16)
    own_up = lax.dynamic_slice_in_dim(up_weight, here_dp * slice_hidden, slice_hidden, 1).T
    own_down = lax.dynamic_slice_in_dim(down_weight, here_dp * slice_hidden, slice_hidden, 0)
    own_feed = jnp.stack([own_up, own_down])

    picks = []
    for core in range(2):
        for chip in range(ways // 2):
            at = (here_dp ^ (2 * chip + core)) * slice_channels
            picks.append(at)
    kernel_rel = jnp.concatenate([lax.dynamic_slice_in_dim(kernel, at, slice_channels, 0) for at in picks])
    pad_rel = jnp.concatenate([lax.dynamic_slice_in_dim(pad_len, at, slice_channels, 0) for at in picks])
    filt = shrink_pool(kernel_rel, pad_rel)
    fspec = filter_spectrum(jnp.pad(filt, ((0, 0), (0, length - filt.shape[1])))[None], tables)

    feed_rows = gather(after(own_feed, mixer_rows), "mp")
    mixer_rows = gather(after(mixer_rows, fspec, normed_low, own_feed), "dp", 2)
    feeds = [
        Gather(after(feed_rows[:, side], mixer_rows), bits).step()
        for side, bits in ((0, first_bits), (1, second_bits))
    ]
    mixer_rows = jnp.stack([mixer_rows, swap(mixer_rows, "dp", 1)])
    mixer_weights = mixer_rows.transpose(3, 2, 0, 1, 4, 5)
    weight_in = mixer_weights[:3].reshape(3 * channels, width)
    weight_out = mixer_weights[3].reshape(channels, width)

    proj = dot(weight_in, normed_low, 1, 1).reshape(3, channels, spots)
    value, gate_one, gate_two = proj[0], proj[1], proj[2]
    mixed_in = (value * gate_one).astype(bf16).reshape(rows_mp, own_channels, spots)
    for feed in feeds:
        feed.x = after(feed.x, mixed_in)
        feed.finish()
    conv_out, uspec = conv_forward(here, exchange(mixed_in), fspec, tables, bf16)
    feeds = [after(feed.x, conv_out).reshape(-1, width) for feed in feeds]
    conv = exchange(conv_out).reshape(channels, spots).astype(f32)
    mixer_low = (gate_two * conv).astype(bf16)
    residual_one = start_rows + dot(mixer_low, weight_out, 0, 0)

    unit_two, inverse_two = norm(residual_one)
    second_low = (unit_two * gain_second).astype(bf16)
    grad_rows = cotangent[0]
    feeds = [[feed, swap(feed, "dp", 1)] for feed in feeds]
    block_out, grad_norm_two = residual_one, 0.0
    up_grads, down_grads = [], []
    for up, down in zip(*feeds):
        act, slope = gelu_both(dot(second_low, up, 1, 1))
        act_low = act.astype(bf16)
        grad_pre = (dot(grad_rows, down, 1, 1) * slope).astype(bf16)
        block_out = block_out + dot(act_low, down, 1, 0)
        grad_norm_two = grad_norm_two + dot(grad_pre, up, 1, 0)
        up_grads.append(dot(grad_pre, second_low, 0, 0).astype(bf16))
        down_grads.append(dot(act_low, grad_rows, 0, 0).astype(bf16))
    grad_mid_norm, gain_second_grad = norm_back(unit_two, inverse_two, gain_second, grad_norm_two)
    grad_mid = grad_rows.astype(f32) + grad_mid_norm
    mid_low = grad_mid.astype(bf16)

    chips_count = ways // 2

    def hidden_sum(parts, bits):
        kept = narrow_sum(parts[0], swap(parts[1], "dp", 1))
        return Reduction(kept.reshape(chips_count, rows_mp, slice_hidden, width), bits)

    down_sum = hidden_sum(down_grads, second_bits)
    up_sum = hidden_sum(up_grads, first_bits)

    def by_slice(parts):
        parts = [part.astype(bf16).reshape(rows_mp, 2, chips_count, slice_channels, width) for part in parts]
        return jnp.concatenate(parts, axis=3).transpose(1, 2, 0, 3, 4)

    grad_mixer = dot(weight_out, mid_low, 1, 1)
    grad_conv = (grad_mixer * gate_two).astype(bf16).reshape(rows_mp, own_channels, spots)
    grad_conv = exchange(grad_conv)
    grad_gate_two = (grad_mixer * conv).astype(bf16)
    out_grad = dot(mixer_low, mid_low, 1, 0)
    late = by_slice([dot(grad_gate_two, normed_low, 1, 0), out_grad])
    late = narrow_sum(late[0], swap(late[1], "dp", 1))
    grad_conv = after(grad_conv, down_sum.x, up_sum.x, late)
    mixed_out, gspec = conv_mixed(here, grad_conv, fspec, tables)
    filt_grad = conv_filt(gspec, uspec, tables, length, length, length)
    down_sum.step()
    up_sum.step()
    late = scatter(late, "dp", 2).astype(bf16)
    grad_mixed = exchange(mixed_out).reshape(channels, spots).astype(f32)
    grad_mixed = after(grad_mixed, down_sum.x, up_sum.x, late)
    grad_value = (grad_mixed * gate_one).astype(bf16)
    grad_gate_one = (grad_mixed * value).astype(bf16)
    rest = by_slice([dot(grad, normed_low, 1, 0) for grad in (grad_value, grad_gate_one)])
    grad_norm_one = dot(jnp.concatenate([grad_value, grad_gate_one, grad_gate_two]), weight_in, 0, 0)
    grad_start, gain_first_grad = norm_back(unit_one, inverse_one, gain_first, grad_norm_one)
    grad_tokens = grad_mid + grad_start

    taps = kernel.shape[1]
    filt_grad = filt_grad[0, :, :taps].astype(bf16).reshape(2, chips_count, -1, width)
    rest = jnp.concatenate([rest.reshape(2, chips_count, -1, width), filt_grad], axis=2)
    rest = scatter(narrow_sum(rest[0], swap(rest[1], "dp", 1)), "dp", 2)
    split = rest.shape[0] - filt_grad.shape[2]
    own_kernel = lax.dynamic_slice_in_dim(kernel, here_dp * slice_channels, slice_channels, 0)
    own_pad = lax.dynamic_slice_in_dim(pad_len, here_dp * slice_channels, slice_channels, 0)
    _, filter_back = jax.vjp(partial(shrink_pool, pad_len=own_pad), own_kernel)
    (own_filt,) = filter_back(rest[split:].reshape(slice_channels, taps))
    rest = scatter(rest[:split].astype(bf16).reshape(rows_mp, 2 * slice_channels, width), "mp")
    rest = spread(jnp.concatenate([rest, own_filt.reshape(-1, width)]))
    bulk = jnp.concatenate([up_sum.finish(), down_sum.finish(), late], axis=1)
    bulk = spread(scatter(bulk, "mp"))

    up_grad = absolute(bulk, 0, slice_hidden).T
    down_grad = absolute(bulk, slice_hidden, slice_hidden)
    in_grad = [
        absolute(rest, 0, slice_channels),
        absolute(rest, slice_channels, slice_channels),
        absolute(bulk, 2 * slice_hidden, slice_channels),
    ]
    in_full = jnp.stack(in_grad).transpose(2, 0, 1)
    out_full = absolute(bulk, 2 * slice_hidden + slice_channels, slice_channels)
    kernel_grad = absolute(rest, 2 * slice_channels, filt_grad.shape[2]).reshape(own_channels, taps)

    gains = sum_all(jnp.stack([gain_first_grad, gain_second_grad]))
    return (
        block_out.astype(bf16)[None],
        grad_tokens[None],
        gains[0],
        in_full,
        kernel_grad,
        out_full,
        gains[1],
        up_grad,
        down_grad,
    )


def whole_call(kernel, outs, scratch=(), name=None, smem=0, count=0, **rest):
    return pl.pallas_call(
        kernel,
        out_shape=tuple(jax.ShapeDtypeStruct(shape, dtype) for shape, dtype in outs),
        in_specs=[SM] * smem + [VM] * count,
        out_specs=tuple(VM for _ in outs),
        scratch_shapes=[pltpu.VMEM(shape, dtype) for shape, dtype in scratch],
        name=name,
        **rest,
    )


def relative_index(here, place, count):
    chip, core = place % (count // 2), place // (count // 2)
    return here ^ (2 * chip + core)


def filter_slices_kernel(
    here_ref, kernel_ref, pad_ref, high_ref, low_ref, twiddle_ref, spec_ref, filt, zh, zl, *, radix, channels, ways
):
    here = here_ref[0]
    rows = channels // ways
    taps = kernel_ref.shape[1]
    filt[...] = jnp.zeros_like(filt)
    spot = lax.broadcasted_iota(jnp.int32, (8, taps), 1)
    for place in range(ways):
        start = relative_index(here, place, ways) * rows
        for tile in range(rows // 8):
            at = pl.ds(pl.multiple_of(start + tile * 8, 8), 8)
            raw = kernel_ref[at, :]
            shrunk = jnp.maximum(raw - thresh, 0.0) - jnp.maximum(-raw - thresh, 0.0)
            before = jnp.where(spot == 0, 0.0, pltpu.roll(shrunk, 1, 1))
            behind = jnp.where(spot == taps - 1, 0.0, pltpu.roll(shrunk, taps - 1, 1))
            pooled = (before + shrunk + behind) / 3.0
            kept = jnp.where(spot < taps - pad_ref[at, :], pooled, 0.0)
            put_rows = place * rows + tile * 8
            filt[0, put_rows : put_rows + 8, :taps] = kept
    filter_kernel(filt, high_ref, low_ref, twiddle_ref, spec_ref, zh, zl, radix=radix, channels=channels)


def filter_slices(here, kernel, pad_len, tables, length, ways):
    high, low, twiddle = tables
    channels = kernel.shape[0]
    radix = length // BASE
    rows = radix * channels
    return whole_call(
        partial(filter_slices_kernel, radix=radix, channels=channels, ways=ways),
        [((rows, 2 * BASE), f32)],
        [((1, channels, length), f32), ((rows, 2 * BASE), bf16), ((rows, 2 * BASE), bf16)],
        name="filter_spectrum",
        smem=1,
        count=5,
    )(here, kernel, pad_len[:, None], high, low, twiddle)[0]


def nt(a, b):
    return dot(a, b, 1, 1)


def tn(a, b):
    return dot(a, b, 0, 0)


def project_kernel(here_ref, x_ref, gain_ref, near_ref, far_ref, u_ref, v_ref, one_ref, two_ref, out_ref, low_ref, low, *, rows):
    mesh_rows = u_ref.shape[0]
    here = here_ref[0]

    @pl.when(pl.program_id(0) == 0)
    def _():
        unit, _ = norm(x_ref[...].astype(f32))
        low[...] = (unit * gain_ref[...]).astype(bf16)
        low_ref[...] = low[...]

    for core, ref in enumerate((near_ref, far_ref)):
        proj = nt(ref[0], low[...])
        for i in range(mesh_rows):
            at = i * 4 * rows
            value, one, two = (proj[at + k * rows : at + (k + 1) * rows] for k in range(3))
            to = i ^ here
            u_ref[to, core, 0] = (value * one).astype(bf16)
            v_ref[to, core, 0] = value
            one_ref[to, core, 0] = one
            two_ref[to, core, 0] = two
            out_ref[to, core, 0] = ref[0, at + 3 * rows : at + 4 * rows, :]


def project(here, x, gain, near, far, mesh_rows):
    spots, width = x.shape
    chips, size = near.shape[:2]
    rows = size // (4 * mesh_rows)
    block = lambda last: pl.BlockSpec((mesh_rows, 2, 1, rows, last), lambda j: (0, 0, j, 0, 0))
    shape = lambda last, dtype: jax.ShapeDtypeStruct((mesh_rows, 2, chips, rows, last), dtype)
    weights = pl.BlockSpec((1, size, width), lambda j: (j, 0, 0))
    full = pl.BlockSpec((spots, width), lambda j: (0, 0))
    return pl.pallas_call(
        partial(project_kernel, rows=rows),
        grid=(chips,),
        in_specs=[SM, full, pl.BlockSpec((1, width), lambda j: (0, 0)), weights, weights],
        out_specs=[block(spots)] * 4 + [block(width), full],
        out_shape=[
            shape(spots, bf16),
            shape(spots, f32),
            shape(spots, f32),
            shape(spots, f32),
            shape(width, bf16),
            jax.ShapeDtypeStruct((spots, width), bf16),
        ],
        scratch_shapes=[pltpu.VMEM((spots, width), bf16)],
        name="project",
    )(here, x, gain[None], near, far)


def feed_step(here, second, grad_rows, up_ref, down_ref, out_acc, norm_acc, up_grad_ref, down_grad_ref, mesh_rows):
    up, down = up_ref[...], down_ref[...]
    act, slope = gelu_both(nt(second, up))
    act_low = act.astype(bf16)
    grad_pre = (nt(grad_rows, down) * slope).astype(bf16)
    out_acc[...] += dot(act_low, down, 1, 0)
    norm_acc[...] += dot(grad_pre, up, 1, 0)
    up_grad = tn(grad_pre, second).astype(bf16)
    down_grad = tn(act_low, grad_rows).astype(bf16)
    for i in range(mesh_rows):
        rows = up.shape[0] // mesh_rows
        to = pl.ds(pl.multiple_of((i ^ here) * rows, rows), rows)
        up_grad_ref[to, :] = up_grad[i * rows : (i + 1) * rows]
        down_grad_ref[to, :] = down_grad[i * rows : (i + 1) * rows]


def feed_first_kernel(
    here_ref, x_ref, two_ref, conv_ref, out_weight_ref, gain_ref, grad_ref, up_ref, down_ref,
    residual_ref, second_ref, mixer_ref, out_acc, norm_acc, up_grad_ref, down_grad_ref, *, mesh_rows,
):
    @pl.when(pl.program_id(0) == 0)
    def _():
        mixer_ref[...] = (two_ref[...] * conv_ref[...].astype(f32)).astype(bf16)
        residual = x_ref[...].astype(f32) + tn(mixer_ref[...], out_weight_ref[...])
        residual_ref[...] = residual
        unit, _ = norm(residual)
        second_ref[...] = (unit * gain_ref[...]).astype(bf16)
        out_acc[...] = jnp.zeros_like(out_acc)
        norm_acc[...] = jnp.zeros_like(norm_acc)

    feed_step(here_ref[0], second_ref[...], grad_ref[...], up_ref, down_ref, out_acc, norm_acc, up_grad_ref, down_grad_ref, mesh_rows)


def feed_second_kernel(
    here_ref, residual_ref, second_ref, out_in_ref, norm_in_ref, grad_ref, gain_ref, out_weight_ref, two_ref, conv_ref, up_ref, down_ref,
    block_ref, mid_ref, mid_low_ref, gain_grad_ref, grad_conv_ref, grad_two_ref, up_grad_ref, down_grad_ref, out_acc, norm_acc, *, mesh_rows,
):
    @pl.when(pl.program_id(0) == 0)
    def _():
        out_acc[...] = out_in_ref[...] + residual_ref[...]
        norm_acc[...] = norm_in_ref[...]

    feed_step(here_ref[0], second_ref[...], grad_ref[...], up_ref, down_ref, out_acc, norm_acc, up_grad_ref, down_grad_ref, mesh_rows)

    @pl.when(pl.program_id(0) == pl.num_programs(0) - 1)
    def _():
        unit, inverse = norm(residual_ref[...])
        grad, gain_grad = norm_back(unit, inverse, gain_ref[...], norm_acc[...])
        gain_grad_ref[...] = gain_grad[None]
        mid = grad_ref[...].astype(f32) + grad
        mid_ref[...] = mid
        mid_low_ref[...] = mid.astype(bf16)
        block_ref[...] = out_acc[...].astype(bf16)
        grad_mixer = nt(out_weight_ref[...], mid_low_ref[...])
        grad_conv_ref[...] = (grad_mixer * two_ref[...]).astype(bf16)
        grad_two_ref[...] = (grad_mixer * conv_ref[...].astype(f32)).astype(bf16)


def feed_call(kernel, here, wholes, blocks, outs, block_rows, scratch, name):
    steps = blocks[0].shape[0] // block_rows
    width = blocks[0].shape[1]
    full = lambda shape: pl.BlockSpec(shape, lambda n: (0,) * len(shape))
    block = pl.BlockSpec((block_rows, width), lambda n: (n, 0))
    return pl.pallas_call(
        kernel,
        grid=(steps,),
        in_specs=[SM] + [VM for x in wholes] + [block] * len(blocks),
        out_specs=[full(shape) for shape, _ in outs] + [block] * len(blocks),
        out_shape=[jax.ShapeDtypeStruct(shape, dtype) for shape, dtype in outs]
        + [jax.ShapeDtypeStruct(b.shape, bf16) for b in blocks],
        scratch_shapes=[pltpu.VMEM(shape, dtype) for shape, dtype in scratch],
        name=name,
    )(here, *wholes, *blocks)


def put_slices(out_ref, index, rows_at, product, mesh_rows, chips, rows):
    for i in range(mesh_rows):
        for core in range(2):
            for chip in range(chips):
                start = ((i * 2 + core) * chips + chip) * rows
                at = rows_at(i)
                out_ref[(core, *index, chip, slice(at, at + rows))] = product[start : start + rows, :].astype(bf16)


def late_kernel(grad_two_ref, low_ref, mixer_ref, mid_low_ref, late_ref, product, *, mesh_rows, chips, rows):
    for kind, pair in enumerate(((mixer_ref, mid_low_ref), (grad_two_ref, low_ref))):
        product[...] = dot(pair[0][...], pair[1][...], 1, 0)
        put_slices(late_ref, (kind,), lambda i: i * rows, product, mesh_rows, chips, rows)


def rest_kernel(
    mixed_ref, value_ref, one_ref, low_ref, filt_ref, rest_ref, grad_value_ref, grad_one_ref, product,
    *, mesh_rows, chips, rows,
):
    mixed = mixed_ref[...].astype(f32)
    grad_value_ref[...] = (mixed * one_ref[...]).astype(bf16)
    grad_one_ref[...] = (mixed * value_ref[...]).astype(bf16)
    for kind, grad_ref in enumerate((grad_value_ref, grad_one_ref)):
        product[...] = dot(grad_ref[...], low_ref[...], 1, 0)
        put_slices(rest_ref, (), lambda i: (2 * i + kind) * rows, product, mesh_rows, chips, rows)
    base = 2 * mesh_rows * rows
    for part in range(filt_ref.shape[0]):
        for core in range(2):
            for chip in range(chips):
                start = (core * chips + chip) * rows
                at = base + part * rows
                rest_ref[core, chip, at : at + rows, :] = filt_ref[part, start : start + rows, :].astype(bf16)


def first_norm_kernel(
    here_ref, grad_value_ref, grad_one_ref, grad_two_ref, near_ref, far_ref, x_ref, gain_ref, mid_ref,
    tokens_ref, gain_grad_ref, gathered, acc, *, mesh_rows, chips, rows,
):
    size = 4 * mesh_rows * rows
    for core, ref in enumerate((near_ref, far_ref)):
        for chip in range(chips):
            for i in range(mesh_rows):
                start = (core * chips + chip) * rows
                for k, grad_ref in enumerate((grad_value_ref, grad_one_ref, grad_two_ref)):
                    at = (i * 4 + k) * rows
                    gathered[at : at + rows, :] = grad_ref[i ^ here_ref[0], start : start + rows, :]
                at = (i * 4 + 3) * rows
                gathered[at : at + rows, :] = jnp.zeros((rows, gathered.shape[1]), bf16)
            term = tn(gathered[...], ref[chip])
            acc[...] = term if core == 0 and chip == 0 else acc[...] + term
    unit, inverse = norm(x_ref[...].astype(f32))
    grad, gain_grad = norm_back(unit, inverse, gain_ref[...], acc[...])
    tokens_ref[...] = mid_ref[...] + grad
    gain_grad_ref[...] = gain_grad[None]


def unpack_bulk_kernel(here_ref, x_ref, up_ref, down_ref, two_ref, out_ref, turned, *, ways, hidden, rows):
    here = here_ref[0]
    for index in range(ways):
        relative = here ^ index
        block = x_ref[(relative & 1) * (ways // 2) + (relative >> 1)].astype(f32)
        at = slice(index * hidden, (index + 1) * hidden)
        turned[at, :] = block[:hidden]
        down_ref[at, :] = block[hidden + rows : 2 * hidden + rows]
        at = slice(index * rows, (index + 1) * rows)
        out_ref[at, :] = block[hidden : hidden + rows]
        two_ref[at, :] = block[2 * hidden + rows :]
    up_ref[...] = turned[...].T


def unpack_rest_kernel(here_ref, x_ref, two_ref, in_ref, kernel_ref, *, ways, rows):
    here = here_ref[0]
    width = x_ref.shape[2]
    taps = kernel_ref.shape[1]
    in_ref[2] = two_ref[...]
    for index in range(ways):
        relative = here ^ index
        block = x_ref[(relative & 1) * (ways // 2) + (relative >> 1)].astype(f32)
        at = slice(index * rows, (index + 1) * rows)
        in_ref[0, at, :] = block[:rows]
        in_ref[1, at, :] = block[rows : 2 * rows]
        for part in range(-(-taps // width)):
            size = min(width, taps - part * width)
            kernel_ref[at, part * width : part * width + size] = block[(2 + part) * rows : (3 + part) * rows, :size]


def fast_body(
    tables,
    tokens,
    gain_first,
    input_weight,
    kernel,
    pad_len,
    output_weight,
    gain_second,
    up_weight,
    down_weight,
    cotangent,
):
    ways, mesh_rows = lax.axis_size("dp"), lax.axis_size("mp")
    here_dp, here_mp = lax.axis_index("dp"), lax.axis_index("mp")
    chip_bits = list(range(1, ways.bit_length() - 1))
    first_bits, second_bits = chip_bits, chip_bits[::-1]
    here, place = here_mp.astype(jnp.int32)[None], here_dp.astype(jnp.int32)[None]
    x, grad_rows = tokens[0], cotangent[0]
    spots, width = x.shape
    length = spots * mesh_rows
    own_channels, taps = kernel.shape
    chips = ways // 2
    rows = own_channels // ways
    hidden = up_weight.shape[1] // ways
    channels = own_channels * mesh_rows
    sizes = dict(mesh_rows=mesh_rows, chips=chips, rows=rows)

    own_in = lax.dynamic_slice_in_dim(input_weight.transpose(1, 2, 0), here_dp * rows, rows, 1)
    own_out = lax.dynamic_slice_in_dim(output_weight, here_dp * rows, rows, 0)
    mixer_rows = gather(jnp.concatenate([own_in, own_out[None]]), "mp")
    own_up = lax.dynamic_slice_in_dim(up_weight, here_dp * hidden, hidden, 1).T
    own_down = lax.dynamic_slice_in_dim(down_weight, here_dp * hidden, hidden, 0)
    own_feed = jnp.stack([own_up, own_down])
    fspec = filter_slices(place, kernel, pad_len, tables, length, ways)
    half = width // 2
    halves = [
        Gather(mixer_rows[..., :half], first_bits),
        Gather(mixer_rows[..., half:], second_bits),
    ]
    feed_rows = parts_of(after(own_feed, mixer_rows), "mp")
    for part in halves:
        part.step(done=(feed_rows[1],))
    near = jnp.concatenate([part.finish(done=(fspec, *feed_rows[2:])) for part in halves], axis=-1)
    feed_rows = jnp.stack(feed_rows)
    feeds = [Gather(feed_rows[:, side], bits) for side, bits in ((0, first_bits), (1, second_bits))]
    near = near.reshape(chips, -1, width)
    far = swap(near, "dp", 1)

    mixed_in, value, gate_one, gate_two, weight_out, normed_low = project(here, x, gain_first, near, far, mesh_rows)
    value, gate_one, gate_two = (part.reshape(channels, spots) for part in (value, gate_one, gate_two))
    weight_out = weight_out.reshape(channels, width)
    mixed_in = mixed_in.reshape(mesh_rows, own_channels, spots)
    in_order = jnp.zeros((1,), jnp.int32)
    for feed in feeds:
        feed.step(done=(mixed_in,))
    conv_out, uspec = conv_forward(in_order, turn(mixed_in), fspec, tables, bf16)
    for feed in feeds:
        feed.finish(done=(conv_out,))
    ups, downs = ([feed.x.reshape(-1, width), swap(feed.x, "dp", 1).reshape(-1, width)] for feed in feeds)
    conv = turn(conv_out).reshape(channels, spots)

    up_grads, down_grads = [None, None], [None, None]
    gain = gain_second[None]
    block_rows = mesh_rows * hidden
    wide, square = ((spots, width), f32), (spots, width)
    residual, second_low, mixer_low, out_acc, norm_acc, up_grads[0], down_grads[0] = feed_call(
        partial(feed_first_kernel, mesh_rows=mesh_rows),
        here,
        (x, gate_two, conv, weight_out, gain, grad_rows),
        (ups[0], downs[0]),
        [wide, (square, bf16), ((channels, spots), bf16), wide, wide],
        block_rows,
        [],
        "feed_first",
    )
    block_out, grad_mid, mid_low, gain_second_grad, grad_conv, grad_two, up_grads[1], down_grads[1] = feed_call(
        partial(feed_second_kernel, mesh_rows=mesh_rows),
        here,
        (residual, second_low, out_acc, norm_acc, grad_rows, gain, weight_out, gate_two, conv),
        (ups[1], downs[1]),
        [(square, bf16), wide, (square, bf16), ((1, width), f32), ((channels, spots), bf16), ((channels, spots), bf16)],
        block_rows,
        [wide, wide],
        "feed_second",
    )

    down_kept, up_kept = (
        narrow_sum(parts[0], swap(parts[1], "dp", 1)).reshape(chips, mesh_rows, hidden, width)
        for parts in (down_grads, up_grads)
    )
    (late,) = whole_call(
        partial(late_kernel, **sizes),
        [((2, 2, chips, mesh_rows * rows, width), bf16)],
        [((channels, width), f32)],
        name="late_grads",
        count=4,
    )(grad_two, normed_low, mixer_low, mid_low)
    late = narrow_sum(late[0], swap(late[1], "dp", 1)).reshape(2, chips, mesh_rows, rows, width)
    up_sum = Reduction(jnp.concatenate([up_kept, late[0]], axis=2), first_bits)
    down_sum = Reduction(jnp.concatenate([down_kept, late[1]], axis=2), second_bits)
    received = after(turn(grad_conv.reshape(mesh_rows, own_channels, spots)), up_sum.x, down_sum.x)

    mixed_out, gspec = conv_mixed(in_order, received, fspec, tables)
    filt_grad = conv_filt(gspec, uspec, tables, taps, width, length)
    down_sum.step(done=(mixed_out,))
    up_sum.step(done=(mixed_out,))
    mixed = after(turn(mixed_out), filt_grad, down_sum.x, up_sum.x).reshape(channels, spots)
    parts = filt_grad.shape[0]
    rest, grad_value, grad_one = whole_call(
        partial(rest_kernel, **sizes),
        [
            ((2, chips, (2 * mesh_rows + parts) * rows, width), bf16),
            ((channels, spots), bf16),
            ((channels, spots), bf16),
        ],
        [((channels, width), f32)],
        name="rest_grads",
        count=5,
    )(mixed, value, gate_one, normed_low, filt_grad)
    grad_tokens, gain_first_grad = whole_call(
        partial(first_norm_kernel, **sizes),
        [wide, ((1, width), f32)],
        [((4 * mesh_rows * rows, spots), bf16), wide],
        name="first_norm_back",
        smem=1,
        count=8,
    )(here, *(part.reshape(mesh_rows, own_channels, spots) for part in (grad_value, grad_one, grad_two)), near, far, x, gain_first[None], grad_mid)

    split = 2 * mesh_rows * rows
    size = rest.shape[2]
    kept = narrow_sum(rest[0], swap(rest[1], "dp", 1))
    kept = [
        Reduction(part, bits)
        for part, bits in ((kept[:, : size // 2], first_bits), (kept[:, size // 2 :], second_bits))
    ]
    for part in kept:
        part.step(done=(grad_tokens,))
    up_sum.finish(done=(grad_tokens,))
    down_sum.finish(done=(grad_tokens,))
    gains = Doubling(jnp.stack([gain_first_grad[0], gain_second_grad[0]]))
    gains.step()
    bulk = turn(jnp.concatenate([up_sum.x, down_sum.x], axis=1))
    rest = jnp.concatenate([part.finish(done=(gains.x,)) for part in kept])
    gains.step()
    own_kernel = lax.dynamic_slice_in_dim(kernel, here_dp * rows, rows, 0)
    own_pad = lax.dynamic_slice_in_dim(pad_len, here_dp * rows, rows, 0)
    _, filter_back = jax.vjp(partial(shrink_pool, pad_len=own_pad), own_kernel)
    filt_rows = rest[split:].astype(f32).reshape(parts, rows, width)
    (own_filt,) = filter_back(jnp.concatenate(list(filt_rows), axis=1)[:, :taps])
    own_filt = jnp.pad(own_filt, ((0, 0), (0, parts * width - taps))).astype(bf16)
    own_filt = jnp.concatenate([own_filt[:, part * width : (part + 1) * width] for part in range(parts)])
    rest = turn(rest[:split].reshape(mesh_rows, 2 * rows, width))
    rest = narrow_sum(*after(rest, gains.x, own_filt))
    gains.step()
    rest = Spread(jnp.concatenate([rest, own_filt]), first_bits, second_bits)
    bulk = narrow_sum(*after(bulk, rest.x[0]))
    bulk = Spread(bulk, first_bits, second_bits)
    rest.step(done=(gains.x,))
    gains.step()
    bulk.step(done=(gains.x,))
    rest = rest.finish()
    gains.finish()
    bulk = bulk.finish(done=(rest, gains.x))
    up_grad, down_grad, two_grad, out_grad = whole_call(
        partial(unpack_bulk_kernel, ways=ways, hidden=hidden, rows=rows),
        [(up_weight.shape, f32), (down_weight.shape, f32), ((own_channels, width), f32), ((own_channels, width), f32)],
        [(down_weight.shape, f32)],
        name="unpack_bulk",
        smem=1,
        count=1,
    )(place, bulk)
    in_grad, kernel_grad = whole_call(
        partial(unpack_rest_kernel, ways=ways, rows=rows),
        [((3, own_channels, width), f32), (kernel.shape, f32)],
        name="unpack_rest",
        smem=1,
        count=2,
    )(place, rest, two_grad)
    gains = gains.x
    return (
        block_out[None],
        grad_tokens[None],
        gains[0],
        in_grad.transpose(2, 0, 1),
        kernel_grad,
        out_grad,
        gains[1],
        up_grad,
        down_grad,
    )


def body(tables, *arrays):
    ways = lax.axis_size("dp")
    whole_tiles = arrays[3].shape[0] % (8 * ways) == 0 and arrays[7].shape[1] % (32 * ways) == 0
    assert arrays[0].shape[0] == 1
    return (fast_body if whole_tiles else plain_body)(tables, *arrays)


def solution(mesh):
    in_specs = (
        P("dp", "mp", None),
        P(),
        P(None, None, "mp"),
        P("mp", None),
        P("mp"),
        P("mp", None),
        P(),
        P(None, "mp"),
        P("mp", None),
        P("dp", "mp", None),
    )
    out_specs = (
        P("dp", "mp", None),
        P("dp", "mp", None),
        P(),
        P(None, None, "mp"),
        P("mp", None),
        P("mp", None),
        P(),
        P(None, "mp"),
        P("mp", None),
    )

    def program(tokens, *rest):
        tables = tuple(jnp.asarray(table) for table in dft_tables(tokens.shape[1]))
        inner = jax.shard_map(
            body, mesh=mesh, in_specs=((P(), P(), P()),) + in_specs, out_specs=out_specs, check_vma=False
        )
        return inner(tables, tokens, *rest)

    return program
```

```python
import math
from functools import partial

import jax
import jax.numpy as jnp
import numpy as np
from jax import lax
from jax.experimental import pallas as pl
from jax.experimental.pallas import tpu as pltpu
from jax.sharding import PartitionSpec as P

LANES = 128
ROWS = 16
BASE = 256
f32 = jnp.float32
bf16 = jnp.bfloat16


def dft_tables(length):
    radix = length // BASE
    spot = lax.iota(jnp.int32, BASE)
    angle = (spot[:, None] * spot[None] % BASE).astype(f32) * (2 * math.pi / BASE)
    cos, sin = jnp.cos(angle), jnp.sin(angle)
    matrix = jnp.concatenate(
        [jnp.concatenate([cos, -sin], axis=1), jnp.concatenate([sin, cos], axis=1)], axis=0
    )
    high = matrix.astype(bf16)
    low = (matrix - high.astype(f32)).astype(bf16)
    turn = 2 * np.pi * np.outer(np.arange(radix) + 0.25, np.arange(BASE)) / length
    twiddle = np.stack([np.cos(turn), np.sin(turn)]).astype(np.float32)
    return high, low, jnp.asarray(twiddle)


def times(re, im, angle):
    c, s = math.cos(angle), math.sin(angle)
    if abs(s) < 1e-12:
        return (re, im) if c > 0 else (-re, -im)
    if abs(c) < 1e-12:
        return (-im, re) if s > 0 else (im, -re)
    if abs(abs(c) - abs(s)) < 1e-12:
        a = abs(c)
        sc, ss = (a if c > 0 else -a), (1.0 if (s > 0) == (c > 0) else -1.0)
        if ss > 0:
            return (re - im) * sc, (re + im) * sc
        return (re + im) * sc, (im - re) * sc
    return re * c - im * s, re * s + im * c


def radix_dft(re, im, sign):
    n = len(re)
    if n == 1:
        return re, im
    er, ei = radix_dft(re[0::2], im[0::2], sign)
    odr, odi = radix_dft(re[1::2], im[1::2], sign)
    lo_r, lo_i, hi_r, hi_i = [], [], [], []
    for k in range(n // 2):
        tr, ti = times(odr[k], odi[k], sign * 2 * math.pi * k / n)
        lo_r.append(er[k] + tr)
        lo_i.append(ei[k] + ti)
        hi_r.append(er[k] - tr)
        hi_i.append(ei[k] - ti)
    return lo_r + hi_r, lo_i + hi_i


def split_in(load, twiddle_ref, store, radix, channels):
    def step(tile, carry):
        rows = pl.ds(pl.multiple_of(tile * ROWS, ROWS), ROWS)
        for half in range(BASE // LANES):
            lanes = slice(half * LANES, (half + 1) * LANES)
            re, im = [], []
            for block in range(radix):
                x = load(rows, block, half)
                angle = -2 * math.pi * block * 0.25 / radix
                re.append(x * math.cos(angle))
                im.append(x * math.sin(angle))
            re, im = radix_dft(re, im, -1)
            for k in range(radix):
                c = twiddle_ref[0, k : k + 1, lanes]
                s = twiddle_ref[1, k : k + 1, lanes]
                store(rows, k, half, re[k] * c + im[k] * s, im[k] * c - re[k] * s)
        return carry

    lax.fori_loop(0, channels // ROWS, step, 0)


def split_out(load, twiddle_ref, store, radix, channels, length):
    def step(tile, carry):
        rows = pl.ds(pl.multiple_of(tile * ROWS, ROWS), ROWS)
        for half in range(BASE // LANES):
            lanes = slice(half * LANES, (half + 1) * LANES)
            re, im = [], []
            for k in range(radix):
                vr, vi = load(rows, k, half)
                c = twiddle_ref[0, k : k + 1, lanes]
                s = twiddle_ref[1, k : k + 1, lanes]
                re.append(vr * c - vi * s)
                im.append(vr * s + vi * c)
            re, im = radix_dft(re, im, 1)
            for block in range(radix):
                angle = 2 * math.pi * block * 0.25 / radix
                store(
                    rows,
                    block,
                    half,
                    re[block] * (math.cos(angle) / length) - im[block] * (math.sin(angle) / length),
                )
        return carry

    lax.fori_loop(0, channels // ROWS, step, 0)


def forward_dot(z, matrix):
    return jnp.dot(z, matrix, preferred_element_type=f32)


def inverse_dot(y, matrix):
    return lax.dot_general(y, matrix, (((1,), (1,)), ((), ())), preferred_element_type=f32)


def product_loop(a_load, b_load, store, total_rows, conj):
    def step(tile, carry):
        rows = pl.ds(pl.multiple_of(tile * ROWS, ROWS), ROWS)
        for half in range(BASE // LANES):
            cr = slice(half * LANES, (half + 1) * LANES)
            ci = slice(BASE + half * LANES, BASE + (half + 1) * LANES)
            ar, ai = a_load(rows, cr), a_load(rows, ci)
            br, bi = b_load(rows, cr), b_load(rows, ci)
            if conj:
                store(rows, cr, ar * br + ai * bi)
                store(rows, ci, ai * br - ar * bi)
            else:
                store(rows, cr, ar * br - ai * bi)
                store(rows, ci, ai * br + ar * bi)
        return carry

    lax.fori_loop(0, total_rows // ROWS, step, 0)


def cut(ref, here, rows, block, half):
    width = ref.shape[-1]
    start = block * BASE + half * LANES
    return ref[(start // width) ^ here, rows, start % width : start % width + LANES].astype(f32)


def put(ref, here, rows, block, half, value):
    width = ref.shape[-1]
    start = block * BASE + half * LANES
    ref[(start // width) ^ here, rows, start % width : start % width + LANES] = value.astype(ref.dtype)


def rowshift(rows, k, channels):
    return pl.ds(pl.multiple_of(rows.start + k * channels, ROWS), ROWS)


def into_scratch(ref, channels):
    def store(rows, k, half, re, im):
        at = rowshift(rows, k, channels)
        ref[at, half * LANES : (half + 1) * LANES] = re.astype(ref.dtype)
        ref[at, BASE + half * LANES : BASE + (half + 1) * LANES] = im.astype(ref.dtype)

    return store


def from_scratch(ref, channels):
    def load(rows, k, half):
        at = rowshift(rows, k, channels)
        return (
            ref[at, half * LANES : (half + 1) * LANES].astype(f32),
            ref[at, BASE + half * LANES : BASE + (half + 1) * LANES].astype(f32),
        )

    return load


def filter_kernel(f_ref, high_ref, low_ref, twiddle_ref, spec_ref, zh, zl, *, radix, channels):
    def store(rows, k, half, re, im):
        at = rowshift(rows, k, channels)
        for value, base in ((re, 0), (im, BASE)):
            lanes = slice(base + half * LANES, base + (half + 1) * LANES)
            top = value.astype(bf16)
            zh[at, lanes] = top
            zl[at, lanes] = (value - top.astype(f32)).astype(bf16)

    split_in(partial(cut, f_ref, 0), twiddle_ref, store, radix, channels)
    spec_ref[...] = (
        forward_dot(zh[...], high_ref[...])
        + forward_dot(zl[...], high_ref[...])
        + forward_dot(zh[...], low_ref[...])
    )


def tile_load(ref):
    return lambda rows, lanes: ref[rows, lanes].astype(f32)


def tile_store(ref):
    def store(rows, lanes, value):
        ref[rows, lanes] = value.astype(ref.dtype)

    return store


def conv_kernel(here_ref, *refs, parts, radix, channels, length):
    sent, (fspec_ref, high_ref, twiddle_ref) = refs[:parts], refs[parts : parts + 3]
    outs, (uspec_ref, z, y, big, turned) = refs[parts + 3 : 2 * parts + 3], refs[2 * parts + 3 :]
    here = here_ref[0]
    for i, ref in enumerate(sent):
        turned[i ^ here] = ref[...]
    split_in(partial(cut, turned, 0), twiddle_ref, into_scratch(z, channels), radix, channels)
    big[...] = forward_dot(z[...], high_ref[...])
    uspec_ref[...] = big[...].astype(uspec_ref.dtype)
    product_loop(tile_load(big), tile_load(fspec_ref), tile_store(y), radix * channels, False)
    big[...] = inverse_dot(y[...], high_ref[...])
    split_out(from_scratch(big, channels), twiddle_ref, partial(put, turned, 0), radix, channels, length)
    for i, ref in enumerate(outs):
        ref[...] = turned[i ^ here]


def conv_mixed_kernel(here_ref, *refs, parts, radix, channels, length):
    sent, (fspec_ref, high_ref, twiddle_ref) = refs[:parts], refs[parts : parts + 3]
    mixed, (spec_ref, z, y, big, turned) = refs[parts + 3 : 2 * parts + 3], refs[2 * parts + 3 :]
    here = here_ref[0]
    for i, ref in enumerate(sent):
        turned[i ^ here] = ref[...]
    split_in(partial(cut, turned, 0), twiddle_ref, into_scratch(z, channels), radix, channels)
    spec_ref[...] = forward_dot(z[...], high_ref[...])
    product_loop(tile_load(spec_ref), tile_load(fspec_ref), tile_store(y), radix * channels, True)
    big[...] = inverse_dot(y[...], high_ref[...])
    split_out(from_scratch(big, channels), twiddle_ref, partial(put, turned, 0), radix, channels, length)
    for i, ref in enumerate(mixed):
        ref[...] = turned[i ^ here]


def conv_filt_kernel(
    gspec_ref, uspec_ref, high_ref, twiddle_ref, filt_ref, y, big, *, radix, channels, length, taps
):
    product_loop(tile_load(gspec_ref), tile_load(uspec_ref), tile_store(y), radix * channels, True)
    big[...] = inverse_dot(y[...], high_ref[...])
    filt_ref[filt_ref.shape[0] - 1] = jnp.zeros(filt_ref.shape[1:], filt_ref.dtype)

    def store(rows, block, half, value):
        if block * BASE + half * LANES < taps:
            put(filt_ref, 0, rows, block, half, value)

    split_out(from_scratch(big, channels), twiddle_ref, store, radix, channels, length)


VM = pl.BlockSpec(memory_space=pltpu.VMEM)
SM = pl.BlockSpec(memory_space=pltpu.SMEM)


def filter_spectrum(filt, tables):
    high, low, twiddle = tables
    channels, length = filt.shape[1], filt.shape[0] * filt.shape[2]
    radix = length // BASE
    rows = radix * channels
    return pl.pallas_call(
        partial(filter_kernel, radix=radix, channels=channels),
        out_shape=jax.ShapeDtypeStruct((rows, 2 * BASE), f32),
        in_specs=[VM] * 4,
        out_specs=VM,
        scratch_shapes=[pltpu.VMEM((rows, 2 * BASE), bf16)] * 2,
        name="filter_spectrum",
    )(filt, high, low, twiddle)


def conv_forward(here, pieces, fspec, tables):
    high, _, twiddle = tables
    parts = len(pieces)
    channels, width = pieces[0].shape
    length = parts * width
    radix = length // BASE
    rows = radix * channels
    return pl.pallas_call(
        partial(conv_kernel, parts=parts, radix=radix, channels=channels, length=length),
        out_shape=[jax.ShapeDtypeStruct((channels, width), bf16)] * parts + [pltpu.HBM((rows, 2 * BASE), bf16)],
        in_specs=[SM] + [VM] * (parts + 3),
        out_specs=[VM] * (parts + 1),
        scratch_shapes=[pltpu.VMEM((rows, 2 * BASE), bf16)] * 2
        + [pltpu.VMEM((rows, 2 * BASE), f32), pltpu.VMEM((parts, channels, width), bf16)],
        compiler_params=pltpu.CompilerParams(vmem_limit_bytes=16 << 20),
        name="conv_forward",
    )(here, *pieces, fspec, high, twiddle)


def conv_mixed(here, pieces, fspec, tables):
    high, _, twiddle = tables
    parts = len(pieces)
    channels, width = pieces[0].shape
    length = parts * width
    radix = length // BASE
    rows = radix * channels
    return pl.pallas_call(
        partial(conv_mixed_kernel, parts=parts, radix=radix, channels=channels, length=length),
        out_shape=[jax.ShapeDtypeStruct((channels, width), bf16)] * parts
        + [jax.ShapeDtypeStruct((rows, 2 * BASE), f32)],
        in_specs=[SM] + [VM] * (parts + 3),
        out_specs=[VM] * (parts + 1),
        scratch_shapes=[pltpu.VMEM((rows, 2 * BASE), bf16)] * 2
        + [pltpu.VMEM((rows, 2 * BASE), f32), pltpu.VMEM((parts, channels, width), bf16)],
        compiler_params=pltpu.CompilerParams(vmem_limit_bytes=16 << 20),
        name="conv_mixed",
    )(here, *pieces, fspec, high, twiddle)


def conv_filt(gspec, uspec, tables, taps, width, length):
    high, _, twiddle = tables
    rows = gspec.shape[0]
    radix = length // BASE
    channels = rows // radix
    return pl.pallas_call(
        partial(conv_filt_kernel, radix=radix, channels=channels, length=length, taps=taps),
        out_shape=jax.ShapeDtypeStruct((-(-taps // width), channels, width), f32),
        in_specs=[VM] * 4,
        out_specs=VM,
        scratch_shapes=[pltpu.VMEM((rows, 2 * BASE), bf16), pltpu.VMEM((rows, 2 * BASE), f32)],
        compiler_params=pltpu.CompilerParams(vmem_limit_bytes=16 << 20),
        name="conv_filt",
    )(gspec, uspec, high, twiddle)


thresh = 0.003
epsilon = 1e-05
gelu_scale = math.sqrt(2 / math.pi)
gelu_cube = 0.044715


def norm(values):
    centered = values - jnp.mean(values, axis=-1, keepdims=True)
    inverse = lax.rsqrt(jnp.mean(centered * centered, axis=-1, keepdims=True) + epsilon)
    return centered * inverse, inverse


def norm_back(unit, inverse, gain, grad):
    scaled = grad * gain
    mean = jnp.mean(scaled, axis=-1, keepdims=True)
    along = jnp.mean(scaled * unit, axis=-1, keepdims=True)
    return inverse * (scaled - mean - unit * along), jnp.sum(grad * unit, axis=0)


def shrink_pool(kernel, pad_len):
    shrunk = jax.nn.relu(kernel - thresh) - jax.nn.relu(-kernel - thresh)
    padded = jnp.pad(shrunk, ((0, 0), (1, 1)))
    pooled = (padded[:, :-2] + padded[:, 1:-1] + padded[:, 2:]) / 3.0
    positions = lax.broadcasted_iota(jnp.int32, pooled.shape, 1)
    return jnp.where(positions < (pooled.shape[1] - pad_len)[:, None], pooled, 0.0)


def gelu_both(values):
    cubic = gelu_cube * values * values
    turn = jnp.tanh(gelu_scale * (values + cubic * values))
    half = 0.5 * (1 + turn)
    slope = half + 0.5 * values * (1 - turn * turn) * (gelu_scale * (1 + 3 * cubic))
    return values * half, slope


def dot(a, b, over_a, over_b):
    return lax.dot_general(a, b, (((over_a,), (over_b,)), ((), ())), preferred_element_type=f32)


def after(x, *waits):
    return lax.optimization_barrier((x, waits))[0] if waits else x


def swap(x, axis, bit, done=()):
    return after(lax.ppermute(x, axis, [(i, i ^ bit) for i in range(lax.axis_size(axis))]), *done)


def gather(x, axis, stride=1, done=()):
    return jnp.stack([x] + [swap(x, axis, i, done) for i in range(stride, lax.axis_size(axis), stride)])


def scatter(x, axis, stride=1, done=()):
    terms = [x[0]] + [swap(x[i], axis, i * stride, done) for i in range(1, x.shape[0])]
    return sum(term.astype(f32) for term in terms)


class Gather:
    def __init__(self, x, bits):
        self.x, self.held, self.left = x, [], list(bits)

    def step(self, count=1, done=()):
        for bit in self.left[:count]:
            place = sum(other > bit for other in self.held)
            self.x = jnp.stack([self.x, swap(self.x, "dp", 1 << bit, done)], axis=place)
            self.held.append(bit)
        self.left = self.left[count:]
        return self

    def finish(self, done=()):
        self.step(len(self.left), done)
        return self.x.reshape((-1,) + self.x.shape[len(self.held) :])


def narrow_sum(*terms):
    return sum(term.astype(f32) for term in terms).astype(bf16)


class Reduction:
    def __init__(self, x, bits):
        self.x = x.reshape((2,) * len(bits) + x.shape[1:])
        self.held, self.left = sorted(bits, reverse=True), list(bits)

    def step(self, count=1, done=()):
        for bit in self.left[:count]:
            place = self.held.index(bit)
            self.held.remove(bit)
            keep, send = (lax.index_in_dim(self.x, side, place, keepdims=False) for side in (0, 1))
            self.x = narrow_sum(keep, swap(send, "dp", 1 << bit, done))
        self.left = self.left[count:]
        return self

    def finish(self, done=()):
        return self.step(len(self.left), done).x


def sum_all(x):
    for axis in ("dp", "mp"):
        bit = 1
        while bit < lax.axis_size(axis):
            x = x + swap(x, axis, bit)
            bit *= 2
    return x


def parts_of(x, axis, stride=1):
    return [x] + [swap(x, axis, i) for i in range(stride, lax.axis_size(axis), stride)]


def parts_for(x, axis):
    return [x[0]] + [swap(x[i], axis, i) for i in range(1, x.shape[0])]


def turn(x):
    return lax.all_to_all(x, "mp", 0, 0)


def exchange(x, done=()):
    return jnp.stack([x[0]] + [swap(x[i], "mp", i, done) for i in range(1, x.shape[0])])


def spread(x, *orders):
    x = x.astype(bf16)
    if orders:
        half = x.shape[0] // 16 * 8
        x = [Gather(part, bits).finish() for part, bits in zip((x[:half], x[half:]), orders)]
        x = jnp.concatenate(x, axis=1)
    else:
        x = gather(x, "dp", 2)
    return jnp.concatenate([x, swap(x, "dp", 1)])


class Spread:
    def __init__(self, x, *orders):
        half = x.shape[0] // 16 * 8
        self.parts = [Gather(part, bits) for part, bits in zip((x[:half], x[half:]), orders)]

    @property
    def x(self):
        return [part.x for part in self.parts]

    def step(self, done=()):
        for part in self.parts:
            part.step(done=done)

    def finish(self, done=()):
        x = jnp.concatenate([part.finish(done=done) for part in self.parts], axis=1)
        return jnp.concatenate([x, swap(x, "dp", 1)])


class Doubling:
    def __init__(self, x):
        self.x = x
        self.left = [
            (axis, 1 << bit) for axis in ("dp", "mp") for bit in range(lax.axis_size(axis).bit_length() - 1)
        ]

    def step(self):
        if self.left:
            self.x = self.x + swap(self.x, *self.left.pop(0))

    def finish(self):
        while self.left:
            self.step()


def absolute(x, start, rows):
    here = lax.axis_index("dp")
    count = x.shape[0]
    picks = []
    for index in range(count):
        relative = here ^ index
        at = (relative & 1) * (count // 2) + (relative >> 1)
        picks.append(lax.dynamic_slice(x, (at, start, 0), (1, rows, x.shape[2]))[0])
    return jnp.concatenate(picks).astype(f32)


def plain_body(
    tables,
    tokens,
    gain_first,
    input_weight,
    kernel,
    pad_len,
    output_weight,
    gain_second,
    up_weight,
    down_weight,
    cotangent,
):
    ways, rows_mp = lax.axis_size("dp"), lax.axis_size("mp")
    here_dp, here_mp = lax.axis_index("dp"), lax.axis_index("mp")
    chips = list(range(1, ways.bit_length() - 1))
    first_bits, second_bits = chips, chips[::-1]
    here = here_mp.astype(jnp.int32)[None]
    spots, width = tokens.shape[1:]
    length = spots * rows_mp
    own_channels = kernel.shape[0]
    slice_channels = own_channels // ways
    slice_hidden = up_weight.shape[1] // ways
    channels = own_channels * rows_mp

    own_in = lax.dynamic_slice_in_dim(input_weight, here_dp * slice_channels, slice_channels, 2)
    own_out = lax.dynamic_slice_in_dim(output_weight, here_dp * slice_channels, slice_channels, 0)
    mixer_rows = gather(jnp.concatenate([own_in.transpose(1, 2, 0), own_out[None]]), "mp")
    start_rows = tokens[0].astype(f32)
    unit_one, inverse_one = norm(start_rows)
    normed_low = (unit_one * gain_first).astype(bf16)
    own_up = lax.dynamic_slice_in_dim(up_weight, here_dp * slice_hidden, slice_hidden, 1).T
    own_down = lax.dynamic_slice_in_dim(down_weight, here_dp * slice_hidden, slice_hidden, 0)
    own_feed = jnp.stack([own_up, own_down])

    picks = []
    for core in range(2):
        for chip in range(ways // 2):
            at = (here_dp ^ (2 * chip + core)) * slice_channels
            picks.append(at)
    kernel_rel = jnp.concatenate([lax.dynamic_slice_in_dim(kernel, at, slice_channels, 0) for at in picks])
    pad_rel = jnp.concatenate([lax.dynamic_slice_in_dim(pad_len, at, slice_channels, 0) for at in picks])
    filt = shrink_pool(kernel_rel, pad_rel)
    fspec = filter_spectrum(jnp.pad(filt, ((0, 0), (0, length - filt.shape[1])))[None], tables)

    feed_rows = gather(after(own_feed, mixer_rows), "mp")
    mixer_rows = gather(after(mixer_rows, fspec, normed_low, own_feed), "dp", 2)
    feeds = [
        Gather(after(feed_rows[:, side], mixer_rows), bits).step()
        for side, bits in ((0, first_bits), (1, second_bits))
    ]
    mixer_rows = jnp.stack([mixer_rows, swap(mixer_rows, "dp", 1)])
    mixer_weights = mixer_rows.transpose(3, 2, 0, 1, 4, 5)
    weight_in = mixer_weights[:3].reshape(3 * channels, width)
    weight_out = mixer_weights[3].reshape(channels, width)

    proj = dot(weight_in, normed_low, 1, 1).reshape(3, channels, spots)
    value, gate_one, gate_two = proj[0], proj[1], proj[2]
    mixed_in = (value * gate_one).astype(bf16).reshape(rows_mp, own_channels, spots)
    for feed in feeds:
        feed.x = after(feed.x, mixed_in)
        feed.finish()
    *conv_out, uspec = conv_forward(here, list(exchange(mixed_in)), fspec, tables)
    conv_out = jnp.stack(conv_out)
    feeds = [after(feed.x, conv_out).reshape(-1, width) for feed in feeds]
    conv = exchange(conv_out).reshape(channels, spots).astype(f32)
    mixer_low = (gate_two * conv).astype(bf16)
    residual_one = start_rows + dot(mixer_low, weight_out, 0, 0)

    unit_two, inverse_two = norm(residual_one)
    second_low = (unit_two * gain_second).astype(bf16)
    grad_rows = cotangent[0]
    feeds = [[feed, swap(feed, "dp", 1)] for feed in feeds]
    block_out, grad_norm_two = residual_one, 0.0
    up_grads, down_grads = [], []
    for up, down in zip(*feeds):
        act, slope = gelu_both(dot(second_low, up, 1, 1))
        act_low = act.astype(bf16)
        grad_pre = (dot(grad_rows, down, 1, 1) * slope).astype(bf16)
        block_out = block_out + dot(act_low, down, 1, 0)
        grad_norm_two = grad_norm_two + dot(grad_pre, up, 1, 0)
        up_grads.append(dot(grad_pre, second_low, 0, 0).astype(bf16))
        down_grads.append(dot(act_low, grad_rows, 0, 0).astype(bf16))
    grad_mid_norm, gain_second_grad = norm_back(unit_two, inverse_two, gain_second, grad_norm_two)
    grad_mid = grad_rows.astype(f32) + grad_mid_norm
    mid_low = grad_mid.astype(bf16)

    chips_count = ways // 2

    def hidden_sum(parts, bits):
        kept = narrow_sum(parts[0], swap(parts[1], "dp", 1))
        return Reduction(kept.reshape(chips_count, rows_mp, slice_hidden, width), bits)

    down_sum = hidden_sum(down_grads, second_bits)
    up_sum = hidden_sum(up_grads, first_bits)

    def by_slice(parts):
        parts = [part.astype(bf16).reshape(rows_mp, 2, chips_count, slice_channels, width) for part in parts]
        return jnp.concatenate(parts, axis=3).transpose(1, 2, 0, 3, 4)

    grad_mixer = dot(weight_out, mid_low, 1, 1)
    grad_conv = (grad_mixer * gate_two).astype(bf16).reshape(rows_mp, own_channels, spots)
    grad_conv = exchange(grad_conv)
    grad_gate_two = (grad_mixer * conv).astype(bf16)
    out_grad = dot(mixer_low, mid_low, 1, 0)
    late = by_slice([dot(grad_gate_two, normed_low, 1, 0), out_grad])
    late = narrow_sum(late[0], swap(late[1], "dp", 1))
    grad_conv = after(grad_conv, down_sum.x, up_sum.x, late)
    *mixed_out, gspec = conv_mixed(here, list(grad_conv), fspec, tables)
    filt_grad = conv_filt(gspec, uspec, tables, length, length, length)
    mixed_out = jnp.stack(mixed_out)
    down_sum.step()
    up_sum.step()
    late = scatter(late, "dp", 2).astype(bf16)
    grad_mixed = exchange(mixed_out).reshape(channels, spots).astype(f32)
    grad_mixed = after(grad_mixed, down_sum.x, up_sum.x, late)
    grad_value = (grad_mixed * gate_one).astype(bf16)
    grad_gate_one = (grad_mixed * value).astype(bf16)
    rest = by_slice([dot(grad, normed_low, 1, 0) for grad in (grad_value, grad_gate_one)])
    grad_norm_one = dot(jnp.concatenate([grad_value, grad_gate_one, grad_gate_two]), weight_in, 0, 0)
    grad_start, gain_first_grad = norm_back(unit_one, inverse_one, gain_first, grad_norm_one)
    grad_tokens = grad_mid + grad_start

    taps = kernel.shape[1]
    filt_grad = filt_grad[0, :, :taps].astype(bf16).reshape(2, chips_count, -1, width)
    rest = jnp.concatenate([rest.reshape(2, chips_count, -1, width), filt_grad], axis=2)
    rest = scatter(narrow_sum(rest[0], swap(rest[1], "dp", 1)), "dp", 2)
    split = rest.shape[0] - filt_grad.shape[2]
    own_kernel = lax.dynamic_slice_in_dim(kernel, here_dp * slice_channels, slice_channels, 0)
    own_pad = lax.dynamic_slice_in_dim(pad_len, here_dp * slice_channels, slice_channels, 0)
    _, filter_back = jax.vjp(partial(shrink_pool, pad_len=own_pad), own_kernel)
    (own_filt,) = filter_back(rest[split:].reshape(slice_channels, taps))
    rest = scatter(rest[:split].astype(bf16).reshape(rows_mp, 2 * slice_channels, width), "mp")
    rest = spread(jnp.concatenate([rest, own_filt.reshape(-1, width)]))
    bulk = jnp.concatenate([up_sum.finish(), down_sum.finish(), late], axis=1)
    bulk = spread(scatter(bulk, "mp"))

    up_grad = absolute(bulk, 0, slice_hidden).T
    down_grad = absolute(bulk, slice_hidden, slice_hidden)
    in_grad = [
        absolute(rest, 0, slice_channels),
        absolute(rest, slice_channels, slice_channels),
        absolute(bulk, 2 * slice_hidden, slice_channels),
    ]
    in_full = jnp.stack(in_grad).transpose(2, 0, 1)
    out_full = absolute(bulk, 2 * slice_hidden + slice_channels, slice_channels)
    kernel_grad = absolute(rest, 2 * slice_channels, filt_grad.shape[2]).reshape(own_channels, taps)

    gains = sum_all(jnp.stack([gain_first_grad, gain_second_grad]))
    return (
        block_out.astype(bf16)[None],
        grad_tokens[None],
        gains[0],
        in_full,
        kernel_grad,
        out_full,
        gains[1],
        up_grad,
        down_grad,
    )


def whole_call(kernel, outs, scratch=(), name=None, smem=0, count=0, room=6):
    return pl.pallas_call(
        kernel,
        out_shape=tuple(out if isinstance(out, pl.MemoryRef) else jax.ShapeDtypeStruct(*out) for out in outs),
        in_specs=[SM] * smem + [VM] * count,
        out_specs=tuple(VM for _ in outs),
        scratch_shapes=[pltpu.VMEM(shape, dtype) for shape, dtype in scratch],
        compiler_params=pltpu.CompilerParams(vmem_limit_bytes=room << 20),
        name=name,
    )


def relative_index(here, place, count):
    chip, core = place % (count // 2), place // (count // 2)
    return here ^ (2 * chip + core)


def filter_slices_kernel(
    here_ref, kernel_ref, pad_ref, high_ref, low_ref, twiddle_ref, spec_ref, filt, zh, zl, *, radix, channels, ways
):
    here = here_ref[0]
    rows = channels // ways
    taps = kernel_ref.shape[1]
    filt[...] = jnp.zeros_like(filt)
    spot = lax.broadcasted_iota(jnp.int32, (8, taps), 1)
    for place in range(ways):
        start = relative_index(here, place, ways) * rows
        for tile in range(rows // 8):
            at = pl.ds(pl.multiple_of(start + tile * 8, 8), 8)
            raw = kernel_ref[at, :]
            shrunk = jnp.maximum(raw - thresh, 0.0) - jnp.maximum(-raw - thresh, 0.0)
            before = jnp.where(spot == 0, 0.0, pltpu.roll(shrunk, 1, 1))
            behind = jnp.where(spot == taps - 1, 0.0, pltpu.roll(shrunk, taps - 1, 1))
            pooled = (before + shrunk + behind) / 3.0
            kept = jnp.where(spot < taps - pad_ref[at, :], pooled, 0.0)
            put_rows = place * rows + tile * 8
            filt[0, put_rows : put_rows + 8, :taps] = kept
    filter_kernel(filt, high_ref, low_ref, twiddle_ref, spec_ref, zh, zl, radix=radix, channels=channels)


def filter_slices(here, kernel, pad_len, tables, length, ways):
    high, low, twiddle = tables
    channels = kernel.shape[0]
    radix = length // BASE
    rows = radix * channels
    return whole_call(
        partial(filter_slices_kernel, radix=radix, channels=channels, ways=ways),
        [((rows, 2 * BASE), f32)],
        [((1, channels, length), f32), ((rows, 2 * BASE), bf16), ((rows, 2 * BASE), bf16)],
        name="filter_spectrum",
        smem=1,
        count=5,
        room=14,
    )(here, kernel, pad_len[:, None], high, low, twiddle)[0]


def nt(a, b):
    return dot(a, b, 1, 1)


def tn(a, b):
    return dot(a, b, 0, 0)


def project_kernel(level_ref, x_ref, gain_ref, *refs, rows, mesh_rows):
    pieces, sends = refs[:8], refs[8 : 8 + mesh_rows]
    v_ref, one_ref, two_ref, out_ref, low_ref, weights, low, proj, sems = refs[8 + mesh_rows :]
    step = pl.program_id(0)
    copies = [pltpu.make_async_copy(piece, weights.at[k], sems.at[k]) for k, piece in enumerate(pieces)]

    @pl.when(step == 0)
    def _():
        for copy in copies:
            copy.start()
        unit, _ = norm(x_ref[...].astype(f32))
        low[...] = (unit * gain_ref[...]).astype(bf16)
        low_ref[...] = low[...]

    for core in range(2):
        slot = core * 4 + step
        pltpu.make_async_copy(pieces[0], weights.at[slot], sems.at[slot]).wait()
        proj[...] = nt(weights[slot], low[...])
        for i, send_ref in enumerate(sends):
            to = i ^ level_ref[0]
            at = pl.multiple_of(to * (4 * rows), 8)
            value, one, two = (proj[pl.ds(at + k * rows, rows), :] for k in range(3))
            send_ref[core, 0] = (value * one).astype(bf16)
            v_ref[to, core, 0] = value
            one_ref[to, core, 0] = one
            two_ref[to, core, 0] = two
            at = (4 * i + 3) * rows
            out_ref[i, core, 0] = weights[slot, at : at + rows, :]


def project(level, x, gain, pieces, mesh_rows):
    spots, width = x.shape
    size = pieces[0].shape[0]
    rows = size // (4 * mesh_rows)
    block = lambda last: pl.BlockSpec((mesh_rows, 2, 1, rows, last), lambda j: (0, 0, j, 0, 0))
    shape = lambda last, dtype: pltpu.HBM((mesh_rows, 2, 4, rows, last), dtype)
    full = pl.BlockSpec((spots, width), lambda j: (0, 0))
    return pl.pallas_call(
        partial(project_kernel, rows=rows, mesh_rows=mesh_rows),
        grid=(4,),
        in_specs=[SM, full, pl.BlockSpec((1, width), lambda j: (0, 0))] + [pl.BlockSpec(memory_space=pl.ANY)] * 8,
        out_specs=[pl.BlockSpec((2, 1, rows, spots), lambda j: (0, j, 0, 0))] * mesh_rows
        + [block(spots)] * 3
        + [block(width), full],
        out_shape=[pltpu.HBM((2, 4, rows, spots), bf16)] * mesh_rows
        + [
            shape(spots, f32),
            shape(spots, f32),
            shape(spots, f32),
            shape(width, bf16),
            pltpu.HBM((spots, width), bf16),
        ],
        scratch_shapes=[
            pltpu.VMEM((8, size, width), bf16),
            pltpu.VMEM((spots, width), bf16),
            pltpu.VMEM((size, spots), f32),
            pltpu.SemaphoreType.DMA((8,)),
        ],
        compiler_params=pltpu.CompilerParams(vmem_limit_bytes=18 << 20),
        name="project",
    )(level, x, gain[None], *pieces)


def stack_kernel(*refs):
    for index, out_ref in enumerate(refs[len(refs) // 3 * 2 :]):
        out_ref[0] = refs[2 * index][...]
        out_ref[1] = refs[2 * index + 1][...]


def feed_kernel(*refs, mesh_rows):
    here_ref, x_ref, two_ref, out_weight_ref, gain_ref, grad_ref = refs[:6]
    sent, refs = refs[6 : 6 + mesh_rows], refs[6 + mesh_rows :]
    ups, downs, up_firsts, down_firsts = refs[:2], refs[2:4], refs[4:8], refs[8:12]
    mixer_ref, block_ref, mid_ref, mid_low_ref, gain_grad_ref, grad_two_ref = refs[12:18]
    sends, refs = refs[18 : 18 + mesh_rows], refs[18 + mesh_rows :]
    up_near, up_far, down_near, down_far = refs[:4]
    residual, second, out_acc, norm_acc, conv, turned, weights, grads, sems, grad_sems = refs[4:]
    step = pl.program_id(0)
    size = weights.shape[2]
    copies = []
    for side, (firsts, pairs) in enumerate(((up_firsts, ups), (down_firsts, downs))):
        for k in range(8):
            core, chip = divmod(k, 4)
            first = (0, 1) if side == 0 else (0, 2)
            if chip in first:
                source = firsts[2 * core + first.index(chip)]
            else:
                source = pairs[core].at[0 if chip == (2 if side == 0 else 1) else 1]
            copies.append(pltpu.make_async_copy(source, weights.at[side, k], sems.at[side, k]))

    @pl.when(step == 0)
    def _():
        for copy in copies:
            copy.start()
        for i, ref in enumerate(sent):
            conv[i ^ here_ref[0]] = ref[...]
        mixer_ref[...] = (two_ref[...] * conv[...].reshape(two_ref.shape).astype(f32)).astype(bf16)
        residual[...] = x_ref[...].astype(f32) + tn(mixer_ref[...], out_weight_ref[...])
        unit, _ = norm(residual[...])
        second[...] = (unit * gain_ref[...]).astype(bf16)
        out_acc[...] = residual[...]
        norm_acc[...] = jnp.zeros_like(norm_acc)

    for side in range(2):
        pltpu.make_async_copy(up_firsts[0], weights.at[side, step], sems.at[side, step]).wait()
    slot = step % 2

    @pl.when(step >= 2)
    def _():
        for side in range(2):
            pltpu.make_async_copy(
                grads.at[side, slot], up_near.at[pl.ds(0, size), :], grad_sems.at[side, slot]
            ).wait()

    up, down = weights[0, step], weights[1, step]
    act, slope = gelu_both(nt(second[...], up))
    act_low = act.astype(bf16)
    grad_pre = (nt(grad_ref[...], down) * slope).astype(bf16)
    out_acc[...] += dot(act_low, down, 1, 0)
    norm_acc[...] += dot(grad_pre, up, 1, 0)
    grads[0, slot] = tn(grad_pre, second[...]).astype(bf16)
    grads[1, slot] = tn(act_low, grad_ref[...]).astype(bf16)
    at = pl.ds(pl.multiple_of((step % 4) * size, size), size)
    for core, outs in enumerate(((up_near, down_near), (up_far, down_far))):

        @pl.when(step // 4 == core)
        def _():
            for side in range(2):
                pltpu.make_async_copy(
                    grads.at[side, slot], outs[side].at[at, :], grad_sems.at[side, slot]
                ).start()

    @pl.when(step == pl.num_programs(0) - 1)
    def _():
        unit, inverse = norm(residual[...])
        grad, gain_grad = norm_back(unit, inverse, gain_ref[...], norm_acc[...])
        gain_grad_ref[...] = gain_grad[None]
        mid = grad_ref[...].astype(f32) + grad
        mid_ref[...] = mid
        mid_low_ref[...] = mid.astype(bf16)
        block_ref[...] = out_acc[...].astype(bf16)
        grad_mixer = nt(out_weight_ref[...], mid_low_ref[...])
        flat = conv[...].reshape(two_ref.shape)
        grad_two_ref[...] = (grad_mixer * flat.astype(f32)).astype(bf16)
        turned[...] = (grad_mixer * two_ref[...]).astype(bf16).reshape(turned.shape)
        for i, ref in enumerate(sends):
            ref[...] = turned[i ^ here_ref[0]]
        for side in range(2):
            for last in range(2):
                pltpu.make_async_copy(
                    grads.at[side, last], up_near.at[pl.ds(0, size), :], grad_sems.at[side, last]
                ).wait()


def feed_forward(here, wholes, conv, ups, downs, channels):
    mesh_rows = len(conv)
    size, width = ups[2].shape
    spots = wholes[0].shape[0]
    shape = jax.ShapeDtypeStruct
    tall = shape((channels, spots), bf16)
    piece = shape((channels // mesh_rows, spots), bf16)
    anywhere = pl.BlockSpec(memory_space=pl.ANY)
    return pl.pallas_call(
        partial(feed_kernel, mesh_rows=mesh_rows),
        grid=(8,),
        in_specs=[SM] + [VM] * (len(wholes) + mesh_rows) + [anywhere] * 12,
        out_specs=[VM] * (6 + mesh_rows) + [anywhere] * 4,
        out_shape=[
            tall,
            pltpu.HBM((spots, width), bf16),
            pltpu.HBM((spots, width), f32),
            shape((spots, width), bf16),
            shape((1, width), f32),
            pltpu.HBM((channels, spots), bf16),
        ]
        + [piece] * mesh_rows
        + [shape((4 * size, width), bf16)] * 4,
        scratch_shapes=[
            pltpu.VMEM((spots, width), f32),
            pltpu.VMEM((spots, width), bf16),
            pltpu.VMEM((spots, width), f32),
            pltpu.VMEM((spots, width), f32),
            pltpu.VMEM((mesh_rows, channels // mesh_rows, spots), bf16),
            pltpu.VMEM((mesh_rows, channels // mesh_rows, spots), bf16),
            pltpu.VMEM((2, 8, size, width), bf16),
            pltpu.VMEM((2, 2, size, width), bf16),
            pltpu.SemaphoreType.DMA((2, 8)),
            pltpu.SemaphoreType.DMA((2, 2)),
        ],
        compiler_params=pltpu.CompilerParams(vmem_limit_bytes=42 << 20),
        name="feed_forward",
    )(here, *wholes, *conv, *ups[:2], *downs[:2], *ups[2:], *downs[2:])


def put_slices(out_refs, rows_at, product, mesh_rows, rows):
    for i in range(mesh_rows):
        for core in range(2):
            for chip in range(4):
                start = ((i * 2 + core) * 4 + chip) * rows
                at = rows_at(i)
                out_refs[core][chip, at : at + rows, :] = product[start : start + rows, :].astype(bf16)


def late_kernel(grad_two_ref, low_ref, mixer_ref, mid_low_ref, near_ref, far_ref, product, *, mesh_rows, rows):
    for kind, pair in enumerate(((mixer_ref, mid_low_ref), (grad_two_ref, low_ref))):
        product[...] = dot(pair[0][...], pair[1][...], 1, 0)
        put_slices((near_ref, far_ref), lambda i: (2 * i + kind) * rows, product, mesh_rows, rows)


def rest_kernel(*refs, mesh_rows, rows):
    here_ref, sent = refs[0], refs[1 : 1 + mesh_rows]
    value_ref, one_ref, low_ref, filt_ref, near_ref, far_ref, grad_value_ref, grad_one_ref, product = refs[1 + mesh_rows :]
    size = sent[0].shape[0]
    for i, ref in enumerate(sent):
        at = pl.ds(pl.multiple_of((i ^ here_ref[0]) * size, size), size)
        mixed = ref[...].astype(f32)
        grad_value_ref[at, :] = (mixed * one_ref[at, :]).astype(bf16)
        grad_one_ref[at, :] = (mixed * value_ref[at, :]).astype(bf16)
    for kind, grad_ref in enumerate((grad_value_ref, grad_one_ref)):
        product[...] = dot(grad_ref[...], low_ref[...], 1, 0)
        put_slices((near_ref, far_ref), lambda i: (2 * i + kind) * rows, product, mesh_rows, rows)
    base = 2 * mesh_rows * rows
    for part in range(filt_ref.shape[0]):
        for core, ref in enumerate((near_ref, far_ref)):
            for chip in range(4):
                start = (core * 4 + chip) * rows
                at = base + part * rows
                ref[chip, at : at + rows, :] = filt_ref[part, start : start + rows, :].astype(bf16)


def first_norm_kernel(*refs, mesh_rows, rows):
    grads, pieces = refs[:3], refs[3:11]
    x_ref, gain_ref, mid_ref, tokens_ref, gain_grad_ref, gathered, acc = refs[11:]
    for slot, ref in enumerate(pieces):
        for i in range(mesh_rows):
            start = (i * 8 + slot) * rows
            for k, grad_ref in enumerate(grads):
                at = (i * 4 + k) * rows
                gathered[at : at + rows, :] = grad_ref[start : start + rows, :]
            at = (i * 4 + 3) * rows
            gathered[at : at + rows, :] = jnp.zeros((rows, gathered.shape[1]), bf16)
        term = tn(gathered[...], ref[...])
        acc[...] = term if slot == 0 else acc[...] + term
    unit, inverse = norm(x_ref[...].astype(f32))
    grad, gain_grad = norm_back(unit, inverse, gain_ref[...], acc[...])
    tokens_ref[...] = mid_ref[...] + grad
    gain_grad_ref[...] = gain_grad[None]


def add_low(*terms):
    return sum(term.astype(f32) for term in terms).astype(bf16)


def kept_kernel(
    up_ref, up_in, down_ref, down_in, late_ref, late_in, up_keep, up_send, down_keep, down_send, *, mesh_rows, hidden, rows
):
    for chip in range(4):
        for i in range(mesh_rows):
            at = slice((chip * mesh_rows + i) * hidden, (chip * mesh_rows + i + 1) * hidden)
            late = [slice((2 * i + kind) * rows, (2 * i + kind + 1) * rows) for kind in range(2)]
            out_ref, side = (up_send if chip & 1 else up_keep), chip >> 1
            out_ref[side, i, :hidden] = add_low(up_ref[at, :], up_in[at, :])
            out_ref[side, i, hidden:] = add_low(late_ref[chip, late[0], :], late_in[chip, late[0], :])
            out_ref, side = (down_send if chip >> 1 else down_keep), chip & 1
            out_ref[side, i, :hidden] = add_low(down_ref[at, :], down_in[at, :])
            out_ref[side, i, hidden:] = add_low(late_ref[chip, late[1], :], late_in[chip, late[1], :])


def pair_kernel(up_ref, up_in, down_ref, down_in, up_keep, up_send, down_keep, down_send):
    up_keep[...] = add_low(up_ref[0], up_in[0])
    up_send[...] = add_low(up_ref[1], up_in[1])
    down_keep[...] = add_low(down_ref[0], down_in[0])
    down_send[...] = add_low(down_ref[1], down_in[1])


def bulk_kernel(up_ref, up_in, down_ref, down_in, bulk_ref):
    mesh_rows, size = up_ref.shape[:2]
    for i in range(mesh_rows):
        bulk_ref[i, :size] = add_low(up_ref[i], up_in[i])
        bulk_ref[i, size:] = add_low(down_ref[i], down_in[i])


def split_kernel(near_ref, far_ref, *outs):
    for chip, out_ref in enumerate(outs):
        out_ref[...] = add_low(near_ref[chip], far_ref[chip])


def split_gain(gain):
    high = gain.astype(bf16)
    return high, (gain - high.astype(f32)).astype(bf16)


def rest_sum_kernel(
    here_ref, level_ref, p0, p1, p2, p3, kernel_ref, pad_ref, gain_one_ref, gain_two_ref, filt_ref, *sends, rows
):
    mesh_rows = len(sends)
    size, width = sends[0].shape
    size = size - 8
    pairs = [split_gain(ref[...]) for ref in (gain_one_ref, gain_two_ref)]
    gains = jnp.concatenate([pair[part].astype(f32) for part in range(2) for pair in pairs], axis=0)
    gains = jnp.concatenate([gains, jnp.zeros_like(gains)], axis=0).astype(bf16)
    for i, ref in enumerate(sends):
        at = pl.ds(pl.multiple_of((i ^ level_ref[0]) * size, 16), size)
        ref[:size] = add_low(*(part[at, :] for part in (p0, p1, p2, p3)))
        ref[size:] = gains
    taps = kernel_ref.shape[1]
    base = mesh_rows * size
    parts = filt_ref.shape[0] // rows
    grad = [
        sum(ref[base + part * rows : base + (part + 1) * rows, :].astype(f32) for ref in (p0, p1, p2, p3))
        for part in range(parts)
    ]
    grad = jnp.concatenate(grad, axis=1)[:, :taps]
    at = pl.ds(pl.multiple_of(here_ref[0] * rows, rows), rows)
    spot = lax.broadcasted_iota(jnp.int32, (rows, taps), 1)
    grad = jnp.where(spot < taps - pad_ref[at, :], grad, 0.0)
    before = jnp.where(spot == 0, 0.0, pltpu.roll(grad, 1, 1))
    behind = jnp.where(spot == taps - 1, 0.0, pltpu.roll(grad, taps - 1, 1))
    grad = jnp.where(jnp.abs(kernel_ref[at, :]) > thresh, (before + grad + behind) / 3.0, 0.0)
    for part in range(parts):
        size = min(width, taps - part * width)
        piece = grad[:, part * width : part * width + size].astype(bf16)
        filt_ref[part * rows : (part + 1) * rows, :size] = piece
        if size < width:
            filt_ref[part * rows : (part + 1) * rows, size:] = jnp.zeros((rows, width - size), bf16)


def mesh_sum_kernel(x_ref, out_ref):
    out_ref[...] = add_low(*(x_ref[i] for i in range(x_ref.shape[0])))


def tree_sum(terms):
    while len(terms) > 1:
        terms = [a + b for a, b in zip(terms[0::2], terms[1::2])]
    return terms[0]


def rest_mesh_sum_kernel(filt_ref, *refs):
    sent, out_ref = refs[:-1], refs[-1]
    size = sent[0].shape[0] - 8
    filt = filt_ref.shape[0]
    out_ref[:size] = add_low(*(ref[:size] for ref in sent))
    out_ref[size : size + filt] = filt_ref[...]
    gains = [ref[size:].astype(f32) for ref in sent]
    gains = tree_sum([gain[:2] + gain[2:4] for gain in gains])
    high, low = split_gain(gains)
    zeros = jnp.zeros((4, gains.shape[1]), f32)
    out_ref[size + filt :] = jnp.concatenate([high.astype(f32), low.astype(f32), zeros], axis=0).astype(bf16)


def slice_at(here, slot, rows):
    start = (here ^ (2 * (slot % 4) + slot // 4)) * rows
    return pl.ds(pl.multiple_of(start, 8), rows)


def unpack_bulk_kernel(here_ref, *refs, hidden, rows):
    pieces, (up_ref, down_ref, two_ref, out_ref, turned) = refs[:8], refs[8:]
    here = here_ref[0]
    size = hidden + rows
    for slot, ref in enumerate(pieces):
        at = slice_at(here, slot, hidden)
        turned[at, :] = ref[:hidden].astype(f32)
        down_ref[at, :] = ref[size : size + hidden].astype(f32)
        at = slice_at(here, slot, rows)
        out_ref[at, :] = ref[hidden:size].astype(f32)
        two_ref[at, :] = ref[size + hidden :].astype(f32)
    up_ref[...] = turned[...].T


def unpack_rest_kernel(here_ref, *refs, rows):
    pieces, (two_ref, in_ref, kernel_ref, gains_ref, gains) = refs[:8], refs[8:]
    width = in_ref.shape[2]
    taps = kernel_ref.shape[1]
    in_ref[2] = two_ref[...]
    for slot, ref in enumerate(pieces):
        at = slice_at(here_ref[0], slot, rows)
        in_ref[0, at, :] = ref[:rows].astype(f32)
        in_ref[1, at, :] = ref[rows : 2 * rows].astype(f32)
        parts = -(-taps // width)
        for part in range(parts):
            size = min(width, taps - part * width)
            block = ref[(2 + part) * rows : (3 + part) * rows].astype(f32)
            kernel_ref[at, part * width : part * width + size] = block[:, :size]
        gain = ref[(2 + parts) * rows :].astype(f32)
        gains[relative_index(here_ref[0], slot, 8)] = gain[:2] + gain[2:4]
    gains_ref[...] = sum(gains[slot] for slot in range(8))


def chips_of(x, done=()):
    return [x] + [swap(x, "dp", 2 * chip, done) for chip in range(1, 4)]


def far(x):
    return pltpu.with_memory_space_constraint(x, pltpu.HBM)


def levels_of(pieces):
    return [pieces[0]] + [swap(pieces[i], "mp", i) for i in range(1, len(pieces))]


def pair_of(pieces, done=()):
    return pieces + [swap(piece, "dp", 1, done) for piece in pieces]


def fast_body(
    tables,
    tokens,
    gain_first,
    input_weight,
    kernel,
    pad_len,
    output_weight,
    gain_second,
    up_weight,
    down_weight,
    cotangent,
):
    ways, mesh_rows = lax.axis_size("dp"), lax.axis_size("mp")
    here = lax.axis_index("dp")
    place = here.astype(jnp.int32)[None]
    level = lax.axis_index("mp").astype(jnp.int32)[None]
    x, grad_rows = tokens[0], cotangent[0]
    spots, width = x.shape
    length = spots * mesh_rows
    own_channels, taps = kernel.shape
    rows = own_channels // ways
    hidden = up_weight.shape[1] // ways
    channels = own_channels * mesh_rows
    sizes = dict(mesh_rows=mesh_rows, rows=rows)
    filt_parts = -(-taps // width)

    own_in = lax.dynamic_slice_in_dim(input_weight.transpose(1, 2, 0), here * rows, rows, 1)
    own_out = lax.dynamic_slice_in_dim(output_weight, here * rows, rows, 0)
    own_mixer = jnp.concatenate([own_in, own_out[None]])
    mixer_rows = turn(jnp.broadcast_to(own_mixer, (mesh_rows,) + own_mixer.shape))
    own_up = lax.dynamic_slice_in_dim(up_weight, here * hidden, hidden, 1).T
    own_down = lax.dynamic_slice_in_dim(down_weight, here * hidden, hidden, 0)
    own_feed = jnp.stack([own_up, own_down])
    own_feed = jnp.broadcast_to(own_feed, (mesh_rows,) + own_feed.shape)
    fspec = filter_slices(place, kernel, pad_len, tables, length, ways)
    feed_rows = turn(after(own_feed, mixer_rows))
    mixer = chips_of(after(mixer_rows, own_feed).reshape(-1, width), done=(fspec,))
    feed_rows = after(feed_rows, *mixer[1:])
    up, down = (feed_rows[:, side].reshape(-1, width) for side in range(2))
    up_x, down_y = swap(up, "dp", 2), swap(down, "dp", 4)
    mixer = [far(piece) for piece in pair_of(mixer)]

    outs = project(level, x, gain_first, mixer, mesh_rows)
    mixed_in, (value, gate_one, gate_two, weight_out, normed_low) = outs[:mesh_rows], outs[mesh_rows:]
    value, gate_one, gate_two = (part.reshape(channels, spots) for part in (value, gate_one, gate_two))
    weight_out = weight_out.reshape(channels, width)
    received = levels_of([part.reshape(own_channels, spots) for part in mixed_in])
    up_x, down_y = after(up_x, *received[1:]), after(down_y, *received[1:])
    quarter = ((2, mesh_rows * hidden, width), bf16)
    up_pair, down_pair = whole_call(stack_kernel, [quarter] * 2, name="feed_pairs", count=4, room=8)(
        up, up_x, down, down_y
    )
    up_pair, down_pair = swap(up_pair, "dp", 4), swap(down_pair, "dp", 2)
    *conv_out, uspec = conv_forward(level, received, fspec, tables)
    conv = levels_of(conv_out)
    ups = [after(up_pair, *conv[1:]), up, up_x]
    downs = [after(down_pair, *conv[1:]), down, down_y]
    ups, downs = (
        [pair, swap(pair, "dp", 1), one, two, swap(one, "dp", 1), swap(two, "dp", 1)]
        for pair, one, two in (ups, downs)
    )

    wide, tall = ((spots, width), f32), ((channels, spots), bf16)
    outs = feed_forward(
        level,
        (far(x), far(gate_two), far(weight_out), gain_second[None], far(grad_rows)),
        conv,
        ups,
        downs,
        channels,
    )
    mixer_low, block_out, grad_mid, mid_low, gain_second_grad, grad_two = outs[:6]
    grad_conv, (up_near, up_far, down_near, down_far) = outs[6 : 6 + mesh_rows], outs[6 + mesh_rows :]
    received = levels_of(grad_conv)
    late_shape = ((4, 2 * mesh_rows * rows, width), bf16)
    late_near, late_far = whole_call(
        partial(late_kernel, **sizes), [late_shape] * 2, [((channels, width), f32)], name="late_grads", count=4
    )(grad_two, normed_low, mixer_low, mid_low)
    half = ((2, mesh_rows, hidden + rows, width), bf16)
    up_keep, up_send, down_keep, down_send = whole_call(
        partial(kept_kernel, hidden=hidden, **sizes), [half] * 4, name="kept", count=6, room=20
    )(
        up_near,
        swap(up_far, "dp", 1, received[1:]),
        down_near,
        swap(down_far, "dp", 1, received[1:]),
        late_near,
        swap(late_far, "dp", 1, received[1:]),
    )
    up_in, down_in = swap(up_send, "dp", 2), swap(down_send, "dp", 4)

    outs = conv_mixed(level, received, fspec, tables)
    mixed_out, gspec = outs[:mesh_rows], outs[mesh_rows]
    mixed = levels_of(mixed_out)
    filt_grad = conv_filt(gspec, uspec, tables, taps, width, length)
    quarter = (half[0][1:], bf16)
    up_keep, up_send, down_keep, down_send = whole_call(
        pair_kernel, [quarter] * 4, name="kept_again", count=4, room=12
    )(up_keep, after(up_in, *mixed[1:]), down_keep, after(down_in, *mixed[1:]))
    up_in, down_in = swap(up_send, "dp", 4), swap(down_send, "dp", 2)
    rest_rows = (2 * mesh_rows + filt_parts) * rows
    rest_near, rest_far, grad_value, grad_one = whole_call(
        partial(rest_kernel, **sizes),
        [((4, rest_rows, width), bf16)] * 2 + [pltpu.HBM(*tall)] * 2,
        [((channels, width), f32)],
        name="rest_grads",
        smem=1,
        count=mesh_rows + 4,
        room=12,
    )(level, *mixed, value, gate_one, normed_low, filt_grad)
    rest = whole_call(split_kernel, [((rest_rows, width), bf16)] * 4, name="rest_kept", count=2)(
        rest_near, swap(rest_far, "dp", 1)
    )
    (bulk,) = whole_call(
        bulk_kernel, [pltpu.HBM((mesh_rows, 2 * (hidden + rows), width), bf16)], name="bulk_sum", count=4
    )(up_keep, after(up_in, rest_near), down_keep, after(down_in, rest_near))
    bulk = turn(bulk)
    rest = [rest[0]] + [swap(rest[chip], "dp", 2 * chip) for chip in range(1, 4)]
    grad_tokens, gain_first_grad = whole_call(
        partial(first_norm_kernel, **sizes),
        [wide, ((1, width), f32)],
        [((4 * mesh_rows * rows, spots), bf16), wide],
        name="first_norm_back",
        count=14,
        room=20,
    )(far(grad_value), far(grad_one), far(grad_two), *mixer, far(x), gain_first[None], far(grad_mid))
    rest = [rest[0]] + [after(piece, grad_tokens) for piece in rest[1:]]
    own_filt, *rest = whole_call(
        partial(rest_sum_kernel, rows=rows),
        [((filt_parts * rows, width), bf16)] + [((2 * rows + 8, width), bf16)] * mesh_rows,
        name="rest_sum",
        smem=2,
        count=8,
    )(place, level, *rest, kernel, pad_len[:, None], gain_first_grad, gain_second_grad)
    rest = levels_of(rest)
    (bulk,) = whole_call(mesh_sum_kernel, [(bulk.shape[1:], bf16)], name="bulk_mesh_sum", count=1)(
        after(bulk, *rest[1:])
    )
    bulk = chips_of(bulk)
    (rest,) = whole_call(
        rest_mesh_sum_kernel, [(((2 + filt_parts) * rows + 8, width), bf16)], name="rest_mesh_sum", count=1 + mesh_rows
    )(own_filt, *rest)
    rest = chips_of(rest)
    bulk = pair_of(bulk)
    rest = pair_of(rest)
    channel_rows = ((own_channels, width), f32)
    up_grad, down_grad, two_grad, out_grad = whole_call(
        partial(unpack_bulk_kernel, hidden=hidden, rows=rows),
        [(up_weight.shape, f32), (down_weight.shape, f32), channel_rows, channel_rows],
        [(down_weight.shape, f32)],
        name="unpack_bulk",
        smem=1,
        count=8,
        room=14,
    )(place, *bulk)
    in_grad, kernel_grad, gains = whole_call(
        partial(unpack_rest_kernel, rows=rows),
        [((3, own_channels, width), f32), (kernel.shape, f32), ((2, width), f32)],
        [((8, 2, width), f32)],
        name="unpack_rest",
        smem=1,
        count=9,
        room=8,
    )(place, *rest, two_grad)
    return (
        block_out[None],
        grad_tokens[None],
        gains[0],
        in_grad.transpose(2, 0, 1),
        kernel_grad,
        out_grad,
        gains[1],
        up_grad,
        down_grad,
    )


def body(tables, *arrays):
    ways = lax.axis_size("dp")
    whole_tiles = arrays[3].shape[0] % (8 * ways) == 0 and arrays[7].shape[1] % (32 * ways) == 0
    assert arrays[0].shape[0] == 1
    return (fast_body if ways == 8 and whole_tiles else plain_body)(tables, *arrays)


def solution(mesh):
    in_specs = (
        P("dp", "mp", None),
        P(),
        P(None, None, "mp"),
        P("mp", None),
        P("mp"),
        P("mp", None),
        P(),
        P(None, "mp"),
        P("mp", None),
        P("dp", "mp", None),
    )
    out_specs = (
        P("dp", "mp", None),
        P("dp", "mp", None),
        P(),
        P(None, None, "mp"),
        P("mp", None),
        P("mp", None),
        P(),
        P(None, "mp"),
        P("mp", None),
    )

    def program(tokens, *rest):
        tables = dft_tables(tokens.shape[1])
        inner = jax.shard_map(
            body, mesh=mesh, in_specs=((P(), P(), P()),) + in_specs, out_specs=out_specs, check_vma=False
        )
        return inner(tables, tokens, *rest)

    return program
```

```python
import math
from functools import partial

import jax
import jax.numpy as jnp
import numpy as np
from jax import lax
from jax.experimental import pallas as pl
from jax.experimental.pallas import tpu as pltpu
from jax.sharding import PartitionSpec as P

LANES = 128
ROWS = 16
BASE = 256
f32 = jnp.float32
bf16 = jnp.bfloat16


def dft_tables(length):
    radix = length // BASE
    spot = lax.iota(jnp.int32, BASE)
    angle = (spot[:, None] * spot[None] % BASE).astype(f32) * (2 * math.pi / BASE)
    cos, sin = jnp.cos(angle), jnp.sin(angle)
    matrix = jnp.concatenate(
        [jnp.concatenate([cos, -sin], axis=1), jnp.concatenate([sin, cos], axis=1)], axis=0
    )
    high = matrix.astype(bf16)
    low = (matrix - high.astype(f32)).astype(bf16)
    turn = 2 * np.pi * np.outer(np.arange(radix) + 0.25, np.arange(BASE)) / length
    twiddle = np.stack([np.cos(turn), np.sin(turn)]).astype(np.float32)
    return high, low, jnp.asarray(twiddle)


def times(re, im, angle):
    c, s = math.cos(angle), math.sin(angle)
    if abs(s) < 1e-12:
        return (re, im) if c > 0 else (-re, -im)
    if abs(c) < 1e-12:
        return (-im, re) if s > 0 else (im, -re)
    if abs(abs(c) - abs(s)) < 1e-12:
        a = abs(c)
        sc, ss = (a if c > 0 else -a), (1.0 if (s > 0) == (c > 0) else -1.0)
        if ss > 0:
            return (re - im) * sc, (re + im) * sc
        return (re + im) * sc, (im - re) * sc
    return re * c - im * s, re * s + im * c


def radix_dft(re, im, sign):
    n = len(re)
    if n == 1:
        return re, im
    er, ei = radix_dft(re[0::2], im[0::2], sign)
    odr, odi = radix_dft(re[1::2], im[1::2], sign)
    lo_r, lo_i, hi_r, hi_i = [], [], [], []
    for k in range(n // 2):
        tr, ti = times(odr[k], odi[k], sign * 2 * math.pi * k / n)
        lo_r.append(er[k] + tr)
        lo_i.append(ei[k] + ti)
        hi_r.append(er[k] - tr)
        hi_i.append(ei[k] - ti)
    return lo_r + hi_r, lo_i + hi_i


def split_in(load, twiddle_ref, store, radix, channels):
    def step(tile, carry):
        rows = pl.ds(pl.multiple_of(tile * ROWS, ROWS), ROWS)
        for half in range(BASE // LANES):
            lanes = slice(half * LANES, (half + 1) * LANES)
            re, im = [], []
            for block in range(radix):
                x = load(rows, block, half)
                angle = -2 * math.pi * block * 0.25 / radix
                re.append(x * math.cos(angle))
                im.append(x * math.sin(angle))
            re, im = radix_dft(re, im, -1)
            for k in range(radix):
                c = twiddle_ref[0, k : k + 1, lanes]
                s = twiddle_ref[1, k : k + 1, lanes]
                store(rows, k, half, re[k] * c + im[k] * s, im[k] * c - re[k] * s)
        return carry

    lax.fori_loop(0, channels // ROWS, step, 0)


def split_out(load, twiddle_ref, store, radix, channels, length):
    def step(tile, carry):
        rows = pl.ds(pl.multiple_of(tile * ROWS, ROWS), ROWS)
        for half in range(BASE // LANES):
            lanes = slice(half * LANES, (half + 1) * LANES)
            re, im = [], []
            for k in range(radix):
                vr, vi = load(rows, k, half)
                c = twiddle_ref[0, k : k + 1, lanes]
                s = twiddle_ref[1, k : k + 1, lanes]
                re.append(vr * c - vi * s)
                im.append(vr * s + vi * c)
            re, im = radix_dft(re, im, 1)
            for block in range(radix):
                angle = 2 * math.pi * block * 0.25 / radix
                store(
                    rows,
                    block,
                    half,
                    re[block] * (math.cos(angle) / length) - im[block] * (math.sin(angle) / length),
                )
        return carry

    lax.fori_loop(0, channels // ROWS, step, 0)


def forward_dot(z, matrix):
    return jnp.dot(z, matrix, preferred_element_type=f32)


def inverse_dot(y, matrix):
    return lax.dot_general(y, matrix, (((1,), (1,)), ((), ())), preferred_element_type=f32)


def product_loop(a_load, b_load, store, total_rows, conj):
    def step(tile, carry):
        rows = pl.ds(pl.multiple_of(tile * ROWS, ROWS), ROWS)
        for half in range(BASE // LANES):
            cr = slice(half * LANES, (half + 1) * LANES)
            ci = slice(BASE + half * LANES, BASE + (half + 1) * LANES)
            ar, ai = a_load(rows, cr), a_load(rows, ci)
            br, bi = b_load(rows, cr), b_load(rows, ci)
            if conj:
                store(rows, cr, ar * br + ai * bi)
                store(rows, ci, ai * br - ar * bi)
            else:
                store(rows, cr, ar * br - ai * bi)
                store(rows, ci, ai * br + ar * bi)
        return carry

    lax.fori_loop(0, total_rows // ROWS, step, 0)


def cut(ref, here, rows, block, half):
    width = ref.shape[-1]
    start = block * BASE + half * LANES
    return ref[(start // width) ^ here, rows, start % width : start % width + LANES].astype(f32)


def put(ref, here, rows, block, half, value):
    width = ref.shape[-1]
    start = block * BASE + half * LANES
    ref[(start // width) ^ here, rows, start % width : start % width + LANES] = value.astype(ref.dtype)


def rowshift(rows, k, channels):
    return pl.ds(pl.multiple_of(rows.start + k * channels, ROWS), ROWS)


def into_scratch(ref, channels):
    def store(rows, k, half, re, im):
        at = rowshift(rows, k, channels)
        ref[at, half * LANES : (half + 1) * LANES] = re.astype(ref.dtype)
        ref[at, BASE + half * LANES : BASE + (half + 1) * LANES] = im.astype(ref.dtype)

    return store


def from_scratch(ref, channels):
    def load(rows, k, half):
        at = rowshift(rows, k, channels)
        return (
            ref[at, half * LANES : (half + 1) * LANES].astype(f32),
            ref[at, BASE + half * LANES : BASE + (half + 1) * LANES].astype(f32),
        )

    return load


def filter_kernel(f_ref, high_ref, low_ref, twiddle_ref, spec_ref, zh, zl, *, radix, channels):
    def store(rows, k, half, re, im):
        at = rowshift(rows, k, channels)
        for value, base in ((re, 0), (im, BASE)):
            lanes = slice(base + half * LANES, base + (half + 1) * LANES)
            top = value.astype(bf16)
            zh[at, lanes] = top
            zl[at, lanes] = (value - top.astype(f32)).astype(bf16)

    split_in(partial(cut, f_ref, 0), twiddle_ref, store, radix, channels)
    spec_ref[...] = (
        forward_dot(zh[...], high_ref[...])
        + forward_dot(zl[...], high_ref[...])
        + forward_dot(zh[...], low_ref[...])
    )


def tile_load(ref):
    return lambda rows, lanes: ref[rows, lanes].astype(f32)


def tile_store(ref):
    def store(rows, lanes, value):
        ref[rows, lanes] = value.astype(ref.dtype)

    return store


def conv_kernel(here_ref, *refs, parts, radix, channels, length):
    sent, (fspec_ref, high_ref, twiddle_ref) = refs[:parts], refs[parts : parts + 3]
    outs, (uspec_ref, z, y, big, turned) = refs[parts + 3 : 2 * parts + 3], refs[2 * parts + 3 :]
    here = here_ref[0]
    for i, ref in enumerate(sent):
        turned[i ^ here] = ref[...]
    split_in(partial(cut, turned, 0), twiddle_ref, into_scratch(z, channels), radix, channels)
    big[...] = forward_dot(z[...], high_ref[...])
    uspec_ref[...] = big[...].astype(uspec_ref.dtype)
    product_loop(tile_load(big), tile_load(fspec_ref), tile_store(y), radix * channels, False)
    big[...] = inverse_dot(y[...], high_ref[...])
    split_out(from_scratch(big, channels), twiddle_ref, partial(put, turned, 0), radix, channels, length)
    for i, ref in enumerate(outs):
        ref[...] = turned[i ^ here]


def conv_mixed_kernel(here_ref, *refs, parts, radix, channels, length):
    sent, (fspec_ref, high_ref, twiddle_ref) = refs[:parts], refs[parts : parts + 3]
    mixed_ref, spec_ref, z, y, big, turned = refs[parts + 3 :]
    here = here_ref[0]
    for i, ref in enumerate(sent):
        turned[i ^ here] = ref[...]
    split_in(partial(cut, turned, 0), twiddle_ref, into_scratch(z, channels), radix, channels)
    big[...] = forward_dot(z[...], high_ref[...])
    spec_ref[...] = big[...].astype(bf16)
    product_loop(tile_load(big), tile_load(fspec_ref), tile_store(y), radix * channels, True)
    big[...] = inverse_dot(y[...], high_ref[...])
    split_out(from_scratch(big, channels), twiddle_ref, partial(put, mixed_ref, 0), radix, channels, length)


def conv_filt_kernel(
    gspec_ref, uspec_ref, high_ref, twiddle_ref, filt_ref, y, big, *, radix, channels, length, taps
):
    product_loop(tile_load(gspec_ref), tile_load(uspec_ref), tile_store(y), radix * channels, True)
    big[...] = inverse_dot(y[...], high_ref[...])
    filt_ref[filt_ref.shape[0] - 1] = jnp.zeros(filt_ref.shape[1:], filt_ref.dtype)

    def store(rows, block, half, value):
        if block * BASE + half * LANES < taps:
            put(filt_ref, 0, rows, block, half, value)

    split_out(from_scratch(big, channels), twiddle_ref, store, radix, channels, length)


VM = pl.BlockSpec(memory_space=pltpu.VMEM)
SM = pl.BlockSpec(memory_space=pltpu.SMEM)


def filter_spectrum(filt, tables):
    high, low, twiddle = tables
    channels, length = filt.shape[1], filt.shape[0] * filt.shape[2]
    radix = length // BASE
    rows = radix * channels
    return pl.pallas_call(
        partial(filter_kernel, radix=radix, channels=channels),
        out_shape=jax.ShapeDtypeStruct((rows, 2 * BASE), f32),
        in_specs=[VM] * 4,
        out_specs=VM,
        scratch_shapes=[pltpu.VMEM((rows, 2 * BASE), bf16)] * 2,
        name="filter_spectrum",
    )(filt, high, low, twiddle)


def conv_forward(here, pieces, fspec, tables):
    high, _, twiddle = tables
    parts = len(pieces)
    channels, width = pieces[0].shape
    length = parts * width
    radix = length // BASE
    rows = radix * channels
    return pl.pallas_call(
        partial(conv_kernel, parts=parts, radix=radix, channels=channels, length=length),
        out_shape=[jax.ShapeDtypeStruct((channels, width), bf16)] * parts + [pltpu.HBM((rows, 2 * BASE), bf16)],
        in_specs=[SM] + [VM] * (parts + 3),
        out_specs=[VM] * (parts + 1),
        scratch_shapes=[pltpu.VMEM((rows, 2 * BASE), bf16)] * 2
        + [pltpu.VMEM((rows, 2 * BASE), f32), pltpu.VMEM((parts, channels, width), bf16)],
        compiler_params=pltpu.CompilerParams(vmem_limit_bytes=16 << 20),
        name="conv_forward",
    )(here, *pieces, fspec, high, twiddle)


def conv_mixed(here, pieces, fspec, tables):
    high, _, twiddle = tables
    parts = len(pieces)
    channels, width = pieces[0].shape
    length = parts * width
    radix = length // BASE
    rows = radix * channels
    return pl.pallas_call(
        partial(conv_mixed_kernel, parts=parts, radix=radix, channels=channels, length=length),
        out_shape=(
            pltpu.HBM((parts, channels, width), bf16),
            pltpu.HBM((rows, 2 * BASE), bf16),
        ),
        in_specs=[SM] + [VM] * (parts + 3),
        out_specs=(VM, VM),
        scratch_shapes=[pltpu.VMEM((rows, 2 * BASE), bf16)] * 2
        + [pltpu.VMEM((rows, 2 * BASE), f32), pltpu.VMEM((parts, channels, width), bf16)],
        compiler_params=pltpu.CompilerParams(vmem_limit_bytes=16 << 20),
        name="conv_mixed",
    )(here, *pieces, fspec, high, twiddle)


def conv_filt(gspec, uspec, tables, taps, width, length):
    high, _, twiddle = tables
    rows = gspec.shape[0]
    radix = length // BASE
    channels = rows // radix
    return pl.pallas_call(
        partial(conv_filt_kernel, radix=radix, channels=channels, length=length, taps=taps),
        out_shape=jax.ShapeDtypeStruct((-(-taps // width), channels, width), f32),
        in_specs=[VM] * 4,
        out_specs=VM,
        scratch_shapes=[pltpu.VMEM((rows, 2 * BASE), bf16), pltpu.VMEM((rows, 2 * BASE), f32)],
        compiler_params=pltpu.CompilerParams(vmem_limit_bytes=16 << 20),
        name="conv_filt",
    )(gspec, uspec, high, twiddle)


thresh = 0.003
epsilon = 1e-05
gelu_scale = math.sqrt(2 / math.pi)
gelu_cube = 0.044715


def norm(values):
    centered = values - jnp.mean(values, axis=-1, keepdims=True)
    inverse = lax.rsqrt(jnp.mean(centered * centered, axis=-1, keepdims=True) + epsilon)
    return centered * inverse, inverse


def norm_back(unit, inverse, gain, grad):
    scaled = grad * gain
    mean = jnp.mean(scaled, axis=-1, keepdims=True)
    along = jnp.mean(scaled * unit, axis=-1, keepdims=True)
    return inverse * (scaled - mean - unit * along), jnp.sum(grad * unit, axis=0)


def shrink_pool(kernel, pad_len):
    shrunk = jax.nn.relu(kernel - thresh) - jax.nn.relu(-kernel - thresh)
    padded = jnp.pad(shrunk, ((0, 0), (1, 1)))
    pooled = (padded[:, :-2] + padded[:, 1:-1] + padded[:, 2:]) / 3.0
    positions = lax.broadcasted_iota(jnp.int32, pooled.shape, 1)
    return jnp.where(positions < (pooled.shape[1] - pad_len)[:, None], pooled, 0.0)


def gelu_both(values):
    cubic = gelu_cube * values * values
    turn = jnp.tanh(gelu_scale * (values + cubic * values))
    half = 0.5 * (1 + turn)
    slope = half + 0.5 * values * (1 - turn * turn) * (gelu_scale * (1 + 3 * cubic))
    return values * half, slope


def dot(a, b, over_a, over_b):
    return lax.dot_general(a, b, (((over_a,), (over_b,)), ((), ())), preferred_element_type=f32)


def after(x, *waits):
    return lax.optimization_barrier((x, waits))[0] if waits else x


def swap(x, axis, bit, done=()):
    return after(lax.ppermute(x, axis, [(i, i ^ bit) for i in range(lax.axis_size(axis))]), *done)


def gather(x, axis, stride=1, done=()):
    return jnp.stack([x] + [swap(x, axis, i, done) for i in range(stride, lax.axis_size(axis), stride)])


def scatter(x, axis, stride=1, done=()):
    terms = [x[0]] + [swap(x[i], axis, i * stride, done) for i in range(1, x.shape[0])]
    return sum(term.astype(f32) for term in terms)


class Gather:
    def __init__(self, x, bits):
        self.x, self.held, self.left = x, [], list(bits)

    def step(self, count=1, done=()):
        for bit in self.left[:count]:
            place = sum(other > bit for other in self.held)
            self.x = jnp.stack([self.x, swap(self.x, "dp", 1 << bit, done)], axis=place)
            self.held.append(bit)
        self.left = self.left[count:]
        return self

    def finish(self, done=()):
        self.step(len(self.left), done)
        return self.x.reshape((-1,) + self.x.shape[len(self.held) :])


def narrow_sum(*terms):
    return sum(term.astype(f32) for term in terms).astype(bf16)


class Reduction:
    def __init__(self, x, bits):
        self.x = x.reshape((2,) * len(bits) + x.shape[1:])
        self.held, self.left = sorted(bits, reverse=True), list(bits)

    def step(self, count=1, done=()):
        for bit in self.left[:count]:
            place = self.held.index(bit)
            self.held.remove(bit)
            keep, send = (lax.index_in_dim(self.x, side, place, keepdims=False) for side in (0, 1))
            self.x = narrow_sum(keep, swap(send, "dp", 1 << bit, done))
        self.left = self.left[count:]
        return self

    def finish(self, done=()):
        return self.step(len(self.left), done).x


def sum_all(x):
    for axis in ("dp", "mp"):
        bit = 1
        while bit < lax.axis_size(axis):
            x = x + swap(x, axis, bit)
            bit *= 2
    return x


def parts_of(x, axis, stride=1):
    return [x] + [swap(x, axis, i) for i in range(stride, lax.axis_size(axis), stride)]


def parts_for(x, axis):
    return [x[0]] + [swap(x[i], axis, i) for i in range(1, x.shape[0])]


def turn(x):
    return lax.all_to_all(x, "mp", 0, 0)


def exchange(x, done=()):
    return jnp.stack([x[0]] + [swap(x[i], "mp", i, done) for i in range(1, x.shape[0])])


def spread(x, *orders):
    x = x.astype(bf16)
    if orders:
        half = x.shape[0] // 16 * 8
        x = [Gather(part, bits).finish() for part, bits in zip((x[:half], x[half:]), orders)]
        x = jnp.concatenate(x, axis=1)
    else:
        x = gather(x, "dp", 2)
    return jnp.concatenate([x, swap(x, "dp", 1)])


class Spread:
    def __init__(self, x, *orders):
        half = x.shape[0] // 16 * 8
        self.parts = [Gather(part, bits) for part, bits in zip((x[:half], x[half:]), orders)]

    @property
    def x(self):
        return [part.x for part in self.parts]

    def step(self, done=()):
        for part in self.parts:
            part.step(done=done)

    def finish(self, done=()):
        x = jnp.concatenate([part.finish(done=done) for part in self.parts], axis=1)
        return jnp.concatenate([x, swap(x, "dp", 1)])


class Doubling:
    def __init__(self, x):
        self.x = x
        self.left = [
            (axis, 1 << bit) for axis in ("dp", "mp") for bit in range(lax.axis_size(axis).bit_length() - 1)
        ]

    def step(self):
        if self.left:
            self.x = self.x + swap(self.x, *self.left.pop(0))

    def finish(self):
        while self.left:
            self.step()


def absolute(x, start, rows):
    here = lax.axis_index("dp")
    count = x.shape[0]
    picks = []
    for index in range(count):
        relative = here ^ index
        at = (relative & 1) * (count // 2) + (relative >> 1)
        picks.append(lax.dynamic_slice(x, (at, start, 0), (1, rows, x.shape[2]))[0])
    return jnp.concatenate(picks).astype(f32)


def plain_body(
    tables,
    tokens,
    gain_first,
    input_weight,
    kernel,
    pad_len,
    output_weight,
    gain_second,
    up_weight,
    down_weight,
    cotangent,
):
    ways, rows_mp = lax.axis_size("dp"), lax.axis_size("mp")
    here_dp, here_mp = lax.axis_index("dp"), lax.axis_index("mp")
    chips = list(range(1, ways.bit_length() - 1))
    first_bits, second_bits = chips, chips[::-1]
    here = here_mp.astype(jnp.int32)[None]
    spots, width = tokens.shape[1:]
    length = spots * rows_mp
    own_channels = kernel.shape[0]
    slice_channels = own_channels // ways
    slice_hidden = up_weight.shape[1] // ways
    channels = own_channels * rows_mp

    own_in = lax.dynamic_slice_in_dim(input_weight, here_dp * slice_channels, slice_channels, 2)
    own_out = lax.dynamic_slice_in_dim(output_weight, here_dp * slice_channels, slice_channels, 0)
    mixer_rows = gather(jnp.concatenate([own_in.transpose(1, 2, 0), own_out[None]]), "mp")
    start_rows = tokens[0].astype(f32)
    unit_one, inverse_one = norm(start_rows)
    normed_low = (unit_one * gain_first).astype(bf16)
    own_up = lax.dynamic_slice_in_dim(up_weight, here_dp * slice_hidden, slice_hidden, 1).T
    own_down = lax.dynamic_slice_in_dim(down_weight, here_dp * slice_hidden, slice_hidden, 0)
    own_feed = jnp.stack([own_up, own_down])

    picks = []
    for core in range(2):
        for chip in range(ways // 2):
            at = (here_dp ^ (2 * chip + core)) * slice_channels
            picks.append(at)
    kernel_rel = jnp.concatenate([lax.dynamic_slice_in_dim(kernel, at, slice_channels, 0) for at in picks])
    pad_rel = jnp.concatenate([lax.dynamic_slice_in_dim(pad_len, at, slice_channels, 0) for at in picks])
    filt = shrink_pool(kernel_rel, pad_rel)
    fspec = filter_spectrum(jnp.pad(filt, ((0, 0), (0, length - filt.shape[1])))[None], tables)

    feed_rows = gather(after(own_feed, mixer_rows), "mp")
    mixer_rows = gather(after(mixer_rows, fspec, normed_low, own_feed), "dp", 2)
    feeds = [
        Gather(after(feed_rows[:, side], mixer_rows), bits).step()
        for side, bits in ((0, first_bits), (1, second_bits))
    ]
    mixer_rows = jnp.stack([mixer_rows, swap(mixer_rows, "dp", 1)])
    mixer_weights = mixer_rows.transpose(3, 2, 0, 1, 4, 5)
    weight_in = mixer_weights[:3].reshape(3 * channels, width)
    weight_out = mixer_weights[3].reshape(channels, width)

    proj = dot(weight_in, normed_low, 1, 1).reshape(3, channels, spots)
    value, gate_one, gate_two = proj[0], proj[1], proj[2]
    mixed_in = (value * gate_one).astype(bf16).reshape(rows_mp, own_channels, spots)
    for feed in feeds:
        feed.x = after(feed.x, mixed_in)
        feed.finish()
    *conv_out, uspec = conv_forward(here, list(exchange(mixed_in)), fspec, tables)
    conv_out = jnp.stack(conv_out)
    feeds = [after(feed.x, conv_out).reshape(-1, width) for feed in feeds]
    conv = exchange(conv_out).reshape(channels, spots).astype(f32)
    mixer_low = (gate_two * conv).astype(bf16)
    residual_one = start_rows + dot(mixer_low, weight_out, 0, 0)

    unit_two, inverse_two = norm(residual_one)
    second_low = (unit_two * gain_second).astype(bf16)
    grad_rows = cotangent[0]
    feeds = [[feed, swap(feed, "dp", 1)] for feed in feeds]
    block_out, grad_norm_two = residual_one, 0.0
    up_grads, down_grads = [], []
    for up, down in zip(*feeds):
        act, slope = gelu_both(dot(second_low, up, 1, 1))
        act_low = act.astype(bf16)
        grad_pre = (dot(grad_rows, down, 1, 1) * slope).astype(bf16)
        block_out = block_out + dot(act_low, down, 1, 0)
        grad_norm_two = grad_norm_two + dot(grad_pre, up, 1, 0)
        up_grads.append(dot(grad_pre, second_low, 0, 0).astype(bf16))
        down_grads.append(dot(act_low, grad_rows, 0, 0).astype(bf16))
    grad_mid_norm, gain_second_grad = norm_back(unit_two, inverse_two, gain_second, grad_norm_two)
    grad_mid = grad_rows.astype(f32) + grad_mid_norm
    mid_low = grad_mid.astype(bf16)

    chips_count = ways // 2

    def hidden_sum(parts, bits):
        kept = narrow_sum(parts[0], swap(parts[1], "dp", 1))
        return Reduction(kept.reshape(chips_count, rows_mp, slice_hidden, width), bits)

    down_sum = hidden_sum(down_grads, second_bits)
    up_sum = hidden_sum(up_grads, first_bits)

    def by_slice(parts):
        parts = [part.astype(bf16).reshape(rows_mp, 2, chips_count, slice_channels, width) for part in parts]
        return jnp.concatenate(parts, axis=3).transpose(1, 2, 0, 3, 4)

    grad_mixer = dot(weight_out, mid_low, 1, 1)
    grad_conv = (grad_mixer * gate_two).astype(bf16).reshape(rows_mp, own_channels, spots)
    grad_conv = exchange(grad_conv)
    grad_gate_two = (grad_mixer * conv).astype(bf16)
    out_grad = dot(mixer_low, mid_low, 1, 0)
    late = by_slice([dot(grad_gate_two, normed_low, 1, 0), out_grad])
    late = narrow_sum(late[0], swap(late[1], "dp", 1))
    grad_conv = after(grad_conv, down_sum.x, up_sum.x, late)
    mixed_out, gspec = conv_mixed(here, list(grad_conv), fspec, tables)
    filt_grad = conv_filt(gspec, uspec, tables, length, length, length)
    mixed_out = jnp.take(mixed_out, lax.iota(jnp.int32, rows_mp) ^ here_mp, axis=0)
    down_sum.step()
    up_sum.step()
    late = scatter(late, "dp", 2).astype(bf16)
    grad_mixed = exchange(mixed_out).reshape(channels, spots).astype(f32)
    grad_mixed = after(grad_mixed, down_sum.x, up_sum.x, late)
    grad_value = (grad_mixed * gate_one).astype(bf16)
    grad_gate_one = (grad_mixed * value).astype(bf16)
    rest = by_slice([dot(grad, normed_low, 1, 0) for grad in (grad_value, grad_gate_one)])
    grad_norm_one = dot(jnp.concatenate([grad_value, grad_gate_one, grad_gate_two]), weight_in, 0, 0)
    grad_start, gain_first_grad = norm_back(unit_one, inverse_one, gain_first, grad_norm_one)
    grad_tokens = grad_mid + grad_start

    taps = kernel.shape[1]
    filt_grad = filt_grad[0, :, :taps].astype(bf16).reshape(2, chips_count, -1, width)
    rest = jnp.concatenate([rest.reshape(2, chips_count, -1, width), filt_grad], axis=2)
    rest = scatter(narrow_sum(rest[0], swap(rest[1], "dp", 1)), "dp", 2)
    split = rest.shape[0] - filt_grad.shape[2]
    own_kernel = lax.dynamic_slice_in_dim(kernel, here_dp * slice_channels, slice_channels, 0)
    own_pad = lax.dynamic_slice_in_dim(pad_len, here_dp * slice_channels, slice_channels, 0)
    _, filter_back = jax.vjp(partial(shrink_pool, pad_len=own_pad), own_kernel)
    (own_filt,) = filter_back(rest[split:].reshape(slice_channels, taps))
    rest = scatter(rest[:split].astype(bf16).reshape(rows_mp, 2 * slice_channels, width), "mp")
    rest = spread(jnp.concatenate([rest, own_filt.reshape(-1, width)]))
    bulk = jnp.concatenate([up_sum.finish(), down_sum.finish(), late], axis=1)
    bulk = spread(scatter(bulk, "mp"))

    up_grad = absolute(bulk, 0, slice_hidden).T
    down_grad = absolute(bulk, slice_hidden, slice_hidden)
    in_grad = [
        absolute(rest, 0, slice_channels),
        absolute(rest, slice_channels, slice_channels),
        absolute(bulk, 2 * slice_hidden, slice_channels),
    ]
    in_full = jnp.stack(in_grad).transpose(2, 0, 1)
    out_full = absolute(bulk, 2 * slice_hidden + slice_channels, slice_channels)
    kernel_grad = absolute(rest, 2 * slice_channels, filt_grad.shape[2]).reshape(own_channels, taps)

    gains = sum_all(jnp.stack([gain_first_grad, gain_second_grad]))
    return (
        block_out.astype(bf16)[None],
        grad_tokens[None],
        gains[0],
        in_full,
        kernel_grad,
        out_full,
        gains[1],
        up_grad,
        down_grad,
    )


def whole_call(kernel, outs, scratch=(), name=None, smem=0, count=0, room=6):
    return pl.pallas_call(
        kernel,
        out_shape=tuple(out if isinstance(out, pl.MemoryRef) else jax.ShapeDtypeStruct(*out) for out in outs),
        in_specs=[SM] * smem + [VM] * count,
        out_specs=tuple(VM for _ in outs),
        scratch_shapes=[pltpu.VMEM(shape, dtype) for shape, dtype in scratch],
        compiler_params=pltpu.CompilerParams(vmem_limit_bytes=room << 20),
        name=name,
    )


def relative_index(here, place, count):
    chip, core = place % (count // 2), place // (count // 2)
    return here ^ (2 * chip + core)


def filter_slices_kernel(
    here_ref, kernel_ref, pad_ref, high_ref, low_ref, twiddle_ref, spec_ref, filt, zh, zl, *, radix, channels, ways
):
    here = here_ref[0]
    rows = channels // ways
    taps = kernel_ref.shape[1]
    filt[...] = jnp.zeros_like(filt)
    spot = lax.broadcasted_iota(jnp.int32, (8, taps), 1)
    for place in range(ways):
        start = relative_index(here, place, ways) * rows
        for tile in range(rows // 8):
            at = pl.ds(pl.multiple_of(start + tile * 8, 8), 8)
            raw = kernel_ref[at, :]
            shrunk = jnp.maximum(raw - thresh, 0.0) - jnp.maximum(-raw - thresh, 0.0)
            before = jnp.where(spot == 0, 0.0, pltpu.roll(shrunk, 1, 1))
            behind = jnp.where(spot == taps - 1, 0.0, pltpu.roll(shrunk, taps - 1, 1))
            pooled = (before + shrunk + behind) / 3.0
            kept = jnp.where(spot < taps - pad_ref[at, :], pooled, 0.0)
            put_rows = place * rows + tile * 8
            filt[0, put_rows : put_rows + 8, :taps] = kept
    filter_kernel(filt, high_ref, low_ref, twiddle_ref, spec_ref, zh, zl, radix=radix, channels=channels)


def filter_slices(here, kernel, pad_len, tables, length, ways):
    high, low, twiddle = tables
    channels = kernel.shape[0]
    radix = length // BASE
    rows = radix * channels
    return whole_call(
        partial(filter_slices_kernel, radix=radix, channels=channels, ways=ways),
        [((rows, 2 * BASE), f32)],
        [((1, channels, length), f32), ((rows, 2 * BASE), bf16), ((rows, 2 * BASE), bf16)],
        name="filter_spectrum",
        smem=1,
        count=5,
        room=14,
    )(here, far(kernel), pad_len[:, None], far(high), far(low), far(twiddle))[0]


def nt(a, b):
    return dot(a, b, 1, 1)


def tn(a, b):
    return dot(a, b, 0, 0)


def first_norm_forward_kernel(x_ref, gain_ref, low_ref):
    unit, _ = norm(x_ref[...].astype(f32))
    low_ref[...] = (unit * gain_ref[...]).astype(bf16)


def project_kernel(level_ref, low_ref, *refs, rows, mesh_rows):
    groups, sends = (refs[:8], refs[8:16]), refs[16 : 16 + mesh_rows]
    v_ref, one_ref, two_ref, out_ref, weights, sems = refs[16 + mesh_rows :]
    step = pl.program_id(0)

    def weight_copy(group, source, slot):
        size = source.shape[0]
        start = group * groups[0][0].shape[0]
        return pltpu.make_async_copy(source, weights.at[slot, pl.ds(start, size), :], sems.at[group, slot])

    @pl.when(step == 0)
    def _():
        for chip in range(4):
            for core in range(2):
                for group, pieces in enumerate(groups):
                    weight_copy(group, pieces[core * 4 + chip], core * 4 + chip).start()

    for core in range(2):
        slot = core * 4 + step
        for group, pieces in enumerate(groups):
            weight_copy(group, pieces[0], slot).wait()
        proj = nt(weights[slot], low_ref[...])
        for i, send_ref in enumerate(sends):
            to = i ^ level_ref[0]
            at = 4 * i * rows
            value, one, two = (proj[at + k * rows : at + (k + 1) * rows] for k in range(3))
            send_ref[core, 0] = (value * one).astype(bf16)
            v_ref[to, core, 0] = value
            one_ref[to, core, 0] = one
            two_ref[to, core, 0] = two
            out_ref[to, core, 0] = weights[slot, at + 3 * rows : at + 4 * rows, :]


def project(level, low, groups, mesh_rows):
    spots, width = low.shape
    size = sum(group[0].shape[0] for group in groups)
    rows = size // (4 * mesh_rows)
    block = lambda last: pl.BlockSpec((mesh_rows, 2, 1, rows, last), lambda j: (0, 0, j, 0, 0))
    shape = lambda last, dtype: pltpu.HBM((mesh_rows, 2, 4, rows, last), dtype)
    return pl.pallas_call(
        partial(project_kernel, rows=rows, mesh_rows=mesh_rows),
        grid=(4,),
        in_specs=[SM, VM] + [pl.BlockSpec(memory_space=pl.ANY)] * 16,
        out_specs=[pl.BlockSpec((2, 1, rows, spots), lambda j: (0, j, 0, 0))] * mesh_rows
        + [block(spots)] * 3
        + [block(width)],
        out_shape=[pltpu.HBM((2, 4, rows, spots), bf16)] * mesh_rows
        + [shape(spots, f32)] * 3
        + [shape(width, bf16)],
        scratch_shapes=[pltpu.VMEM((8, size, width), bf16), pltpu.SemaphoreType.DMA((2, 8))],
        compiler_params=pltpu.CompilerParams(vmem_limit_bytes=18 << 20),
        name="project",
    )(level, low, *groups[0], *groups[1])


def stack_kernel(*refs):
    for index, out_ref in enumerate(refs[len(refs) // 3 * 2 :]):
        out_ref[0] = refs[2 * index][...]
        out_ref[1] = refs[2 * index + 1][...]


def feed_kernel(*refs, mesh_rows):
    here_ref, x_ref, two_ref, out_weight_ref, gain_ref, grad_ref = refs[:6]
    sent, refs = refs[6 : 6 + mesh_rows], refs[6 + mesh_rows :]
    ups, downs, up_firsts, down_firsts = refs[:2], refs[2:4], refs[4:8], refs[8:12]
    mixer_ref, block_ref, mid_ref, mid_low_ref, gain_grad_ref, grad_two_ref = refs[12:18]
    sends, refs = refs[18 : 18 + mesh_rows], refs[18 + mesh_rows :]
    up_near, down_near, far_grads = refs[:3]
    residual, second, out_acc, norm_acc, conv, turned, weights, grads, sems, grad_sems = refs[3:]
    step = pl.program_id(0)
    size = weights.shape[2]
    copies = []
    for side, (firsts, pairs) in enumerate(((up_firsts, ups), (down_firsts, downs))):
        for k in range(8):
            core, chip = divmod(k, 4)
            first = (0, 1) if side == 0 else (0, 2)
            if chip in first:
                source = firsts[2 * core + first.index(chip)]
            else:
                source = pairs[core].at[0 if chip == (2 if side == 0 else 1) else 1]
            copies.append(pltpu.make_async_copy(source, weights.at[side, k], sems.at[side, k]))

    @pl.when(step == 0)
    def _():
        for copy in copies:
            copy.start()
        for i, ref in enumerate(sent):
            conv[i ^ here_ref[0]] = ref[...]
        mixer_ref[...] = (two_ref[...] * conv[...].reshape(two_ref.shape).astype(f32)).astype(bf16)
        residual[...] = x_ref[...].astype(f32) + tn(mixer_ref[...], out_weight_ref[...])
        unit, _ = norm(residual[...])
        second[...] = (unit * gain_ref[...]).astype(bf16)
        out_acc[...] = residual[...]
        norm_acc[...] = jnp.zeros_like(norm_acc)

    for side in range(2):
        pltpu.make_async_copy(up_firsts[0], weights.at[side, step], sems.at[side, step]).wait()
    slot = step % 2

    @pl.when(step >= 2)
    def _():
        for side in range(2):
            pltpu.make_async_copy(
                grads.at[side, slot], up_near.at[pl.ds(0, size), :], grad_sems.at[side, slot]
            ).wait()

    up, down = weights[0, step], weights[1, step]
    act, slope = gelu_both(nt(second[...], up))
    act_low = act.astype(bf16)
    grad_pre = (nt(grad_ref[...], down) * slope).astype(bf16)
    out_acc[...] += dot(act_low, down, 1, 0)
    norm_acc[...] += dot(grad_pre, up, 1, 0)
    grads[0, slot] = tn(grad_pre, second[...]).astype(bf16)
    grads[1, slot] = tn(act_low, grad_ref[...]).astype(bf16)
    at = pl.ds(pl.multiple_of((step % 4) * size, size), size)
    for core, outs in enumerate(((up_near, down_near), (far_grads.at[0], far_grads.at[1]))):

        @pl.when(step // 4 == core)
        def _():
            for side in range(2):
                pltpu.make_async_copy(
                    grads.at[side, slot], outs[side].at[at, :], grad_sems.at[side, slot]
                ).start()

    @pl.when(step == pl.num_programs(0) - 1)
    def _():
        unit, inverse = norm(residual[...])
        grad, gain_grad = norm_back(unit, inverse, gain_ref[...], norm_acc[...])
        gain_grad_ref[...] = gain_grad[None]
        mid = grad_ref[...].astype(f32) + grad
        mid_ref[...] = mid
        mid_low_ref[...] = mid.astype(bf16)
        block_ref[...] = out_acc[...].astype(bf16)
        grad_mixer = nt(out_weight_ref[...], mid_low_ref[...])
        flat = conv[...].reshape(two_ref.shape)
        grad_two_ref[...] = (grad_mixer * flat.astype(f32)).astype(bf16)
        turned[...] = (grad_mixer * two_ref[...]).astype(bf16).reshape(turned.shape)
        for i, ref in enumerate(sends):
            ref[...] = turned[i ^ here_ref[0]]
        for side in range(2):
            for last in range(2):
                pltpu.make_async_copy(
                    grads.at[side, last], up_near.at[pl.ds(0, size), :], grad_sems.at[side, last]
                ).wait()


def feed_forward(here, wholes, conv, ups, downs, channels):
    mesh_rows = len(conv)
    size, width = ups[2].shape
    spots = wholes[0].shape[0]
    shape = jax.ShapeDtypeStruct
    tall = shape((channels, spots), bf16)
    piece = shape((channels // mesh_rows, spots), bf16)
    anywhere = pl.BlockSpec(memory_space=pl.ANY)
    return pl.pallas_call(
        partial(feed_kernel, mesh_rows=mesh_rows),
        grid=(8,),
        in_specs=[SM] + [VM] * (len(wholes) + mesh_rows) + [anywhere] * 12,
        out_specs=[VM] * (6 + mesh_rows) + [anywhere] * 3,
        out_shape=[
            tall,
            pltpu.HBM((spots, width), bf16),
            pltpu.HBM((spots, width), f32),
            shape((spots, width), bf16),
            shape((1, width), f32),
            pltpu.HBM((channels, spots), bf16),
        ]
        + [piece] * mesh_rows
        + [shape((4 * size, width), bf16)] * 2
        + [shape((2, 4 * size, width), bf16)],
        scratch_shapes=[
            pltpu.VMEM((spots, width), f32),
            pltpu.VMEM((spots, width), bf16),
            pltpu.VMEM((spots, width), f32),
            pltpu.VMEM((spots, width), f32),
            pltpu.VMEM((mesh_rows, channels // mesh_rows, spots), bf16),
            pltpu.VMEM((mesh_rows, channels // mesh_rows, spots), bf16),
            pltpu.VMEM((2, 8, size, width), bf16),
            pltpu.VMEM((2, 2, size, width), bf16),
            pltpu.SemaphoreType.DMA((2, 8)),
            pltpu.SemaphoreType.DMA((2, 2)),
        ],
        compiler_params=pltpu.CompilerParams(vmem_limit_bytes=42 << 20),
        name="feed_forward",
    )(here, *wholes, *conv, *ups[:2], *downs[:2], *ups[2:], *downs[2:])


def put_slices(out_refs, rows_at, product, mesh_rows, rows):
    for i in range(mesh_rows):
        for core in range(2):
            for chip in range(4):
                start = ((i * 2 + core) * 4 + chip) * rows
                at = rows_at(i)
                out_refs[core][chip, at : at + rows, :] = product[start : start + rows, :].astype(bf16)


def late_kernel(grad_two_ref, low_ref, mixer_ref, mid_low_ref, near_ref, far_ref, product, *, mesh_rows, rows):
    for kind, pair in enumerate(((mixer_ref, mid_low_ref), (grad_two_ref, low_ref))):
        product[...] = dot(pair[0][...], pair[1][...], 1, 0)
        put_slices((near_ref, far_ref), lambda i: (2 * i + kind) * rows, product, mesh_rows, rows)


def rest_kernel(
    mixed_ref, value_ref, one_ref, low_ref, filt_ref, near_ref, far_ref, grad_value_ref, grad_one_ref, product,
    *, mesh_rows, rows,
):
    mixed = mixed_ref[...].astype(f32)
    grad_value_ref[...] = (mixed * one_ref[...]).astype(bf16)
    grad_one_ref[...] = (mixed * value_ref[...]).astype(bf16)
    for kind, grad_ref in enumerate((grad_value_ref, grad_one_ref)):
        product[...] = dot(grad_ref[...], low_ref[...], 1, 0)
        put_slices((near_ref, far_ref), lambda i: (2 * i + kind) * rows, product, mesh_rows, rows)
    base = 2 * mesh_rows * rows
    for part in range(filt_ref.shape[0]):
        for core, ref in enumerate((near_ref, far_ref)):
            for chip in range(4):
                start = (core * 4 + chip) * rows
                at = base + part * rows
                ref[chip, at : at + rows, :] = filt_ref[part, start : start + rows, :].astype(bf16)


def first_norm_kernel(level_ref, *refs, mesh_rows, rows):
    grads, groups = refs[:3], (refs[3:11], refs[11:19])
    x_ref, gain_ref, mid_ref, tokens_ref, gain_grad_ref, gathered, acc = refs[19:]
    split = groups[0][0].shape[0]
    for slot in range(8):
        for i in range(mesh_rows):
            start = slot * rows
            for k, grad_ref in enumerate(grads):
                at = (i * 4 + k) * rows
                gathered[at : at + rows, :] = grad_ref[i ^ level_ref[0], start : start + rows, :]
            at = (i * 4 + 3) * rows
            gathered[at : at + rows, :] = jnp.zeros((rows, gathered.shape[1]), bf16)
        term = tn(gathered[:split], groups[0][slot][...]) + tn(gathered[split:], groups[1][slot][...])
        acc[...] = term if slot == 0 else acc[...] + term
    unit, inverse = norm(x_ref[...].astype(f32))
    grad, gain_grad = norm_back(unit, inverse, gain_ref[...], acc[...])
    tokens_ref[...] = mid_ref[...] + grad
    gain_grad_ref[...] = gain_grad[None]


def add_low(*terms):
    return sum(term.astype(f32) for term in terms).astype(bf16)


def kept_kernel(
    up_ref, down_ref, far_in, late_ref, late_in, up_keep, up_send, down_keep, down_send, *, mesh_rows, hidden, rows
):
    for chip in range(4):
        for i in range(mesh_rows):
            at = slice((chip * mesh_rows + i) * hidden, (chip * mesh_rows + i + 1) * hidden)
            late = [slice((2 * i + kind) * rows, (2 * i + kind + 1) * rows) for kind in range(2)]
            out_ref, side = (up_send if chip & 1 else up_keep), chip >> 1
            out_ref[side, i, :hidden] = add_low(up_ref[at, :], far_in[0, at, :])
            out_ref[side, i, hidden:] = add_low(late_ref[chip, late[0], :], late_in[chip, late[0], :])
            out_ref, side = (down_send if chip >> 1 else down_keep), chip & 1
            out_ref[side, i, :hidden] = add_low(down_ref[at, :], far_in[1, at, :])
            out_ref[side, i, hidden:] = add_low(late_ref[chip, late[1], :], late_in[chip, late[1], :])


def pair_kernel(up_ref, up_in, down_ref, down_in, up_keep, up_send, down_keep, down_send):
    up_keep[...] = add_low(up_ref[0], up_in[0])
    up_send[...] = add_low(up_ref[1], up_in[1])
    down_keep[...] = add_low(down_ref[0], down_in[0])
    down_send[...] = add_low(down_ref[1], down_in[1])


def bulk_kernel(up_ref, up_in, down_ref, down_in, bulk_ref):
    mesh_rows, size = up_ref.shape[:2]
    for i in range(mesh_rows):
        bulk_ref[i, :size] = add_low(up_ref[i], up_in[i])
        bulk_ref[i, size:] = add_low(down_ref[i], down_in[i])


def split_kernel(near_ref, far_ref, *outs):
    for chip, out_ref in enumerate(outs):
        out_ref[...] = add_low(near_ref[chip], far_ref[chip])


def split_gain(gain):
    high = gain.astype(bf16)
    return high, (gain - high.astype(f32)).astype(bf16)


def rest_sum_kernel(
    here_ref, level_ref, p0, p1, p2, p3, kernel_ref, pad_ref, gain_one_ref, gain_two_ref, filt_ref, *sends, rows
):
    mesh_rows = len(sends)
    size, width = sends[0].shape
    size = size - 8
    pairs = [split_gain(ref[...]) for ref in (gain_one_ref, gain_two_ref)]
    gains = jnp.concatenate([pair[part].astype(f32) for part in range(2) for pair in pairs], axis=0)
    gains = jnp.concatenate([gains, jnp.zeros_like(gains)], axis=0).astype(bf16)
    for i, ref in enumerate(sends):
        at = pl.ds(pl.multiple_of((i ^ level_ref[0]) * size, 16), size)
        ref[:size] = add_low(*(part[at, :] for part in (p0, p1, p2, p3)))
        ref[size:] = gains
    taps = kernel_ref.shape[1]
    base = mesh_rows * size
    parts = filt_ref.shape[0] // rows
    grad = [
        sum(ref[base + part * rows : base + (part + 1) * rows, :].astype(f32) for ref in (p0, p1, p2, p3))
        for part in range(parts)
    ]
    grad = jnp.concatenate(grad, axis=1)[:, :taps]
    at = pl.ds(pl.multiple_of(here_ref[0] * rows, rows), rows)
    spot = lax.broadcasted_iota(jnp.int32, (rows, taps), 1)
    grad = jnp.where(spot < taps - pad_ref[at, :], grad, 0.0)
    before = jnp.where(spot == 0, 0.0, pltpu.roll(grad, 1, 1))
    behind = jnp.where(spot == taps - 1, 0.0, pltpu.roll(grad, taps - 1, 1))
    grad = jnp.where(jnp.abs(kernel_ref[at, :]) > thresh, (before + grad + behind) / 3.0, 0.0)
    for part in range(parts):
        size = min(width, taps - part * width)
        piece = grad[:, part * width : part * width + size].astype(bf16)
        filt_ref[part * rows : (part + 1) * rows, :size] = piece
        if size < width:
            filt_ref[part * rows : (part + 1) * rows, size:] = jnp.zeros((rows, width - size), bf16)


def mesh_sum_kernel(x_ref, out_ref):
    out_ref[...] = add_low(*(x_ref[i] for i in range(x_ref.shape[0])))


def tree_sum(terms):
    while len(terms) > 1:
        terms = [a + b for a, b in zip(terms[0::2], terms[1::2])]
    return terms[0]


def rest_mesh_sum_kernel(bulk_ref, filt_ref, *refs):
    sent, out_ref = refs[:-1], refs[-1]
    base = bulk_ref.shape[1]
    size = sent[0].shape[0] - 8
    filt = filt_ref.shape[0]
    mesh_sum_kernel(bulk_ref, out_ref.at[:base])
    out_ref[base : base + size] = add_low(*(ref[:size] for ref in sent))
    out_ref[base + size : base + size + filt] = filt_ref[...]
    gains = [ref[size:].astype(f32) for ref in sent]
    gains = tree_sum([gain[:2] + gain[2:4] for gain in gains])
    high, low = split_gain(gains)
    zeros = jnp.zeros((4, gains.shape[1]), f32)
    out_ref[base + size + filt :] = jnp.concatenate(
        [high.astype(f32), low.astype(f32), zeros], axis=0
    ).astype(bf16)


def slice_at(here, slot, rows):
    start = (here ^ (2 * (slot % 4) + slot // 4)) * rows
    return pl.ds(pl.multiple_of(start, 8), rows)


def unpack_kernel(here_ref, *refs, hidden, rows):
    pieces, (up_ref, down_ref, out_ref, in_ref, kernel_ref, gains_ref, turned, gains) = refs[:8], refs[8:]
    here = here_ref[0]
    width = in_ref.shape[2]
    taps = kernel_ref.shape[1]
    parts = -(-taps // width)
    for slot, ref in enumerate(pieces):
        at = slice_at(here, slot, hidden)
        turned[at, :] = ref[:hidden].astype(f32)
        start = hidden + rows
        down_ref[at, :] = ref[start : start + hidden].astype(f32)
        at = slice_at(here, slot, rows)
        out_ref[at, :] = ref[hidden : hidden + rows].astype(f32)
        start = 2 * hidden + rows
        for place, gate in enumerate((2, 0, 1)):
            in_ref[gate, at, :] = ref[start + place * rows : start + (place + 1) * rows].astype(f32)
        for part in range(parts):
            size = min(width, taps - part * width)
            block = ref[start + (3 + part) * rows : start + (4 + part) * rows].astype(f32)
            kernel_ref[at, part * width : part * width + size] = block[:, :size]
        gain = ref[start + (3 + parts) * rows :].astype(f32)
        gains[relative_index(here, slot, 8)] = gain[:2] + gain[2:4]
    gains_ref[...] = sum(gains[slot] for slot in range(8))
    up_ref[...] = turned[...].T


def chips_of(x, done=()):
    return [x] + [swap(x, "dp", 2 * chip, done) for chip in range(1, 4)]


def far(x):
    return pltpu.with_memory_space_constraint(x, pltpu.HBM)


def levels_of(pieces):
    return [pieces[0]] + [swap(pieces[i], "mp", i) for i in range(1, len(pieces))]


def stacked(*parts):
    shape = (len(parts),) + parts[0].shape
    (out,) = whole_call(stack_kernel, [(shape, bf16)], name="mixer_group", count=len(parts))(*parts)
    return out.reshape(-1, shape[-1])


def pair_of(pieces, done=()):
    return pieces + [swap(piece, "dp", 1, done) for piece in pieces]


def fast_body(
    tables,
    tokens,
    gain_first,
    input_weight,
    kernel,
    pad_len,
    output_weight,
    gain_second,
    up_weight,
    down_weight,
    cotangent,
):
    ways, mesh_rows = lax.axis_size("dp"), lax.axis_size("mp")
    here = lax.axis_index("dp")
    place = here.astype(jnp.int32)[None]
    level = lax.axis_index("mp").astype(jnp.int32)[None]
    x, grad_rows = tokens[0], cotangent[0]
    spots, width = x.shape
    length = spots * mesh_rows
    own_channels, taps = kernel.shape
    rows = own_channels // ways
    hidden = up_weight.shape[1] // ways
    channels = own_channels * mesh_rows
    sizes = dict(mesh_rows=mesh_rows, rows=rows)
    filt_parts = -(-taps // width)

    own_in = lax.dynamic_slice_in_dim(input_weight.transpose(1, 2, 0), here * rows, rows, 1)
    own_out = lax.dynamic_slice_in_dim(output_weight, here * rows, rows, 0)
    own_mixer = jnp.concatenate([own_in, own_out[None]]).reshape(-1, width)
    next_mixer = swap(own_mixer, "mp", 1)
    own_up = lax.dynamic_slice_in_dim(up_weight, here * hidden, hidden, 1).T
    own_down = lax.dynamic_slice_in_dim(down_weight, here * hidden, hidden, 0)
    own_feed = jnp.stack([own_up, own_down])
    own_feed = jnp.broadcast_to(own_feed, (mesh_rows,) + own_feed.shape)
    other_mixers = [swap(after(own_mixer, next_mixer), "mp", i) for i in range(2, mesh_rows)]
    fspec = filter_slices(place, kernel, pad_len, tables, length, ways)
    (normed_low,) = whole_call(
        first_norm_forward_kernel, [((spots, width), bf16)], name="first_norm", count=2, room=10
    )(x, gain_first[None])
    first_group = chips_of(stacked(own_mixer, next_mixer))
    other_mixers = [after(part, *first_group[1:], fspec, normed_low) for part in other_mixers]
    second_group = chips_of(stacked(*other_mixers))
    feed_rows = turn(after(own_feed, *other_mixers))
    mixer = [[far(piece) for piece in pair_of(group)] for group in (first_group, second_group)]

    outs = project(level, normed_low, mixer, mesh_rows)
    mixed_in, (value, gate_one, gate_two, weight_out) = outs[:mesh_rows], outs[mesh_rows:]
    value, gate_one, gate_two = (part.reshape(channels, spots) for part in (value, gate_one, gate_two))
    weight_out = weight_out.reshape(channels, width)
    received = levels_of([part.reshape(own_channels, spots) for part in mixed_in])
    feed_rows = after(feed_rows, value)
    up, down = (feed_rows[:, side].reshape(-1, width) for side in range(2))
    up_x, down_y = swap(up, "dp", 2), swap(down, "dp", 4)
    up_x, down_y = after(up_x, *received[1:]), after(down_y, *received[1:])
    quarter = ((2, mesh_rows * hidden, width), bf16)
    up_pair, down_pair = whole_call(stack_kernel, [quarter] * 2, name="feed_pairs", count=4, room=8)(
        up, up_x, down, down_y
    )
    up_pair, down_pair = swap(up_pair, "dp", 4), swap(down_pair, "dp", 2)
    *conv_out, uspec = conv_forward(level, received, fspec, tables)
    conv = levels_of(conv_out)
    ups = [after(up_pair, *conv[1:]), up, up_x]
    downs = [after(down_pair, *conv[1:]), down, down_y]
    ups, downs = (
        [pair, swap(pair, "dp", 1), one, two, swap(one, "dp", 1), swap(two, "dp", 1)]
        for pair, one, two in (ups, downs)
    )

    wide, tall = ((spots, width), f32), ((channels, spots), bf16)
    outs = feed_forward(
        level,
        (far(x), far(gate_two), far(weight_out), gain_second[None], far(grad_rows)),
        conv,
        ups,
        downs,
        channels,
    )
    mixer_low, block_out, grad_mid, mid_low, gain_second_grad, grad_two = outs[:6]
    grad_conv, (up_near, down_near, far_grads) = outs[6 : 6 + mesh_rows], outs[6 + mesh_rows :]
    received = levels_of(grad_conv)
    late_shape = ((4, 2 * mesh_rows * rows, width), bf16)
    late_near, late_far = whole_call(
        partial(late_kernel, **sizes), [late_shape] * 2, [((channels, width), f32)], name="late_grads", count=4
    )(far(grad_two), far(normed_low), mixer_low, mid_low)
    half = ((2, mesh_rows, hidden + rows, width), bf16)
    up_keep, up_send, down_keep, down_send = whole_call(
        partial(kept_kernel, hidden=hidden, **sizes), [pltpu.HBM(*half), half] * 2, name="kept", count=5, room=20
    )(up_near, down_near, swap(far_grads, "dp", 1), late_near, swap(late_far, "dp", 1))
    up_in, down_in = swap(up_send, "dp", 2), swap(down_send, "dp", 4)

    received = [received[0]] + [after(piece, up_keep) for piece in received[1:]]
    mixed_out, gspec = conv_mixed(level, received, fspec, tables)
    mixed = turn(mixed_out).reshape(channels, spots)
    filt_grad = conv_filt(gspec, uspec, tables, taps, width, length)
    quarter = (half[0][1:], bf16)
    up_keep, up_send, down_keep, down_send = whole_call(
        pair_kernel, [pltpu.HBM(*quarter), quarter] * 2, name="kept_again", count=4, room=12
    )(up_keep, after(up_in, mixed_out), down_keep, after(down_in, mixed_out))
    up_in, down_in = swap(up_send, "dp", 4), swap(down_send, "dp", 2)
    rest_rows = (2 * mesh_rows + filt_parts) * rows
    rest_near, rest_far, grad_value, grad_one = whole_call(
        partial(rest_kernel, **sizes),
        [pltpu.HBM((4, rest_rows, width), bf16), ((4, rest_rows, width), bf16)] + [pltpu.HBM(*tall)] * 2,
        [((channels, width), f32)],
        name="rest_grads",
        count=5,
        room=12,
    )(mixed, far(value), far(gate_one), far(normed_low), filt_grad)
    rest = whole_call(split_kernel, [((rest_rows, width), bf16)] * 4, name="rest_kept", count=2)(
        rest_near, swap(rest_far, "dp", 1)
    )
    (bulk,) = whole_call(
        bulk_kernel, [pltpu.HBM((mesh_rows, 2 * (hidden + rows), width), bf16)], name="bulk_sum", count=4
    )(up_keep, after(up_in, rest_near), down_keep, after(down_in, rest_near))
    bulk = turn(bulk)
    rest = [rest[0]] + [swap(rest[chip], "dp", 2 * chip) for chip in range(1, 4)]
    grad_tokens, gain_first_grad = whole_call(
        partial(first_norm_kernel, **sizes),
        [wide, ((1, width), f32)],
        [((4 * mesh_rows * rows, spots), bf16), wide],
        name="first_norm_back",
        smem=1,
        count=22,
        room=20,
    )(
        level,
        *(far(part.reshape(mesh_rows, own_channels, spots)) for part in (grad_value, grad_one, grad_two)),
        *mixer[0],
        *mixer[1],
        far(x),
        gain_first[None],
        far(grad_mid),
    )
    rest = [rest[0]] + [after(piece, grad_tokens) for piece in rest[1:]]
    own_filt, *rest = whole_call(
        partial(rest_sum_kernel, rows=rows),
        [((filt_parts * rows, width), bf16)] + [((2 * rows + 8, width), bf16)] * mesh_rows,
        name="rest_sum",
        smem=2,
        count=8,
    )(place, level, *rest, kernel, pad_len[:, None], gain_first_grad, gain_second_grad)
    rest = levels_of(rest)
    (mine,) = whole_call(
        rest_mesh_sum_kernel,
        [((bulk.shape[1] + (2 + filt_parts) * rows + 8, width), bf16)],
        name="mesh_sum",
        count=2 + mesh_rows,
        room=8,
    )(after(bulk, *rest[1:]), own_filt, *rest)
    up_grad, down_grad, out_grad, in_grad, kernel_grad, gains = whole_call(
        partial(unpack_kernel, hidden=hidden, rows=rows),
        [
            (up_weight.shape, f32),
            (down_weight.shape, f32),
            ((own_channels, width), f32),
            ((3, own_channels, width), f32),
            (kernel.shape, f32),
            ((2, width), f32),
        ],
        [(down_weight.shape, f32), ((8, 2, width), f32)],
        name="unpack",
        smem=1,
        count=8,
        room=24,
    )(place, *pair_of(chips_of(mine)))
    return (
        block_out[None],
        grad_tokens[None],
        gains[0],
        in_grad.transpose(2, 0, 1),
        kernel_grad,
        out_grad,
        gains[1],
        up_grad,
        down_grad,
    )


def body(tables, *arrays):
    ways = lax.axis_size("dp")
    whole_tiles = arrays[3].shape[0] % (8 * ways) == 0 and arrays[7].shape[1] % (32 * ways) == 0
    assert arrays[0].shape[0] == 1
    return (fast_body if ways == 8 and whole_tiles else plain_body)(tables, *arrays)


def solution(mesh):
    in_specs = (
        P("dp", "mp", None),
        P(),
        P(None, None, "mp"),
        P("mp", None),
        P("mp"),
        P("mp", None),
        P(),
        P(None, "mp"),
        P("mp", None),
        P("dp", "mp", None),
    )
    out_specs = (
        P("dp", "mp", None),
        P("dp", "mp", None),
        P(),
        P(None, None, "mp"),
        P("mp", None),
        P("mp", None),
        P(),
        P(None, "mp"),
        P("mp", None),
    )

    def program(tokens, *rest):
        tables = dft_tables(tokens.shape[1])
        inner = jax.shard_map(
            body, mesh=mesh, in_specs=((P(), P(), P()),) + in_specs, out_specs=out_specs, check_vma=False
        )
        return inner(tables, tokens, *rest)

    return program
```

```python
import math
from functools import partial

import jax
import jax.numpy as jnp
import numpy as np
from jax import lax
from jax.experimental import pallas as pl
from jax.experimental.pallas import tpu as pltpu
from jax.sharding import PartitionSpec as P

LANES = 128
FEED_PACK = 2
ROWS = 16
BASE = 256
f32 = jnp.float32
bf16 = jnp.bfloat16


def dft_tables(length):
    radix = length // BASE
    spot = lax.iota(jnp.int32, BASE)
    angle = (spot[:, None] * spot[None] % BASE).astype(f32) * (2 * math.pi / BASE)
    cos, sin = jnp.cos(angle), jnp.sin(angle)
    matrix = jnp.concatenate(
        [jnp.concatenate([cos, -sin], axis=1), jnp.concatenate([sin, cos], axis=1)], axis=0
    )
    high = matrix.astype(bf16)
    low = (matrix - high.astype(f32)).astype(bf16)
    turn = 2 * np.pi * np.outer(np.arange(radix) + 0.25, np.arange(BASE)) / length
    twiddle = np.stack([np.cos(turn), np.sin(turn)]).astype(np.float32)
    return high, low, jnp.asarray(twiddle)


def times(re, im, angle):
    c, s = math.cos(angle), math.sin(angle)
    if abs(s) < 1e-12:
        return (re, im) if c > 0 else (-re, -im)
    if abs(c) < 1e-12:
        return (-im, re) if s > 0 else (im, -re)
    if abs(abs(c) - abs(s)) < 1e-12:
        a = abs(c)
        sc, ss = (a if c > 0 else -a), (1.0 if (s > 0) == (c > 0) else -1.0)
        if ss > 0:
            return (re - im) * sc, (re + im) * sc
        return (re + im) * sc, (im - re) * sc
    return re * c - im * s, re * s + im * c


def radix_dft(re, im, sign):
    n = len(re)
    if n == 1:
        return re, im
    er, ei = radix_dft(re[0::2], im[0::2], sign)
    odr, odi = radix_dft(re[1::2], im[1::2], sign)
    lo_r, lo_i, hi_r, hi_i = [], [], [], []
    for k in range(n // 2):
        tr, ti = times(odr[k], odi[k], sign * 2 * math.pi * k / n)
        lo_r.append(er[k] + tr)
        lo_i.append(ei[k] + ti)
        hi_r.append(er[k] - tr)
        hi_i.append(ei[k] - ti)
    return lo_r + hi_r, lo_i + hi_i


def split_in(load, twiddle_ref, store, radix, channels):
    def step(tile, carry):
        rows = pl.ds(pl.multiple_of(tile * ROWS, ROWS), ROWS)
        for half in range(BASE // LANES):
            lanes = slice(half * LANES, (half + 1) * LANES)
            re, im = [], []
            for block in range(radix):
                x = load(rows, block, half)
                angle = -2 * math.pi * block * 0.25 / radix
                re.append(x * math.cos(angle))
                im.append(x * math.sin(angle))
            re, im = radix_dft(re, im, -1)
            for k in range(radix):
                c = twiddle_ref[0, k : k + 1, lanes]
                s = twiddle_ref[1, k : k + 1, lanes]
                store(rows, k, half, re[k] * c + im[k] * s, im[k] * c - re[k] * s)
        return carry

    lax.fori_loop(0, channels // ROWS, step, 0)


def split_out(load, twiddle_ref, store, radix, channels, length):
    def step(tile, carry):
        rows = pl.ds(pl.multiple_of(tile * ROWS, ROWS), ROWS)
        for half in range(BASE // LANES):
            lanes = slice(half * LANES, (half + 1) * LANES)
            re, im = [], []
            for k in range(radix):
                vr, vi = load(rows, k, half)
                c = twiddle_ref[0, k : k + 1, lanes]
                s = twiddle_ref[1, k : k + 1, lanes]
                re.append(vr * c - vi * s)
                im.append(vr * s + vi * c)
            re, im = radix_dft(re, im, 1)
            for block in range(radix):
                angle = 2 * math.pi * block * 0.25 / radix
                store(
                    rows,
                    block,
                    half,
                    re[block] * (math.cos(angle) / length) - im[block] * (math.sin(angle) / length),
                )
        return carry

    lax.fori_loop(0, channels // ROWS, step, 0)


def forward_dot(z, matrix):
    return jnp.dot(z, matrix, preferred_element_type=f32)


def inverse_dot(y, matrix):
    return lax.dot_general(y, matrix, (((1,), (1,)), ((), ())), preferred_element_type=f32)


def product_loop(a_load, b_load, store, total_rows, conj):
    def step(tile, carry):
        rows = pl.ds(pl.multiple_of(tile * ROWS, ROWS), ROWS)
        for half in range(BASE // LANES):
            cr = slice(half * LANES, (half + 1) * LANES)
            ci = slice(BASE + half * LANES, BASE + (half + 1) * LANES)
            ar, ai = a_load(rows, cr), a_load(rows, ci)
            br, bi = b_load(rows, cr), b_load(rows, ci)
            if conj:
                store(rows, cr, ar * br + ai * bi)
                store(rows, ci, ai * br - ar * bi)
            else:
                store(rows, cr, ar * br - ai * bi)
                store(rows, ci, ai * br + ar * bi)
        return carry

    lax.fori_loop(0, total_rows // ROWS, step, 0)


def cut(ref, here, rows, block, half):
    width = ref.shape[-1]
    start = block * BASE + half * LANES
    return ref[(start // width) ^ here, rows, start % width : start % width + LANES].astype(f32)


def put(ref, here, rows, block, half, value):
    width = ref.shape[-1]
    start = block * BASE + half * LANES
    ref[(start // width) ^ here, rows, start % width : start % width + LANES] = value.astype(ref.dtype)


def rowshift(rows, k, channels):
    return pl.ds(pl.multiple_of(rows.start + k * channels, ROWS), ROWS)


def into_scratch(ref, channels):
    def store(rows, k, half, re, im):
        at = rowshift(rows, k, channels)
        ref[at, half * LANES : (half + 1) * LANES] = re.astype(ref.dtype)
        ref[at, BASE + half * LANES : BASE + (half + 1) * LANES] = im.astype(ref.dtype)

    return store


def from_scratch(ref, channels):
    def load(rows, k, half):
        at = rowshift(rows, k, channels)
        return (
            ref[at, half * LANES : (half + 1) * LANES].astype(f32),
            ref[at, BASE + half * LANES : BASE + (half + 1) * LANES].astype(f32),
        )

    return load


def filter_kernel(f_ref, high_ref, low_ref, twiddle_ref, spec_ref, zh, zl, *, radix, channels):
    def store(rows, k, half, re, im):
        at = rowshift(rows, k, channels)
        for value, base in ((re, 0), (im, BASE)):
            lanes = slice(base + half * LANES, base + (half + 1) * LANES)
            top = value.astype(bf16)
            zh[at, lanes] = top
            zl[at, lanes] = (value - top.astype(f32)).astype(bf16)

    split_in(partial(cut, f_ref, 0), twiddle_ref, store, radix, channels)
    spec_ref[...] = (
        forward_dot(zh[...], high_ref[...])
        + forward_dot(zl[...], high_ref[...])
        + forward_dot(zh[...], low_ref[...])
    )


def tile_load(ref):
    return lambda rows, lanes: ref[rows, lanes].astype(f32)


def tile_store(ref):
    def store(rows, lanes, value):
        ref[rows, lanes] = value.astype(ref.dtype)

    return store


def conv_kernel(here_ref, *refs, parts, radix, channels, length):
    sent, (fspec_ref, high_ref, twiddle_ref) = refs[:parts], refs[parts : parts + 3]
    outs, (uspec_ref, z, y, big, turned) = refs[parts + 3 : 2 * parts + 3], refs[2 * parts + 3 :]
    here = here_ref[0]
    for i, ref in enumerate(sent):
        turned[i ^ here] = ref[...]
    split_in(partial(cut, turned, 0), twiddle_ref, into_scratch(z, channels), radix, channels)
    big[...] = forward_dot(z[...], high_ref[...])
    uspec_ref[...] = big[...].astype(uspec_ref.dtype)
    product_loop(tile_load(big), tile_load(fspec_ref), tile_store(y), radix * channels, False)
    big[...] = inverse_dot(y[...], high_ref[...])
    split_out(from_scratch(big, channels), twiddle_ref, partial(put, turned, 0), radix, channels, length)
    for i, ref in enumerate(outs):
        ref[...] = turned[i ^ here]


def conv_mixed_kernel(here_ref, *refs, parts, radix, channels, length):
    sent, (fspec_ref, high_ref, twiddle_ref) = refs[:parts], refs[parts : parts + 3]
    mixed_ref, spec_ref, z, y, big, turned = refs[parts + 3 :]
    here = here_ref[0]
    for i, ref in enumerate(sent):
        turned[i ^ here] = ref[...]
    split_in(partial(cut, turned, 0), twiddle_ref, into_scratch(z, channels), radix, channels)
    big[...] = forward_dot(z[...], high_ref[...])
    spec_ref[...] = big[...].astype(bf16)
    product_loop(tile_load(big), tile_load(fspec_ref), tile_store(y), radix * channels, True)
    big[...] = inverse_dot(y[...], high_ref[...])
    split_out(from_scratch(big, channels), twiddle_ref, partial(put, mixed_ref, 0), radix, channels, length)


def conv_filt_kernel(
    gspec_ref, uspec_ref, high_ref, twiddle_ref, filt_ref, y, big, *, radix, channels, length, taps
):
    product_loop(tile_load(gspec_ref), tile_load(uspec_ref), tile_store(y), radix * channels, True)
    big[...] = inverse_dot(y[...], high_ref[...])
    filt_ref[filt_ref.shape[0] - 1] = jnp.zeros(filt_ref.shape[1:], filt_ref.dtype)

    def store(rows, block, half, value):
        if block * BASE + half * LANES < taps:
            put(filt_ref, 0, rows, block, half, value)

    split_out(from_scratch(big, channels), twiddle_ref, store, radix, channels, length)


VM = pl.BlockSpec(memory_space=pltpu.VMEM)
SM = pl.BlockSpec(memory_space=pltpu.SMEM)


def filter_spectrum(filt, tables):
    high, low, twiddle = tables
    channels, length = filt.shape[1], filt.shape[0] * filt.shape[2]
    radix = length // BASE
    rows = radix * channels
    return pl.pallas_call(
        partial(filter_kernel, radix=radix, channels=channels),
        out_shape=jax.ShapeDtypeStruct((rows, 2 * BASE), f32),
        in_specs=[VM] * 4,
        out_specs=VM,
        scratch_shapes=[pltpu.VMEM((rows, 2 * BASE), bf16)] * 2,
        name="filter_spectrum",
    )(filt, high, low, twiddle)


def conv_forward(here, pieces, fspec, tables):
    high, _, twiddle = tables
    parts = len(pieces)
    channels, width = pieces[0].shape
    length = parts * width
    radix = length // BASE
    rows = radix * channels
    return pl.pallas_call(
        partial(conv_kernel, parts=parts, radix=radix, channels=channels, length=length),
        out_shape=[jax.ShapeDtypeStruct((channels, width), bf16)] * parts + [pltpu.HBM((rows, 2 * BASE), bf16)],
        in_specs=[SM] + [VM] * (parts + 3),
        out_specs=[VM] * (parts + 1),
        scratch_shapes=[pltpu.VMEM((rows, 2 * BASE), bf16)] * 2
        + [pltpu.VMEM((rows, 2 * BASE), f32), pltpu.VMEM((parts, channels, width), bf16)],
        compiler_params=pltpu.CompilerParams(vmem_limit_bytes=16 << 20),
        name="conv_forward",
    )(here, *pieces, fspec, high, twiddle)


def conv_mixed(here, pieces, fspec, tables):
    high, _, twiddle = tables
    parts = len(pieces)
    channels, width = pieces[0].shape
    length = parts * width
    radix = length // BASE
    rows = radix * channels
    return pl.pallas_call(
        partial(conv_mixed_kernel, parts=parts, radix=radix, channels=channels, length=length),
        out_shape=(
            pltpu.HBM((parts, channels, width), bf16),
            pltpu.HBM((rows, 2 * BASE), bf16),
        ),
        in_specs=[SM] + [VM] * (parts + 3),
        out_specs=(VM, VM),
        scratch_shapes=[pltpu.VMEM((rows, 2 * BASE), bf16)] * 2
        + [pltpu.VMEM((rows, 2 * BASE), f32), pltpu.VMEM((parts, channels, width), bf16)],
        compiler_params=pltpu.CompilerParams(vmem_limit_bytes=16 << 20),
        name="conv_mixed",
    )(here, *pieces, fspec, high, twiddle)


def conv_filt(gspec, uspec, tables, taps, width, length):
    high, _, twiddle = tables
    rows = gspec.shape[0]
    radix = length // BASE
    channels = rows // radix
    return pl.pallas_call(
        partial(conv_filt_kernel, radix=radix, channels=channels, length=length, taps=taps),
        out_shape=jax.ShapeDtypeStruct((-(-taps // width), channels, width), f32),
        in_specs=[VM] * 4,
        out_specs=VM,
        scratch_shapes=[pltpu.VMEM((rows, 2 * BASE), bf16), pltpu.VMEM((rows, 2 * BASE), f32)],
        compiler_params=pltpu.CompilerParams(vmem_limit_bytes=16 << 20),
        name="conv_filt",
    )(gspec, uspec, high, twiddle)


thresh = 0.003
epsilon = 1e-05
gelu_scale = math.sqrt(2 / math.pi)
gelu_cube = 0.044715


def norm(values):
    centered = values - jnp.mean(values, axis=-1, keepdims=True)
    inverse = lax.rsqrt(jnp.mean(centered * centered, axis=-1, keepdims=True) + epsilon)
    return centered * inverse, inverse


def norm_back(unit, inverse, gain, grad):
    scaled = grad * gain
    mean = jnp.mean(scaled, axis=-1, keepdims=True)
    along = jnp.mean(scaled * unit, axis=-1, keepdims=True)
    return inverse * (scaled - mean - unit * along), jnp.sum(grad * unit, axis=0)


def shrink_pool(kernel, pad_len):
    shrunk = jax.nn.relu(kernel - thresh) - jax.nn.relu(-kernel - thresh)
    padded = jnp.pad(shrunk, ((0, 0), (1, 1)))
    pooled = (padded[:, :-2] + padded[:, 1:-1] + padded[:, 2:]) / 3.0
    positions = lax.broadcasted_iota(jnp.int32, pooled.shape, 1)
    return jnp.where(positions < (pooled.shape[1] - pad_len)[:, None], pooled, 0.0)


def gelu_both(values):
    cubic = gelu_cube * values * values
    turn = jnp.tanh(gelu_scale * (values + cubic * values))
    half = 0.5 * (1 + turn)
    slope = half + 0.5 * values * (1 - turn * turn) * (gelu_scale * (1 + 3 * cubic))
    return values * half, slope


def dot(a, b, over_a, over_b):
    return lax.dot_general(a, b, (((over_a,), (over_b,)), ((), ())), preferred_element_type=f32)


def after(x, *waits):
    return lax.optimization_barrier((x, waits))[0] if waits else x


def swap(x, axis, bit, done=()):
    return after(lax.ppermute(x, axis, [(i, i ^ bit) for i in range(lax.axis_size(axis))]), *done)


def gather(x, axis, stride=1, done=()):
    return jnp.stack([x] + [swap(x, axis, i, done) for i in range(stride, lax.axis_size(axis), stride)])


def scatter(x, axis, stride=1, done=()):
    terms = [x[0]] + [swap(x[i], axis, i * stride, done) for i in range(1, x.shape[0])]
    return sum(term.astype(f32) for term in terms)


class Gather:
    def __init__(self, x, bits):
        self.x, self.held, self.left = x, [], list(bits)

    def step(self, count=1, done=()):
        for bit in self.left[:count]:
            place = sum(other > bit for other in self.held)
            self.x = jnp.stack([self.x, swap(self.x, "dp", 1 << bit, done)], axis=place)
            self.held.append(bit)
        self.left = self.left[count:]
        return self

    def finish(self, done=()):
        self.step(len(self.left), done)
        return self.x.reshape((-1,) + self.x.shape[len(self.held) :])


def narrow_sum(*terms):
    return sum(term.astype(f32) for term in terms).astype(bf16)


class Reduction:
    def __init__(self, x, bits):
        self.x = x.reshape((2,) * len(bits) + x.shape[1:])
        self.held, self.left = sorted(bits, reverse=True), list(bits)

    def step(self, count=1, done=()):
        for bit in self.left[:count]:
            place = self.held.index(bit)
            self.held.remove(bit)
            keep, send = (lax.index_in_dim(self.x, side, place, keepdims=False) for side in (0, 1))
            self.x = narrow_sum(keep, swap(send, "dp", 1 << bit, done))
        self.left = self.left[count:]
        return self

    def finish(self, done=()):
        return self.step(len(self.left), done).x


def sum_all(x):
    for axis in ("dp", "mp"):
        bit = 1
        while bit < lax.axis_size(axis):
            x = x + swap(x, axis, bit)
            bit *= 2
    return x


def parts_of(x, axis, stride=1):
    return [x] + [swap(x, axis, i) for i in range(stride, lax.axis_size(axis), stride)]


def parts_for(x, axis):
    return [x[0]] + [swap(x[i], axis, i) for i in range(1, x.shape[0])]


def turn(x):
    return lax.all_to_all(x, "mp", 0, 0)


def exchange(x, done=()):
    return jnp.stack([x[0]] + [swap(x[i], "mp", i, done) for i in range(1, x.shape[0])])


def spread(x, *orders):
    x = x.astype(bf16)
    if orders:
        half = x.shape[0] // 16 * 8
        x = [Gather(part, bits).finish() for part, bits in zip((x[:half], x[half:]), orders)]
        x = jnp.concatenate(x, axis=1)
    else:
        x = gather(x, "dp", 2)
    return jnp.concatenate([x, swap(x, "dp", 1)])


class Spread:
    def __init__(self, x, *orders):
        half = x.shape[0] // 16 * 8
        self.parts = [Gather(part, bits) for part, bits in zip((x[:half], x[half:]), orders)]

    @property
    def x(self):
        return [part.x for part in self.parts]

    def step(self, done=()):
        for part in self.parts:
            part.step(done=done)

    def finish(self, done=()):
        x = jnp.concatenate([part.finish(done=done) for part in self.parts], axis=1)
        return jnp.concatenate([x, swap(x, "dp", 1)])


class Doubling:
    def __init__(self, x):
        self.x = x
        self.left = [
            (axis, 1 << bit) for axis in ("dp", "mp") for bit in range(lax.axis_size(axis).bit_length() - 1)
        ]

    def step(self):
        if self.left:
            self.x = self.x + swap(self.x, *self.left.pop(0))

    def finish(self):
        while self.left:
            self.step()


def absolute(x, start, rows):
    here = lax.axis_index("dp")
    count = x.shape[0]
    picks = []
    for index in range(count):
        relative = here ^ index
        at = (relative & 1) * (count // 2) + (relative >> 1)
        picks.append(lax.dynamic_slice(x, (at, start, 0), (1, rows, x.shape[2]))[0])
    return jnp.concatenate(picks).astype(f32)


def plain_body(
    tables,
    tokens,
    gain_first,
    input_weight,
    kernel,
    pad_len,
    output_weight,
    gain_second,
    up_weight,
    down_weight,
    cotangent,
):
    ways, rows_mp = lax.axis_size("dp"), lax.axis_size("mp")
    here_dp, here_mp = lax.axis_index("dp"), lax.axis_index("mp")
    chips = list(range(1, ways.bit_length() - 1))
    first_bits, second_bits = chips, chips[::-1]
    here = here_mp.astype(jnp.int32)[None]
    spots, width = tokens.shape[1:]
    length = spots * rows_mp
    own_channels = kernel.shape[0]
    slice_channels = own_channels // ways
    slice_hidden = up_weight.shape[1] // ways
    channels = own_channels * rows_mp

    own_in = lax.dynamic_slice_in_dim(input_weight, here_dp * slice_channels, slice_channels, 2)
    own_out = lax.dynamic_slice_in_dim(output_weight, here_dp * slice_channels, slice_channels, 0)
    mixer_rows = gather(jnp.concatenate([own_in.transpose(1, 2, 0), own_out[None]]), "mp")
    start_rows = tokens[0].astype(f32)
    unit_one, inverse_one = norm(start_rows)
    normed_low = (unit_one * gain_first).astype(bf16)
    own_up = lax.dynamic_slice_in_dim(up_weight, here_dp * slice_hidden, slice_hidden, 1).T
    own_down = lax.dynamic_slice_in_dim(down_weight, here_dp * slice_hidden, slice_hidden, 0)
    own_feed = jnp.stack([own_up, own_down])

    picks = []
    for core in range(2):
        for chip in range(ways // 2):
            at = (here_dp ^ (2 * chip + core)) * slice_channels
            picks.append(at)
    kernel_rel = jnp.concatenate([lax.dynamic_slice_in_dim(kernel, at, slice_channels, 0) for at in picks])
    pad_rel = jnp.concatenate([lax.dynamic_slice_in_dim(pad_len, at, slice_channels, 0) for at in picks])
    filt = shrink_pool(kernel_rel, pad_rel)
    fspec = filter_spectrum(jnp.pad(filt, ((0, 0), (0, length - filt.shape[1])))[None], tables)

    feed_rows = gather(after(own_feed, mixer_rows), "mp")
    mixer_rows = gather(after(mixer_rows, fspec, normed_low, own_feed), "dp", 2)
    feeds = [
        Gather(after(feed_rows[:, side], mixer_rows), bits).step()
        for side, bits in ((0, first_bits), (1, second_bits))
    ]
    mixer_rows = jnp.stack([mixer_rows, swap(mixer_rows, "dp", 1)])
    mixer_weights = mixer_rows.transpose(3, 2, 0, 1, 4, 5)
    weight_in = mixer_weights[:3].reshape(3 * channels, width)
    weight_out = mixer_weights[3].reshape(channels, width)

    proj = dot(weight_in, normed_low, 1, 1).reshape(3, channels, spots)
    value, gate_one, gate_two = proj[0], proj[1], proj[2]
    mixed_in = (value * gate_one).astype(bf16).reshape(rows_mp, own_channels, spots)
    for feed in feeds:
        feed.x = after(feed.x, mixed_in)
        feed.finish()
    *conv_out, uspec = conv_forward(here, list(exchange(mixed_in)), fspec, tables)
    conv_out = jnp.stack(conv_out)
    feeds = [after(feed.x, conv_out).reshape(-1, width) for feed in feeds]
    conv = exchange(conv_out).reshape(channels, spots).astype(f32)
    mixer_low = (gate_two * conv).astype(bf16)
    residual_one = start_rows + dot(mixer_low, weight_out, 0, 0)

    unit_two, inverse_two = norm(residual_one)
    second_low = (unit_two * gain_second).astype(bf16)
    grad_rows = cotangent[0]
    feeds = [[feed, swap(feed, "dp", 1)] for feed in feeds]
    block_out, grad_norm_two = residual_one, 0.0
    up_grads, down_grads = [], []
    for up, down in zip(*feeds):
        act, slope = gelu_both(dot(second_low, up, 1, 1))
        act_low = act.astype(bf16)
        grad_pre = (dot(grad_rows, down, 1, 1) * slope).astype(bf16)
        block_out = block_out + dot(act_low, down, 1, 0)
        grad_norm_two = grad_norm_two + dot(grad_pre, up, 1, 0)
        up_grads.append(dot(grad_pre, second_low, 0, 0).astype(bf16))
        down_grads.append(dot(act_low, grad_rows, 0, 0).astype(bf16))
    grad_mid_norm, gain_second_grad = norm_back(unit_two, inverse_two, gain_second, grad_norm_two)
    grad_mid = grad_rows.astype(f32) + grad_mid_norm
    mid_low = grad_mid.astype(bf16)

    chips_count = ways // 2

    def hidden_sum(parts, bits):
        kept = narrow_sum(parts[0], swap(parts[1], "dp", 1))
        return Reduction(kept.reshape(chips_count, rows_mp, slice_hidden, width), bits)

    down_sum = hidden_sum(down_grads, second_bits)
    up_sum = hidden_sum(up_grads, first_bits)

    def by_slice(parts):
        parts = [part.astype(bf16).reshape(rows_mp, 2, chips_count, slice_channels, width) for part in parts]
        return jnp.concatenate(parts, axis=3).transpose(1, 2, 0, 3, 4)

    grad_mixer = dot(weight_out, mid_low, 1, 1)
    grad_conv = (grad_mixer * gate_two).astype(bf16).reshape(rows_mp, own_channels, spots)
    grad_conv = exchange(grad_conv)
    grad_gate_two = (grad_mixer * conv).astype(bf16)
    out_grad = dot(mixer_low, mid_low, 1, 0)
    late = by_slice([dot(grad_gate_two, normed_low, 1, 0), out_grad])
    late = narrow_sum(late[0], swap(late[1], "dp", 1))
    grad_conv = after(grad_conv, down_sum.x, up_sum.x, late)
    mixed_out, gspec = conv_mixed(here, list(grad_conv), fspec, tables)
    filt_grad = conv_filt(gspec, uspec, tables, length, length, length)
    mixed_out = jnp.take(mixed_out, lax.iota(jnp.int32, rows_mp) ^ here_mp, axis=0)
    down_sum.step()
    up_sum.step()
    late = scatter(late, "dp", 2).astype(bf16)
    grad_mixed = exchange(mixed_out).reshape(channels, spots).astype(f32)
    grad_mixed = after(grad_mixed, down_sum.x, up_sum.x, late)
    grad_value = (grad_mixed * gate_one).astype(bf16)
    grad_gate_one = (grad_mixed * value).astype(bf16)
    rest = by_slice([dot(grad, normed_low, 1, 0) for grad in (grad_value, grad_gate_one)])
    grad_norm_one = dot(jnp.concatenate([grad_value, grad_gate_one, grad_gate_two]), weight_in, 0, 0)
    grad_start, gain_first_grad = norm_back(unit_one, inverse_one, gain_first, grad_norm_one)
    grad_tokens = grad_mid + grad_start

    taps = kernel.shape[1]
    filt_grad = filt_grad[0, :, :taps].astype(bf16).reshape(2, chips_count, -1, width)
    rest = jnp.concatenate([rest.reshape(2, chips_count, -1, width), filt_grad], axis=2)
    rest = scatter(narrow_sum(rest[0], swap(rest[1], "dp", 1)), "dp", 2)
    split = rest.shape[0] - filt_grad.shape[2]
    own_kernel = lax.dynamic_slice_in_dim(kernel, here_dp * slice_channels, slice_channels, 0)
    own_pad = lax.dynamic_slice_in_dim(pad_len, here_dp * slice_channels, slice_channels, 0)
    _, filter_back = jax.vjp(partial(shrink_pool, pad_len=own_pad), own_kernel)
    (own_filt,) = filter_back(rest[split:].reshape(slice_channels, taps))
    rest = scatter(rest[:split].astype(bf16).reshape(rows_mp, 2 * slice_channels, width), "mp")
    rest = spread(jnp.concatenate([rest, own_filt.reshape(-1, width)]))
    bulk = jnp.concatenate([up_sum.finish(), down_sum.finish(), late], axis=1)
    bulk = spread(scatter(bulk, "mp"))

    up_grad = absolute(bulk, 0, slice_hidden).T
    down_grad = absolute(bulk, slice_hidden, slice_hidden)
    in_grad = [
        absolute(rest, 0, slice_channels),
        absolute(rest, slice_channels, slice_channels),
        absolute(bulk, 2 * slice_hidden, slice_channels),
    ]
    in_full = jnp.stack(in_grad).transpose(2, 0, 1)
    out_full = absolute(bulk, 2 * slice_hidden + slice_channels, slice_channels)
    kernel_grad = absolute(rest, 2 * slice_channels, filt_grad.shape[2]).reshape(own_channels, taps)

    gains = sum_all(jnp.stack([gain_first_grad, gain_second_grad]))
    return (
        block_out.astype(bf16)[None],
        grad_tokens[None],
        gains[0],
        in_full,
        kernel_grad,
        out_full,
        gains[1],
        up_grad,
        down_grad,
    )


def whole_call(kernel, outs, scratch=(), name=None, smem=0, count=0, room=6):
    return pl.pallas_call(
        kernel,
        out_shape=tuple(out if isinstance(out, pl.MemoryRef) else jax.ShapeDtypeStruct(*out) for out in outs),
        in_specs=[SM] * smem + [VM] * count,
        out_specs=tuple(VM for _ in outs),
        scratch_shapes=[pltpu.VMEM(shape, dtype) for shape, dtype in scratch],
        compiler_params=pltpu.CompilerParams(vmem_limit_bytes=room << 20),
        name=name,
    )


def relative_index(here, place, count):
    chip, core = place % (count // 2), place // (count // 2)
    return here ^ (2 * chip + core)


def filter_slices_kernel(
    here_ref, kernel_ref, pad_ref, high_ref, low_ref, twiddle_ref, spec_ref, filt, zh, zl, *, radix, channels, ways
):
    here = here_ref[0]
    rows = channels // ways
    taps = kernel_ref.shape[1]
    filt[...] = jnp.zeros_like(filt)
    spot = lax.broadcasted_iota(jnp.int32, (8, taps), 1)

    def step(tile, carry):
        place = tile // (rows // 8)
        start = relative_index(here, place, ways) * rows + (tile % (rows // 8)) * 8
        at = pl.ds(pl.multiple_of(start, 8), 8)
        raw = kernel_ref[at, :]
        shrunk = jnp.maximum(raw - thresh, 0.0) - jnp.maximum(-raw - thresh, 0.0)
        before = jnp.where(spot == 0, 0.0, pltpu.roll(shrunk, 1, 1))
        behind = jnp.where(spot == taps - 1, 0.0, pltpu.roll(shrunk, taps - 1, 1))
        pooled = (before + shrunk + behind) / 3.0
        filt[0, pl.ds(pl.multiple_of(tile * 8, 8), 8), :taps] = jnp.where(spot < taps - pad_ref[at, :], pooled, 0.0)
        return carry

    lax.fori_loop(0, channels // 8, step, 0)
    filter_kernel(filt, high_ref, low_ref, twiddle_ref, spec_ref, zh, zl, radix=radix, channels=channels)


def filter_slices(here, kernel, pad_len, tables, length, ways):
    high, low, twiddle = tables
    channels = kernel.shape[0]
    radix = length // BASE
    rows = radix * channels
    return whole_call(
        partial(filter_slices_kernel, radix=radix, channels=channels, ways=ways),
        [((rows, 2 * BASE), f32)],
        [((1, channels, length), f32), ((rows, 2 * BASE), bf16), ((rows, 2 * BASE), bf16)],
        name="filter_spectrum",
        smem=1,
        count=5,
        room=14,
    )(here, far(kernel), pad_len[:, None], far(high), far(low), far(twiddle))[0]


def nt(a, b):
    return dot(a, b, 1, 1)


def tn(a, b):
    return dot(a, b, 0, 0)


def first_norm_forward_kernel(x_ref, gain_ref, low_ref):
    unit, _ = norm(x_ref[...].astype(f32))
    low_ref[...] = (unit * gain_ref[...]).astype(bf16)


def project_kernel(level_ref, low_ref, *refs, rows, mesh_rows):
    groups, sends = (refs[:8], refs[8:16]), refs[16 : 16 + mesh_rows]
    v_ref, one_ref, two_ref, out_ref, weights, sems = refs[16 + mesh_rows :]
    step = pl.program_id(0)

    def weight_copy(group, source, slot):
        size = source.shape[0]
        start = group * groups[0][0].shape[0]
        return pltpu.make_async_copy(source, weights.at[slot, pl.ds(start, size), :], sems.at[group, slot])

    @pl.when(step == 0)
    def _():
        for chip in range(4):
            for core in range(2):
                for group, pieces in enumerate(groups):
                    weight_copy(group, pieces[core * 4 + chip], 2 * chip + core).start()

    for core in range(2):
        for group, pieces in enumerate(groups):
            weight_copy(group, pieces[0], 2 * step + core).wait()
    size = weights.shape[1]
    proj = nt(weights[pl.ds(2 * step, 2)].reshape(2 * size, weights.shape[2]), low_ref[...])
    for core in range(2):
        for i, send_ref in enumerate(sends):
            to = i ^ level_ref[0]
            at = 4 * i * rows
            start = core * size + at
            value, one, two = (proj[start + k * rows : start + (k + 1) * rows] for k in range(3))
            send_ref[core, 0] = (value * one).astype(bf16)
            v_ref[to, core, 0] = value
            one_ref[to, core, 0] = one
            two_ref[to, core, 0] = two
            out_ref[to, core, 0] = weights[2 * step + core, at + 3 * rows : at + 4 * rows, :]


def project(level, low, groups, mesh_rows):
    spots, width = low.shape
    size = sum(group[0].shape[0] for group in groups)
    rows = size // (4 * mesh_rows)
    block = lambda last: pl.BlockSpec((mesh_rows, 2, 1, rows, last), lambda j: (0, 0, j, 0, 0))
    shape = lambda last, dtype: pltpu.HBM((mesh_rows, 2, 4, rows, last), dtype)
    return pl.pallas_call(
        partial(project_kernel, rows=rows, mesh_rows=mesh_rows),
        grid=(4,),
        in_specs=[SM, VM] + [pl.BlockSpec(memory_space=pl.ANY)] * 16,
        out_specs=[pl.BlockSpec((2, 1, rows, spots), lambda j: (0, j, 0, 0))] * mesh_rows
        + [block(spots)] * 3
        + [block(width)],
        out_shape=[pltpu.HBM((2, 4, rows, spots), bf16)] * mesh_rows
        + [shape(spots, f32)] * 3
        + [shape(width, bf16)],
        scratch_shapes=[pltpu.VMEM((8, size, width), bf16), pltpu.SemaphoreType.DMA((2, 8))],
        compiler_params=pltpu.CompilerParams(vmem_limit_bytes=18 << 20),
        name="project",
    )(level, low, *groups[0], *groups[1])


def stack_kernel(*refs):
    for index, out_ref in enumerate(refs[len(refs) // 3 * 2 :]):
        out_ref[0] = refs[2 * index][...]
        out_ref[1] = refs[2 * index + 1][...]


def feed_kernel(*refs, mesh_rows):
    here_ref, x_ref, two_ref, out_weight_ref, gain_ref, grad_ref = refs[:6]
    sent, refs = refs[6 : 6 + mesh_rows], refs[6 + mesh_rows :]
    ups, downs, up_firsts, down_firsts = refs[:2], refs[2:4], refs[4:8], refs[8:12]
    mixer_ref, block_ref, mid_ref, mid_low_ref, gain_grad_ref, grad_two_ref = refs[12:18]
    sends, refs = refs[18 : 18 + mesh_rows], refs[18 + mesh_rows :]
    up_near, down_near, far_grads = refs[:3]
    residual, second, out_acc, norm_acc, conv, turned, weights, grads, sems, grad_sems = refs[3:]
    step = pl.program_id(0)
    size = weights.shape[2]
    pack = grads.shape[2] // size
    copies = []
    for side, (firsts, pairs) in enumerate(((up_firsts, ups), (down_firsts, downs))):
        for k in range(8):
            core, chip = divmod(k, 4)
            first = (0, 1) if side == 0 else (0, 2)
            if chip in first:
                source = firsts[2 * core + first.index(chip)]
            else:
                source = pairs[core].at[0 if chip == (2 if side == 0 else 1) else 1]
            copies.append(pltpu.make_async_copy(source, weights.at[side, k], sems.at[side, k]))

    @pl.when(step == 0)
    def _():
        for copy in copies:
            copy.start()
        for i, ref in enumerate(sent):
            conv[i ^ here_ref[0]] = ref[...]
        mixer_ref[...] = (two_ref[...] * conv[...].reshape(two_ref.shape).astype(f32)).astype(bf16)
        residual[...] = x_ref[...].astype(f32) + tn(mixer_ref[...], out_weight_ref[...])
        unit, _ = norm(residual[...])
        second[...] = (unit * gain_ref[...]).astype(bf16)
        out_acc[...] = residual[...]
        norm_acc[...] = jnp.zeros_like(norm_acc)

    for side in range(2):
        for k in range(pack):
            at = step * pack + k
            pltpu.make_async_copy(up_firsts[0], weights.at[side, at], sems.at[side, at]).wait()
    slot = step % 2

    @pl.when(step >= 2)
    def _():
        for side in range(2):
            pltpu.make_async_copy(
                grads.at[side, slot], up_near.at[pl.ds(0, pack * size), :], grad_sems.at[side, slot]
            ).wait()

    width = second.shape[1]
    up, down = (weights[side, pl.ds(step * pack, pack)].reshape(pack * size, width) for side in range(2))
    act, slope = gelu_both(nt(second[...], up))
    act_low = act.astype(bf16)
    grad_pre = (nt(grad_ref[...], down) * slope).astype(bf16)
    out_acc[...] += dot(act_low, down, 1, 0)
    norm_acc[...] += dot(grad_pre, up, 1, 0)
    grads[0, slot] = tn(grad_pre, second[...]).astype(bf16)
    grads[1, slot] = tn(act_low, grad_ref[...]).astype(bf16)
    steps = 4 // pack
    at = pl.ds(pl.multiple_of((step % steps) * pack * size, size), pack * size)
    for core, outs in enumerate(((up_near, down_near), (far_grads.at[0], far_grads.at[1]))):

        @pl.when(step // steps == core)
        def _():
            for side in range(2):
                pltpu.make_async_copy(
                    grads.at[side, slot], outs[side].at[at, :], grad_sems.at[side, slot]
                ).start()

    @pl.when(step == pl.num_programs(0) - 1)
    def _():
        unit, inverse = norm(residual[...])
        grad, gain_grad = norm_back(unit, inverse, gain_ref[...], norm_acc[...])
        gain_grad_ref[...] = gain_grad[None]
        mid = grad_ref[...].astype(f32) + grad
        mid_ref[...] = mid
        mid_low_ref[...] = mid.astype(bf16)
        block_ref[...] = out_acc[...].astype(bf16)
        grad_mixer = nt(out_weight_ref[...], mid_low_ref[...])
        flat = conv[...].reshape(two_ref.shape)
        grad_two_ref[...] = (grad_mixer * flat.astype(f32)).astype(bf16)
        turned[...] = (grad_mixer * two_ref[...]).astype(bf16).reshape(turned.shape)
        for i, ref in enumerate(sends):
            ref[...] = turned[i ^ here_ref[0]]
        for side in range(2):
            for last in range(2):
                pltpu.make_async_copy(
                    grads.at[side, last], up_near.at[pl.ds(0, pack * size), :], grad_sems.at[side, last]
                ).wait()


def feed_forward(here, wholes, conv, ups, downs, channels):
    mesh_rows = len(conv)
    size, width = ups[2].shape
    spots = wholes[0].shape[0]
    shape = jax.ShapeDtypeStruct
    tall = shape((channels, spots), bf16)
    piece = shape((channels // mesh_rows, spots), bf16)
    anywhere = pl.BlockSpec(memory_space=pl.ANY)
    return pl.pallas_call(
        partial(feed_kernel, mesh_rows=mesh_rows),
        grid=(8 // FEED_PACK,),
        in_specs=[SM] + [VM] * (len(wholes) + mesh_rows) + [anywhere] * 12,
        out_specs=[VM] * (6 + mesh_rows) + [anywhere] * 3,
        out_shape=[
            tall,
            pltpu.HBM((spots, width), bf16),
            pltpu.HBM((spots, width), f32),
            shape((spots, width), bf16),
            shape((1, width), f32),
            pltpu.HBM((channels, spots), bf16),
        ]
        + [piece] * mesh_rows
        + [shape((4 * size, width), bf16)] * 2
        + [shape((2, 4 * size, width), bf16)],
        scratch_shapes=[
            pltpu.VMEM((spots, width), f32),
            pltpu.VMEM((spots, width), bf16),
            pltpu.VMEM((spots, width), f32),
            pltpu.VMEM((spots, width), f32),
            pltpu.VMEM((mesh_rows, channels // mesh_rows, spots), bf16),
            pltpu.VMEM((mesh_rows, channels // mesh_rows, spots), bf16),
            pltpu.VMEM((2, 8, size, width), bf16),
            pltpu.VMEM((2, 2, FEED_PACK * size, width), bf16),
            pltpu.SemaphoreType.DMA((2, 8)),
            pltpu.SemaphoreType.DMA((2, 2)),
        ],
        compiler_params=pltpu.CompilerParams(vmem_limit_bytes=38 << 20),
        name="feed_forward",
    )(here, *wholes, *conv, *ups[:2], *downs[:2], *ups[2:], *downs[2:])


def put_slices(out_refs, rows_at, product, mesh_rows, rows):
    for i in range(mesh_rows):
        for core in range(2):
            for chip in range(4):
                start = ((i * 2 + core) * 4 + chip) * rows
                at = rows_at(i)
                out_refs[core][chip, at : at + rows, :] = product[start : start + rows, :].astype(bf16)


def late_kernel(grad_two_ref, low_ref, mixer_ref, mid_low_ref, near_ref, far_ref, product, *, mesh_rows, rows):
    for kind, pair in enumerate(((mixer_ref, mid_low_ref), (grad_two_ref, low_ref))):
        product[...] = dot(pair[0][...], pair[1][...], 1, 0)
        put_slices((near_ref, far_ref), lambda i: (2 * i + kind) * rows, product, mesh_rows, rows)


def rest_kernel(
    mixed_ref, value_ref, one_ref, low_ref, filt_ref, near_ref, far_ref, grad_value_ref, grad_one_ref, product,
    *, mesh_rows, rows,
):
    mixed = mixed_ref[...].astype(f32)
    grad_value_ref[...] = (mixed * one_ref[...]).astype(bf16)
    grad_one_ref[...] = (mixed * value_ref[...]).astype(bf16)
    for kind, grad_ref in enumerate((grad_value_ref, grad_one_ref)):
        product[...] = dot(grad_ref[...], low_ref[...], 1, 0)
        put_slices((near_ref, far_ref), lambda i: (2 * i + kind) * rows, product, mesh_rows, rows)
    base = 2 * mesh_rows * rows
    for part in range(filt_ref.shape[0]):
        for core, ref in enumerate((near_ref, far_ref)):
            for chip in range(4):
                start = (core * 4 + chip) * rows
                at = base + part * rows
                ref[chip, at : at + rows, :] = filt_ref[part, start : start + rows, :].astype(bf16)


def first_norm_kernel(level_ref, *refs, mesh_rows, rows):
    grads, groups = refs[:3], (refs[3:11], refs[11:19])
    x_ref, gain_ref, mid_ref, tokens_ref, gain_grad_ref, gathered, acc = refs[19:]
    split = groups[0][0].shape[0]
    for slot in range(8):
        for i in range(mesh_rows):
            start = slot * rows
            for k, grad_ref in enumerate(grads):
                at = (i * 4 + k) * rows
                gathered[at : at + rows, :] = grad_ref[i ^ level_ref[0], start : start + rows, :]
            at = (i * 4 + 3) * rows
            gathered[at : at + rows, :] = jnp.zeros((rows, gathered.shape[1]), bf16)
        term = tn(gathered[:split], groups[0][slot][...]) + tn(gathered[split:], groups[1][slot][...])
        acc[...] = term if slot == 0 else acc[...] + term
    unit, inverse = norm(x_ref[...].astype(f32))
    grad, gain_grad = norm_back(unit, inverse, gain_ref[...], acc[...])
    tokens_ref[...] = mid_ref[...] + grad
    gain_grad_ref[...] = gain_grad[None]


def add_low(*terms):
    return sum(term.astype(f32) for term in terms).astype(bf16)


def kept_kernel(
    up_ref, down_ref, far_in, late_ref, late_in, up_keep, up_send, down_keep, down_send, *, mesh_rows, hidden, rows
):
    for chip in range(4):
        for i in range(mesh_rows):
            at = slice((chip * mesh_rows + i) * hidden, (chip * mesh_rows + i + 1) * hidden)
            late = [slice((2 * i + kind) * rows, (2 * i + kind + 1) * rows) for kind in range(2)]
            out_ref, side = (up_send if chip & 1 else up_keep), chip >> 1
            out_ref[side, i, :hidden] = add_low(up_ref[at, :], far_in[0, at, :])
            out_ref[side, i, hidden:] = add_low(late_ref[chip, late[0], :], late_in[chip, late[0], :])
            out_ref, side = (down_send if chip >> 1 else down_keep), chip & 1
            out_ref[side, i, :hidden] = add_low(down_ref[at, :], far_in[1, at, :])
            out_ref[side, i, hidden:] = add_low(late_ref[chip, late[1], :], late_in[chip, late[1], :])


def pair_kernel(up_ref, up_in, down_ref, down_in, up_keep, up_send, down_keep, down_send):
    up_keep[...] = add_low(up_ref[0], up_in[0])
    up_send[...] = add_low(up_ref[1], up_in[1])
    down_keep[...] = add_low(down_ref[0], down_in[0])
    down_send[...] = add_low(down_ref[1], down_in[1])


def bulk_kernel(up_ref, up_in, down_ref, down_in, bulk_ref):
    mesh_rows, size = up_ref.shape[:2]
    for i in range(mesh_rows):
        bulk_ref[i, :size] = add_low(up_ref[i], up_in[i])
        bulk_ref[i, size:] = add_low(down_ref[i], down_in[i])


def split_kernel(near_ref, far_ref, *outs):
    for chip, out_ref in enumerate(outs):
        out_ref[...] = add_low(near_ref[chip], far_ref[chip])


def split_gain(gain):
    high = gain.astype(bf16)
    return high, (gain - high.astype(f32)).astype(bf16)


def rest_sum_kernel(
    here_ref, level_ref, p0, p1, p2, p3, kernel_ref, pad_ref, gain_one_ref, gain_two_ref, filt_ref, *sends, rows
):
    mesh_rows = len(sends)
    size, width = sends[0].shape
    size = size - 8
    pairs = [split_gain(ref[...]) for ref in (gain_one_ref, gain_two_ref)]
    gains = jnp.concatenate([pair[part].astype(f32) for part in range(2) for pair in pairs], axis=0)
    gains = jnp.concatenate([gains, jnp.zeros_like(gains)], axis=0).astype(bf16)
    for i, ref in enumerate(sends):
        at = pl.ds(pl.multiple_of((i ^ level_ref[0]) * size, 16), size)
        ref[:size] = add_low(*(part[at, :] for part in (p0, p1, p2, p3)))
        ref[size:] = gains
    taps = kernel_ref.shape[1]
    base = mesh_rows * size
    parts = filt_ref.shape[0] // rows
    grad = [
        sum(ref[base + part * rows : base + (part + 1) * rows, :].astype(f32) for ref in (p0, p1, p2, p3))
        for part in range(parts)
    ]
    grad = jnp.concatenate(grad, axis=1)[:, :taps]
    at = pl.ds(pl.multiple_of(here_ref[0] * rows, rows), rows)
    spot = lax.broadcasted_iota(jnp.int32, (rows, taps), 1)
    grad = jnp.where(spot < taps - pad_ref[at, :], grad, 0.0)
    before = jnp.where(spot == 0, 0.0, pltpu.roll(grad, 1, 1))
    behind = jnp.where(spot == taps - 1, 0.0, pltpu.roll(grad, taps - 1, 1))
    grad = jnp.where(jnp.abs(kernel_ref[at, :]) > thresh, (before + grad + behind) / 3.0, 0.0)
    for part in range(parts):
        size = min(width, taps - part * width)
        piece = grad[:, part * width : part * width + size].astype(bf16)
        filt_ref[part * rows : (part + 1) * rows, :size] = piece
        if size < width:
            filt_ref[part * rows : (part + 1) * rows, size:] = jnp.zeros((rows, width - size), bf16)


def mesh_sum_kernel(x_ref, out_ref):
    out_ref[...] = add_low(*(x_ref[i] for i in range(x_ref.shape[0])))


def tree_sum(terms):
    while len(terms) > 1:
        terms = [a + b for a, b in zip(terms[0::2], terms[1::2])]
    return terms[0]


def rest_mesh_sum_kernel(bulk_ref, filt_ref, *refs):
    sent, out_ref = refs[:-1], refs[-1]
    base = bulk_ref.shape[1]
    size = sent[0].shape[0] - 8
    filt = filt_ref.shape[0]
    mesh_sum_kernel(bulk_ref, out_ref.at[:base])
    out_ref[base : base + size] = add_low(*(ref[:size] for ref in sent))
    out_ref[base + size : base + size + filt] = filt_ref[...]
    gains = [ref[size:].astype(f32) for ref in sent]
    gains = tree_sum([gain[:2] + gain[2:4] for gain in gains])
    high, low = split_gain(gains)
    zeros = jnp.zeros((4, gains.shape[1]), f32)
    out_ref[base + size + filt :] = jnp.concatenate(
        [high.astype(f32), low.astype(f32), zeros], axis=0
    ).astype(bf16)


def slice_at(here, slot, rows):
    start = (here ^ (2 * (slot % 4) + slot // 4)) * rows
    return pl.ds(pl.multiple_of(start, 8), rows)


def unpack_kernel(here_ref, *refs, hidden, rows):
    pieces, outs, gains_ref = refs[:8], refs[8:13], refs[13]
    held, (turned, gains, sems) = refs[14:19], refs[19:]
    up, down, out, given, kernel = held
    copies = [pltpu.make_async_copy(source, to, sems.at[k]) for k, (source, to) in enumerate(zip(held, outs))]
    here = here_ref[0]
    width = given.shape[2]
    taps = kernel.shape[1]
    parts = -(-taps // width)
    for slot, ref in enumerate(pieces):
        turned[slice_at(here, slot, hidden), :] = ref[:hidden].astype(f32)
    up[...] = turned[...].T
    copies[0].start()
    for slot, ref in enumerate(pieces):
        start = hidden + rows
        down[slice_at(here, slot, hidden), :] = ref[start : start + hidden].astype(f32)
    copies[1].start()
    start = 2 * hidden + rows
    for slot, ref in enumerate(pieces):
        at = slice_at(here, slot, rows)
        out[at, :] = ref[hidden : hidden + rows].astype(f32)
        for place, gate in enumerate((2, 0, 1)):
            given[gate, at, :] = ref[start + place * rows : start + (place + 1) * rows].astype(f32)
    copies[2].start()
    copies[3].start()
    for slot, ref in enumerate(pieces):
        at = slice_at(here, slot, rows)
        for part in range(parts):
            size = min(width, taps - part * width)
            block = ref[start + (3 + part) * rows : start + (4 + part) * rows].astype(f32)
            kernel[at, part * width : part * width + size] = block[:, :size]
        gain = ref[start + (3 + parts) * rows :].astype(f32)
        gains[relative_index(here, slot, 8)] = gain[:2] + gain[2:4]
    copies[4].start()
    gains_ref[...] = sum(gains[slot] for slot in range(8))
    for copy in copies:
        copy.wait()


def chips_of(x, done=()):
    return [x] + [swap(x, "dp", 2 * chip, done) for chip in range(1, 4)]


def far(x):
    return pltpu.with_memory_space_constraint(x, pltpu.HBM)


def levels_of(pieces):
    return [pieces[0]] + [swap(pieces[i], "mp", i) for i in range(1, len(pieces))]


def stacked(*parts):
    shape = (len(parts),) + parts[0].shape
    (out,) = whole_call(stack_kernel, [(shape, bf16)], name="mixer_group", count=len(parts))(*parts)
    return out.reshape(-1, shape[-1])


def pair_of(pieces, done=()):
    return pieces + [swap(piece, "dp", 1, done) for piece in pieces]


def fast_body(
    tables,
    tokens,
    gain_first,
    input_weight,
    kernel,
    pad_len,
    output_weight,
    gain_second,
    up_weight,
    down_weight,
    cotangent,
):
    ways, mesh_rows = lax.axis_size("dp"), lax.axis_size("mp")
    here = lax.axis_index("dp")
    place = here.astype(jnp.int32)[None]
    level = lax.axis_index("mp").astype(jnp.int32)[None]
    x, grad_rows = tokens[0], cotangent[0]
    spots, width = x.shape
    length = spots * mesh_rows
    own_channels, taps = kernel.shape
    rows = own_channels // ways
    hidden = up_weight.shape[1] // ways
    channels = own_channels * mesh_rows
    sizes = dict(mesh_rows=mesh_rows, rows=rows)
    filt_parts = -(-taps // width)

    own_in = lax.dynamic_slice_in_dim(input_weight.transpose(1, 2, 0), here * rows, rows, 1)
    own_out = lax.dynamic_slice_in_dim(output_weight, here * rows, rows, 0)
    own_mixer = jnp.concatenate([own_in, own_out[None]]).reshape(-1, width)
    next_mixer = swap(own_mixer, "mp", 1)
    own_up = lax.dynamic_slice_in_dim(up_weight, here * hidden, hidden, 1).T
    own_down = lax.dynamic_slice_in_dim(down_weight, here * hidden, hidden, 0)
    own_feed = jnp.stack([own_up, own_down])
    own_feed = jnp.broadcast_to(own_feed, (mesh_rows,) + own_feed.shape)
    other_mixers = [swap(after(own_mixer, next_mixer), "mp", i) for i in range(2, mesh_rows)]
    (normed_low,) = whole_call(
        first_norm_forward_kernel, [((spots, width), bf16)], name="first_norm", count=2, room=10
    )(x, gain_first[None])
    first_group = chips_of(stacked(own_mixer, next_mixer))
    other_mixers = [after(part, *first_group[1:], normed_low, tables) for part in other_mixers]
    second_group = chips_of(stacked(*other_mixers))
    feed_rows = turn(after(own_feed, *other_mixers))
    mixer = [[far(piece) for piece in pair_of(group)] for group in (first_group, second_group)]

    outs = project(level, normed_low, mixer, mesh_rows)
    mixed_in, (value, gate_one, gate_two, weight_out) = outs[:mesh_rows], outs[mesh_rows:]
    value, gate_one, gate_two = (part.reshape(channels, spots) for part in (value, gate_one, gate_two))
    weight_out = weight_out.reshape(channels, width)
    received = levels_of([part.reshape(own_channels, spots) for part in mixed_in])
    feed_rows = after(feed_rows, value)
    up, down = (feed_rows[:, side].reshape(-1, width) for side in range(2))
    up_x, down_y = swap(up, "dp", 2), swap(down, "dp", 4)
    fspec = filter_slices(place, after(kernel, gate_two), pad_len, tables, length, ways)
    up_x, down_y = after(up_x, *received[1:], fspec), after(down_y, *received[1:], fspec)
    quarter = ((2, mesh_rows * hidden, width), bf16)
    up_pair, down_pair = whole_call(stack_kernel, [quarter] * 2, name="feed_pairs", count=4, room=8)(
        up, up_x, down, down_y
    )
    up_pair, down_pair = swap(up_pair, "dp", 4), swap(down_pair, "dp", 2)
    received = [received[0]] + [after(piece, fspec) for piece in received[1:]]
    *conv_out, uspec = conv_forward(level, received, fspec, tables)
    conv = levels_of(conv_out)
    ups = [after(up_pair, *conv[1:]), up, up_x]
    downs = [after(down_pair, *conv[1:]), down, down_y]
    ups, downs = (
        [pair, swap(pair, "dp", 1), one, two, swap(one, "dp", 1), swap(two, "dp", 1)]
        for pair, one, two in (ups, downs)
    )

    wide, tall = ((spots, width), f32), ((channels, spots), bf16)
    outs = feed_forward(
        level,
        (far(x), far(gate_two), far(weight_out), gain_second[None], far(grad_rows)),
        conv,
        ups,
        downs,
        channels,
    )
    mixer_low, block_out, grad_mid, mid_low, gain_second_grad, grad_two = outs[:6]
    grad_conv, (up_near, down_near, far_grads) = outs[6 : 6 + mesh_rows], outs[6 + mesh_rows :]
    received = levels_of(grad_conv)
    late_shape = ((4, 2 * mesh_rows * rows, width), bf16)
    late_near, late_far = whole_call(
        partial(late_kernel, **sizes), [late_shape] * 2, [((channels, width), f32)], name="late_grads", count=4
    )(far(grad_two), far(normed_low), mixer_low, mid_low)
    half = ((2, mesh_rows, hidden + rows, width), bf16)
    up_keep, up_send, down_keep, down_send = whole_call(
        partial(kept_kernel, hidden=hidden, **sizes), [pltpu.HBM(*half), half] * 2, name="kept", count=5, room=20
    )(up_near, down_near, swap(far_grads, "dp", 1), late_near, swap(late_far, "dp", 1))
    up_in, down_in = swap(up_send, "dp", 2), swap(down_send, "dp", 4)

    received = [received[0]] + [after(piece, up_keep) for piece in received[1:]]
    mixed_out, gspec = conv_mixed(level, received, fspec, tables)
    mixed = turn(mixed_out).reshape(channels, spots)
    filt_grad = conv_filt(gspec, uspec, tables, taps, width, length)
    quarter = (half[0][1:], bf16)
    up_keep, up_send, down_keep, down_send = whole_call(
        pair_kernel, [pltpu.HBM(*quarter), quarter] * 2, name="kept_again", count=4, room=12
    )(far(up_keep), after(up_in, mixed_out), far(down_keep), after(down_in, mixed_out))
    up_in, down_in = swap(up_send, "dp", 4), swap(down_send, "dp", 2)
    rest_rows = (2 * mesh_rows + filt_parts) * rows
    rest_near, rest_far, grad_value, grad_one = whole_call(
        partial(rest_kernel, **sizes),
        [pltpu.HBM((4, rest_rows, width), bf16)] * 2 + [pltpu.HBM(*tall)] * 2,
        [((channels, width), f32)],
        name="rest_grads",
        count=5,
        room=12,
    )(mixed, far(value), far(gate_one), far(normed_low), filt_grad)
    rest = whole_call(split_kernel, [((rest_rows, width), bf16)] * 4, name="rest_kept", count=2)(
        far(rest_near), swap(rest_far, "dp", 1)
    )
    (bulk,) = whole_call(
        bulk_kernel, [pltpu.HBM((mesh_rows, 2 * (hidden + rows), width), bf16)], name="bulk_sum", count=4
    )(far(up_keep), after(up_in, rest_near), far(down_keep), after(down_in, rest_near))
    bulk = turn(bulk)
    rest = [rest[0]] + [swap(rest[chip], "dp", 2 * chip) for chip in range(1, 4)]
    grad_tokens, gain_first_grad = whole_call(
        partial(first_norm_kernel, **sizes),
        [wide, ((1, width), f32)],
        [((4 * mesh_rows * rows, spots), bf16), wide],
        name="first_norm_back",
        smem=1,
        count=22,
        room=20,
    )(
        level,
        *(far(part.reshape(mesh_rows, own_channels, spots)) for part in (grad_value, grad_one, grad_two)),
        *mixer[0],
        *mixer[1],
        far(x),
        gain_first[None],
        far(grad_mid),
    )
    rest = [rest[0]] + [after(piece, grad_tokens) for piece in rest[1:]]
    own_filt, *rest = whole_call(
        partial(rest_sum_kernel, rows=rows),
        [((filt_parts * rows, width), bf16)] + [((2 * rows + 8, width), bf16)] * mesh_rows,
        name="rest_sum",
        smem=2,
        count=8,
    )(place, level, *rest, kernel, pad_len[:, None], gain_first_grad, gain_second_grad)
    rest = levels_of(rest)
    (mine,) = whole_call(
        rest_mesh_sum_kernel,
        [((bulk.shape[1] + (2 + filt_parts) * rows + 8, width), bf16)],
        name="mesh_sum",
        count=2 + mesh_rows,
        room=8,
    )(after(bulk, *rest[1:]), own_filt, *rest)
    shapes = [up_weight.shape, down_weight.shape, (own_channels, width), (3, own_channels, width), kernel.shape]
    up_grad, down_grad, out_grad, in_grad, kernel_grad, gains = pl.pallas_call(
        partial(unpack_kernel, hidden=hidden, rows=rows),
        out_shape=[jax.ShapeDtypeStruct(shape, f32) for shape in shapes + [(2, width)]],
        in_specs=[SM] + [VM] * 8,
        out_specs=[pl.BlockSpec(memory_space=pl.ANY)] * 5 + [VM],
        scratch_shapes=[pltpu.VMEM(shape, f32) for shape in shapes + [down_weight.shape, (8, 2, width)]]
        + [pltpu.SemaphoreType.DMA((5,))],
        compiler_params=pltpu.CompilerParams(vmem_limit_bytes=24 << 20),
        name="unpack",
    )(place, *pair_of(chips_of(mine)))
    return (
        block_out[None],
        grad_tokens[None],
        gains[0],
        in_grad.transpose(2, 0, 1),
        kernel_grad,
        out_grad,
        gains[1],
        up_grad,
        down_grad,
    )


def body(tables, *arrays):
    ways = lax.axis_size("dp")
    whole_tiles = arrays[3].shape[0] % (8 * ways) == 0 and arrays[7].shape[1] % (32 * ways) == 0
    assert arrays[0].shape[0] == 1
    return (fast_body if ways == 8 and whole_tiles else plain_body)(tables, *arrays)


def solution(mesh):
    in_specs = (
        P("dp", "mp", None),
        P(),
        P(None, None, "mp"),
        P("mp", None),
        P("mp"),
        P("mp", None),
        P(),
        P(None, "mp"),
        P("mp", None),
        P("dp", "mp", None),
    )
    out_specs = (
        P("dp", "mp", None),
        P("dp", "mp", None),
        P(),
        P(None, None, "mp"),
        P("mp", None),
        P("mp", None),
        P(),
        P(None, "mp"),
        P("mp", None),
    )

    def program(tokens, *rest):
        tables = dft_tables(tokens.shape[1])
        inner = jax.shard_map(
            body, mesh=mesh, in_specs=((P(), P(), P()),) + in_specs, out_specs=out_specs, check_vma=False
        )
        return inner(tables, tokens, *rest)

    return program
```

```python
import math
from functools import partial

import jax
import jax.numpy as jnp
import numpy as np
from jax import lax
from jax.experimental import pallas as pl
from jax.experimental.pallas import tpu as pltpu
from jax.sharding import PartitionSpec as P

LANES = 128
FEED_PACK = 2
ROWS = 16
BASE = 256
f32 = jnp.float32
bf16 = jnp.bfloat16


def dft_tables(length):
    radix = length // BASE
    spot = lax.iota(jnp.int32, BASE)
    angle = (spot[:, None] * spot[None] % BASE).astype(f32) * (2 * math.pi / BASE)
    cos, sin = jnp.cos(angle), jnp.sin(angle)
    matrix = jnp.concatenate(
        [jnp.concatenate([cos, -sin], axis=1), jnp.concatenate([sin, cos], axis=1)], axis=0
    )
    high = matrix.astype(bf16)
    low = (matrix - high.astype(f32)).astype(bf16)
    turn = 2 * np.pi * np.outer(np.arange(radix) + 0.25, np.arange(BASE)) / length
    twiddle = np.stack([np.cos(turn), np.sin(turn)]).astype(np.float32)
    return high, low, jnp.asarray(twiddle)


def times(re, im, angle):
    c, s = math.cos(angle), math.sin(angle)
    if abs(s) < 1e-12:
        return (re, im) if c > 0 else (-re, -im)
    if abs(c) < 1e-12:
        return (-im, re) if s > 0 else (im, -re)
    if abs(abs(c) - abs(s)) < 1e-12:
        a = abs(c)
        sc, ss = (a if c > 0 else -a), (1.0 if (s > 0) == (c > 0) else -1.0)
        if ss > 0:
            return (re - im) * sc, (re + im) * sc
        return (re + im) * sc, (im - re) * sc
    return re * c - im * s, re * s + im * c


def radix_dft(re, im, sign):
    n = len(re)
    if n == 1:
        return re, im
    er, ei = radix_dft(re[0::2], im[0::2], sign)
    odr, odi = radix_dft(re[1::2], im[1::2], sign)
    lo_r, lo_i, hi_r, hi_i = [], [], [], []
    for k in range(n // 2):
        tr, ti = times(odr[k], odi[k], sign * 2 * math.pi * k / n)
        lo_r.append(er[k] + tr)
        lo_i.append(ei[k] + ti)
        hi_r.append(er[k] - tr)
        hi_i.append(ei[k] - ti)
    return lo_r + hi_r, lo_i + hi_i


def split_in(load, twiddle_ref, store, radix, channels):
    def step(tile, carry):
        rows = pl.ds(pl.multiple_of(tile * ROWS, ROWS), ROWS)
        for half in range(BASE // LANES):
            lanes = slice(half * LANES, (half + 1) * LANES)
            re, im = [], []
            for block in range(radix):
                x = load(rows, block, half)
                angle = -2 * math.pi * block * 0.25 / radix
                re.append(x * math.cos(angle))
                im.append(x * math.sin(angle))
            re, im = radix_dft(re, im, -1)
            for k in range(radix):
                c = twiddle_ref[0, k : k + 1, lanes]
                s = twiddle_ref[1, k : k + 1, lanes]
                store(rows, k, half, re[k] * c + im[k] * s, im[k] * c - re[k] * s)
        return carry

    lax.fori_loop(0, channels // ROWS, step, 0)


def split_out(load, twiddle_ref, store, radix, channels, length):
    def step(tile, carry):
        rows = pl.ds(pl.multiple_of(tile * ROWS, ROWS), ROWS)
        for half in range(BASE // LANES):
            lanes = slice(half * LANES, (half + 1) * LANES)
            re, im = [], []
            for k in range(radix):
                vr, vi = load(rows, k, half)
                c = twiddle_ref[0, k : k + 1, lanes]
                s = twiddle_ref[1, k : k + 1, lanes]
                re.append(vr * c - vi * s)
                im.append(vr * s + vi * c)
            re, im = radix_dft(re, im, 1)
            for block in range(radix):
                angle = 2 * math.pi * block * 0.25 / radix
                store(
                    rows,
                    block,
                    half,
                    re[block] * (math.cos(angle) / length) - im[block] * (math.sin(angle) / length),
                )
        return carry

    lax.fori_loop(0, channels // ROWS, step, 0)


def forward_dot(z, matrix):
    return jnp.dot(z, matrix, preferred_element_type=f32)


def inverse_dot(y, matrix):
    return lax.dot_general(y, matrix, (((1,), (1,)), ((), ())), preferred_element_type=f32)


def product_loop(a_load, b_load, store, total_rows, conj):
    def step(tile, carry):
        rows = pl.ds(pl.multiple_of(tile * ROWS, ROWS), ROWS)
        for half in range(BASE // LANES):
            cr = slice(half * LANES, (half + 1) * LANES)
            ci = slice(BASE + half * LANES, BASE + (half + 1) * LANES)
            ar, ai = a_load(rows, cr), a_load(rows, ci)
            br, bi = b_load(rows, cr), b_load(rows, ci)
            if conj:
                store(rows, cr, ar * br + ai * bi)
                store(rows, ci, ai * br - ar * bi)
            else:
                store(rows, cr, ar * br - ai * bi)
                store(rows, ci, ai * br + ar * bi)
        return carry

    lax.fori_loop(0, total_rows // ROWS, step, 0)


def cut(ref, here, rows, block, half):
    width = ref.shape[-1]
    start = block * BASE + half * LANES
    return ref[(start // width) ^ here, rows, start % width : start % width + LANES].astype(f32)


def put(ref, here, rows, block, half, value):
    width = ref.shape[-1]
    start = block * BASE + half * LANES
    ref[(start // width) ^ here, rows, start % width : start % width + LANES] = value.astype(ref.dtype)


def rowshift(rows, k, channels):
    return pl.ds(pl.multiple_of(rows.start + k * channels, ROWS), ROWS)


def into_scratch(ref, channels):
    def store(rows, k, half, re, im):
        at = rowshift(rows, k, channels)
        ref[at, half * LANES : (half + 1) * LANES] = re.astype(ref.dtype)
        ref[at, BASE + half * LANES : BASE + (half + 1) * LANES] = im.astype(ref.dtype)

    return store


def from_scratch(ref, channels):
    def load(rows, k, half):
        at = rowshift(rows, k, channels)
        return (
            ref[at, half * LANES : (half + 1) * LANES].astype(f32),
            ref[at, BASE + half * LANES : BASE + (half + 1) * LANES].astype(f32),
        )

    return load


def filter_kernel(f_ref, high_ref, low_ref, twiddle_ref, spec_ref, zh, zl, *, radix, channels):
    def store(rows, k, half, re, im):
        at = rowshift(rows, k, channels)
        for value, base in ((re, 0), (im, BASE)):
            lanes = slice(base + half * LANES, base + (half + 1) * LANES)
            top = value.astype(bf16)
            zh[at, lanes] = top
            zl[at, lanes] = (value - top.astype(f32)).astype(bf16)

    split_in(partial(cut, f_ref, 0), twiddle_ref, store, radix, channels)
    spec_ref[...] = (
        forward_dot(zh[...], high_ref[...])
        + forward_dot(zl[...], high_ref[...])
        + forward_dot(zh[...], low_ref[...])
    )


def tile_load(ref):
    return lambda rows, lanes: ref[rows, lanes].astype(f32)


def tile_store(ref):
    def store(rows, lanes, value):
        ref[rows, lanes] = value.astype(ref.dtype)

    return store


def conv_kernel(here_ref, *refs, parts, radix, channels, length):
    sent, (fspec_ref, high_ref, twiddle_ref) = refs[:parts], refs[parts : parts + 3]
    outs, (uspec_ref, z, y, big, turned) = refs[parts + 3 : 2 * parts + 3], refs[2 * parts + 3 :]
    here = here_ref[0]
    for i, ref in enumerate(sent):
        turned[i ^ here] = ref[...]
    split_in(partial(cut, turned, 0), twiddle_ref, into_scratch(z, channels), radix, channels)
    big[...] = forward_dot(z[...], high_ref[...])
    uspec_ref[...] = big[...].astype(uspec_ref.dtype)
    product_loop(tile_load(big), tile_load(fspec_ref), tile_store(y), radix * channels, False)
    big[...] = inverse_dot(y[...], high_ref[...])
    split_out(from_scratch(big, channels), twiddle_ref, partial(put, turned, 0), radix, channels, length)
    for i, ref in enumerate(outs):
        ref[...] = turned[i ^ here]


def conv_mixed_kernel(here_ref, *refs, parts, radix, channels, length):
    sent, (fspec_ref, high_ref, twiddle_ref) = refs[:parts], refs[parts : parts + 3]
    mixed_ref, spec_ref, z, y, big, turned = refs[parts + 3 :]
    here = here_ref[0]
    for i, ref in enumerate(sent):
        turned[i ^ here] = ref[...]
    split_in(partial(cut, turned, 0), twiddle_ref, into_scratch(z, channels), radix, channels)
    big[...] = forward_dot(z[...], high_ref[...])
    spec_ref[...] = big[...].astype(bf16)
    product_loop(tile_load(big), tile_load(fspec_ref), tile_store(y), radix * channels, True)
    big[...] = inverse_dot(y[...], high_ref[...])
    split_out(from_scratch(big, channels), twiddle_ref, partial(put, mixed_ref, 0), radix, channels, length)


def conv_filt_kernel(
    gspec_ref, uspec_ref, high_ref, twiddle_ref, filt_ref, y, big, *, radix, channels, length, taps
):
    product_loop(tile_load(gspec_ref), tile_load(uspec_ref), tile_store(y), radix * channels, True)
    big[...] = inverse_dot(y[...], high_ref[...])
    filt_ref[filt_ref.shape[0] - 1] = jnp.zeros(filt_ref.shape[1:], filt_ref.dtype)

    def store(rows, block, half, value):
        if block * BASE + half * LANES < taps:
            put(filt_ref, 0, rows, block, half, value)

    split_out(from_scratch(big, channels), twiddle_ref, store, radix, channels, length)


VM = pl.BlockSpec(memory_space=pltpu.VMEM)
SM = pl.BlockSpec(memory_space=pltpu.SMEM)


def filter_spectrum(filt, tables):
    high, low, twiddle = tables
    channels, length = filt.shape[1], filt.shape[0] * filt.shape[2]
    radix = length // BASE
    rows = radix * channels
    return pl.pallas_call(
        partial(filter_kernel, radix=radix, channels=channels),
        out_shape=jax.ShapeDtypeStruct((rows, 2 * BASE), f32),
        in_specs=[VM] * 4,
        out_specs=VM,
        scratch_shapes=[pltpu.VMEM((rows, 2 * BASE), bf16)] * 2,
        name="filter_spectrum",
    )(filt, high, low, twiddle)


def conv_forward(here, pieces, fspec, tables):
    high, _, twiddle = tables
    parts = len(pieces)
    channels, width = pieces[0].shape
    length = parts * width
    radix = length // BASE
    rows = radix * channels
    return pl.pallas_call(
        partial(conv_kernel, parts=parts, radix=radix, channels=channels, length=length),
        out_shape=[jax.ShapeDtypeStruct((channels, width), bf16)] * parts + [pltpu.HBM((rows, 2 * BASE), bf16)],
        in_specs=[SM] + [VM] * (parts + 3),
        out_specs=[VM] * (parts + 1),
        scratch_shapes=[pltpu.VMEM((rows, 2 * BASE), bf16)] * 2
        + [pltpu.VMEM((rows, 2 * BASE), f32), pltpu.VMEM((parts, channels, width), bf16)],
        compiler_params=pltpu.CompilerParams(vmem_limit_bytes=16 << 20),
        name="conv_forward",
    )(here, *pieces, fspec, high, twiddle)


def conv_mixed(here, pieces, fspec, tables):
    high, _, twiddle = tables
    parts = len(pieces)
    channels, width = pieces[0].shape
    length = parts * width
    radix = length // BASE
    rows = radix * channels
    return pl.pallas_call(
        partial(conv_mixed_kernel, parts=parts, radix=radix, channels=channels, length=length),
        out_shape=(
            pltpu.HBM((parts, channels, width), bf16),
            pltpu.HBM((rows, 2 * BASE), bf16),
        ),
        in_specs=[SM] + [VM] * (parts + 3),
        out_specs=(VM, VM),
        scratch_shapes=[pltpu.VMEM((rows, 2 * BASE), bf16)] * 2
        + [pltpu.VMEM((rows, 2 * BASE), f32), pltpu.VMEM((parts, channels, width), bf16)],
        compiler_params=pltpu.CompilerParams(vmem_limit_bytes=16 << 20),
        name="conv_mixed",
    )(here, *pieces, fspec, high, twiddle)


def conv_filt(gspec, uspec, tables, taps, width, length):
    high, _, twiddle = tables
    rows = gspec.shape[0]
    radix = length // BASE
    channels = rows // radix
    return pl.pallas_call(
        partial(conv_filt_kernel, radix=radix, channels=channels, length=length, taps=taps),
        out_shape=jax.ShapeDtypeStruct((-(-taps // width), channels, width), f32),
        in_specs=[VM] * 4,
        out_specs=VM,
        scratch_shapes=[pltpu.VMEM((rows, 2 * BASE), bf16), pltpu.VMEM((rows, 2 * BASE), f32)],
        compiler_params=pltpu.CompilerParams(vmem_limit_bytes=16 << 20),
        name="conv_filt",
    )(gspec, uspec, high, twiddle)


thresh = 0.003
epsilon = 1e-05
gelu_scale = math.sqrt(2 / math.pi)
gelu_cube = 0.044715


def norm(values):
    centered = values - jnp.mean(values, axis=-1, keepdims=True)
    inverse = lax.rsqrt(jnp.mean(centered * centered, axis=-1, keepdims=True) + epsilon)
    return centered * inverse, inverse


def norm_back(unit, inverse, gain, grad):
    scaled = grad * gain
    mean = jnp.mean(scaled, axis=-1, keepdims=True)
    along = jnp.mean(scaled * unit, axis=-1, keepdims=True)
    return inverse * (scaled - mean - unit * along), jnp.sum(grad * unit, axis=0)


def shrink_pool(kernel, pad_len):
    shrunk = jax.nn.relu(kernel - thresh) - jax.nn.relu(-kernel - thresh)
    padded = jnp.pad(shrunk, ((0, 0), (1, 1)))
    pooled = (padded[:, :-2] + padded[:, 1:-1] + padded[:, 2:]) / 3.0
    positions = lax.broadcasted_iota(jnp.int32, pooled.shape, 1)
    return jnp.where(positions < (pooled.shape[1] - pad_len)[:, None], pooled, 0.0)


def gelu_both(values):
    cubic = gelu_cube * values * values
    turn = jnp.tanh(gelu_scale * (values + cubic * values))
    half = 0.5 * (1 + turn)
    slope = half + 0.5 * values * (1 - turn * turn) * (gelu_scale * (1 + 3 * cubic))
    return values * half, slope


def dot(a, b, over_a, over_b):
    return lax.dot_general(a, b, (((over_a,), (over_b,)), ((), ())), preferred_element_type=f32)


def after(x, *waits):
    return lax.optimization_barrier((x, waits))[0] if waits else x


def swap(x, axis, bit, done=()):
    return after(lax.ppermute(x, axis, [(i, i ^ bit) for i in range(lax.axis_size(axis))]), *done)


def gather(x, axis, stride=1, done=()):
    return jnp.stack([x] + [swap(x, axis, i, done) for i in range(stride, lax.axis_size(axis), stride)])


def scatter(x, axis, stride=1, done=()):
    terms = [x[0]] + [swap(x[i], axis, i * stride, done) for i in range(1, x.shape[0])]
    return sum(term.astype(f32) for term in terms)


class Gather:
    def __init__(self, x, bits):
        self.x, self.held, self.left = x, [], list(bits)

    def step(self, count=1, done=()):
        for bit in self.left[:count]:
            place = sum(other > bit for other in self.held)
            self.x = jnp.stack([self.x, swap(self.x, "dp", 1 << bit, done)], axis=place)
            self.held.append(bit)
        self.left = self.left[count:]
        return self

    def finish(self, done=()):
        self.step(len(self.left), done)
        return self.x.reshape((-1,) + self.x.shape[len(self.held) :])


def narrow_sum(*terms):
    return sum(term.astype(f32) for term in terms).astype(bf16)


class Reduction:
    def __init__(self, x, bits):
        self.x = x.reshape((2,) * len(bits) + x.shape[1:])
        self.held, self.left = sorted(bits, reverse=True), list(bits)

    def step(self, count=1, done=()):
        for bit in self.left[:count]:
            place = self.held.index(bit)
            self.held.remove(bit)
            keep, send = (lax.index_in_dim(self.x, side, place, keepdims=False) for side in (0, 1))
            self.x = narrow_sum(keep, swap(send, "dp", 1 << bit, done))
        self.left = self.left[count:]
        return self

    def finish(self, done=()):
        return self.step(len(self.left), done).x


def sum_all(x):
    for axis in ("dp", "mp"):
        bit = 1
        while bit < lax.axis_size(axis):
            x = x + swap(x, axis, bit)
            bit *= 2
    return x


def parts_of(x, axis, stride=1):
    return [x] + [swap(x, axis, i) for i in range(stride, lax.axis_size(axis), stride)]


def parts_for(x, axis):
    return [x[0]] + [swap(x[i], axis, i) for i in range(1, x.shape[0])]


def turn(x):
    return lax.all_to_all(x, "mp", 0, 0)


def exchange(x, done=()):
    return jnp.stack([x[0]] + [swap(x[i], "mp", i, done) for i in range(1, x.shape[0])])


def spread(x, *orders):
    x = x.astype(bf16)
    if orders:
        half = x.shape[0] // 16 * 8
        x = [Gather(part, bits).finish() for part, bits in zip((x[:half], x[half:]), orders)]
        x = jnp.concatenate(x, axis=1)
    else:
        x = gather(x, "dp", 2)
    return jnp.concatenate([x, swap(x, "dp", 1)])


class Spread:
    def __init__(self, x, *orders):
        half = x.shape[0] // 16 * 8
        self.parts = [Gather(part, bits) for part, bits in zip((x[:half], x[half:]), orders)]

    @property
    def x(self):
        return [part.x for part in self.parts]

    def step(self, done=()):
        for part in self.parts:
            part.step(done=done)

    def finish(self, done=()):
        x = jnp.concatenate([part.finish(done=done) for part in self.parts], axis=1)
        return jnp.concatenate([x, swap(x, "dp", 1)])


class Doubling:
    def __init__(self, x):
        self.x = x
        self.left = [
            (axis, 1 << bit) for axis in ("dp", "mp") for bit in range(lax.axis_size(axis).bit_length() - 1)
        ]

    def step(self):
        if self.left:
            self.x = self.x + swap(self.x, *self.left.pop(0))

    def finish(self):
        while self.left:
            self.step()


def absolute(x, start, rows):
    here = lax.axis_index("dp")
    count = x.shape[0]
    picks = []
    for index in range(count):
        relative = here ^ index
        at = (relative & 1) * (count // 2) + (relative >> 1)
        picks.append(lax.dynamic_slice(x, (at, start, 0), (1, rows, x.shape[2]))[0])
    return jnp.concatenate(picks).astype(f32)


def plain_body(
    tables,
    tokens,
    gain_first,
    input_weight,
    kernel,
    pad_len,
    output_weight,
    gain_second,
    up_weight,
    down_weight,
    cotangent,
):
    ways, rows_mp = lax.axis_size("dp"), lax.axis_size("mp")
    here_dp, here_mp = lax.axis_index("dp"), lax.axis_index("mp")
    chips = list(range(1, ways.bit_length() - 1))
    first_bits, second_bits = chips, chips[::-1]
    here = here_mp.astype(jnp.int32)[None]
    spots, width = tokens.shape[1:]
    length = spots * rows_mp
    own_channels = kernel.shape[0]
    slice_channels = own_channels // ways
    slice_hidden = up_weight.shape[1] // ways
    channels = own_channels * rows_mp

    own_in = lax.dynamic_slice_in_dim(input_weight, here_dp * slice_channels, slice_channels, 2)
    own_out = lax.dynamic_slice_in_dim(output_weight, here_dp * slice_channels, slice_channels, 0)
    mixer_rows = gather(jnp.concatenate([own_in.transpose(1, 2, 0), own_out[None]]), "mp")
    start_rows = tokens[0].astype(f32)
    unit_one, inverse_one = norm(start_rows)
    normed_low = (unit_one * gain_first).astype(bf16)
    own_up = lax.dynamic_slice_in_dim(up_weight, here_dp * slice_hidden, slice_hidden, 1).T
    own_down = lax.dynamic_slice_in_dim(down_weight, here_dp * slice_hidden, slice_hidden, 0)
    own_feed = jnp.stack([own_up, own_down])

    picks = []
    for core in range(2):
        for chip in range(ways // 2):
            at = (here_dp ^ (2 * chip + core)) * slice_channels
            picks.append(at)
    kernel_rel = jnp.concatenate([lax.dynamic_slice_in_dim(kernel, at, slice_channels, 0) for at in picks])
    pad_rel = jnp.concatenate([lax.dynamic_slice_in_dim(pad_len, at, slice_channels, 0) for at in picks])
    filt = shrink_pool(kernel_rel, pad_rel)
    fspec = filter_spectrum(jnp.pad(filt, ((0, 0), (0, length - filt.shape[1])))[None], tables)

    feed_rows = gather(after(own_feed, mixer_rows), "mp")
    mixer_rows = gather(after(mixer_rows, fspec, normed_low, own_feed), "dp", 2)
    feeds = [
        Gather(after(feed_rows[:, side], mixer_rows), bits).step()
        for side, bits in ((0, first_bits), (1, second_bits))
    ]
    mixer_rows = jnp.stack([mixer_rows, swap(mixer_rows, "dp", 1)])
    mixer_weights = mixer_rows.transpose(3, 2, 0, 1, 4, 5)
    weight_in = mixer_weights[:3].reshape(3 * channels, width)
    weight_out = mixer_weights[3].reshape(channels, width)

    proj = dot(weight_in, normed_low, 1, 1).reshape(3, channels, spots)
    value, gate_one, gate_two = proj[0], proj[1], proj[2]
    mixed_in = (value * gate_one).astype(bf16).reshape(rows_mp, own_channels, spots)
    for feed in feeds:
        feed.x = after(feed.x, mixed_in)
        feed.finish()
    *conv_out, uspec = conv_forward(here, list(exchange(mixed_in)), fspec, tables)
    conv_out = jnp.stack(conv_out)
    feeds = [after(feed.x, conv_out).reshape(-1, width) for feed in feeds]
    conv = exchange(conv_out).reshape(channels, spots).astype(f32)
    mixer_low = (gate_two * conv).astype(bf16)
    residual_one = start_rows + dot(mixer_low, weight_out, 0, 0)

    unit_two, inverse_two = norm(residual_one)
    second_low = (unit_two * gain_second).astype(bf16)
    grad_rows = cotangent[0]
    feeds = [[feed, swap(feed, "dp", 1)] for feed in feeds]
    block_out, grad_norm_two = residual_one, 0.0
    up_grads, down_grads = [], []
    for up, down in zip(*feeds):
        act, slope = gelu_both(dot(second_low, up, 1, 1))
        act_low = act.astype(bf16)
        grad_pre = (dot(grad_rows, down, 1, 1) * slope).astype(bf16)
        block_out = block_out + dot(act_low, down, 1, 0)
        grad_norm_two = grad_norm_two + dot(grad_pre, up, 1, 0)
        up_grads.append(dot(grad_pre, second_low, 0, 0).astype(bf16))
        down_grads.append(dot(act_low, grad_rows, 0, 0).astype(bf16))
    grad_mid_norm, gain_second_grad = norm_back(unit_two, inverse_two, gain_second, grad_norm_two)
    grad_mid = grad_rows.astype(f32) + grad_mid_norm
    mid_low = grad_mid.astype(bf16)

    chips_count = ways // 2

    def hidden_sum(parts, bits):
        kept = narrow_sum(parts[0], swap(parts[1], "dp", 1))
        return Reduction(kept.reshape(chips_count, rows_mp, slice_hidden, width), bits)

    down_sum = hidden_sum(down_grads, second_bits)
    up_sum = hidden_sum(up_grads, first_bits)

    def by_slice(parts):
        parts = [part.astype(bf16).reshape(rows_mp, 2, chips_count, slice_channels, width) for part in parts]
        return jnp.concatenate(parts, axis=3).transpose(1, 2, 0, 3, 4)

    grad_mixer = dot(weight_out, mid_low, 1, 1)
    grad_conv = (grad_mixer * gate_two).astype(bf16).reshape(rows_mp, own_channels, spots)
    grad_conv = exchange(grad_conv)
    grad_gate_two = (grad_mixer * conv).astype(bf16)
    out_grad = dot(mixer_low, mid_low, 1, 0)
    late = by_slice([dot(grad_gate_two, normed_low, 1, 0), out_grad])
    late = narrow_sum(late[0], swap(late[1], "dp", 1))
    grad_conv = after(grad_conv, down_sum.x, up_sum.x, late)
    mixed_out, gspec = conv_mixed(here, list(grad_conv), fspec, tables)
    filt_grad = conv_filt(gspec, uspec, tables, length, length, length)
    mixed_out = jnp.take(mixed_out, lax.iota(jnp.int32, rows_mp) ^ here_mp, axis=0)
    down_sum.step()
    up_sum.step()
    late = scatter(late, "dp", 2).astype(bf16)
    grad_mixed = exchange(mixed_out).reshape(channels, spots).astype(f32)
    grad_mixed = after(grad_mixed, down_sum.x, up_sum.x, late)
    grad_value = (grad_mixed * gate_one).astype(bf16)
    grad_gate_one = (grad_mixed * value).astype(bf16)
    rest = by_slice([dot(grad, normed_low, 1, 0) for grad in (grad_value, grad_gate_one)])
    grad_norm_one = dot(jnp.concatenate([grad_value, grad_gate_one, grad_gate_two]), weight_in, 0, 0)
    grad_start, gain_first_grad = norm_back(unit_one, inverse_one, gain_first, grad_norm_one)
    grad_tokens = grad_mid + grad_start

    taps = kernel.shape[1]
    filt_grad = filt_grad[0, :, :taps].astype(bf16).reshape(2, chips_count, -1, width)
    rest = jnp.concatenate([rest.reshape(2, chips_count, -1, width), filt_grad], axis=2)
    rest = scatter(narrow_sum(rest[0], swap(rest[1], "dp", 1)), "dp", 2)
    split = rest.shape[0] - filt_grad.shape[2]
    own_kernel = lax.dynamic_slice_in_dim(kernel, here_dp * slice_channels, slice_channels, 0)
    own_pad = lax.dynamic_slice_in_dim(pad_len, here_dp * slice_channels, slice_channels, 0)
    _, filter_back = jax.vjp(partial(shrink_pool, pad_len=own_pad), own_kernel)
    (own_filt,) = filter_back(rest[split:].reshape(slice_channels, taps))
    rest = scatter(rest[:split].astype(bf16).reshape(rows_mp, 2 * slice_channels, width), "mp")
    rest = spread(jnp.concatenate([rest, own_filt.reshape(-1, width)]))
    bulk = jnp.concatenate([up_sum.finish(), down_sum.finish(), late], axis=1)
    bulk = spread(scatter(bulk, "mp"))

    up_grad = absolute(bulk, 0, slice_hidden).T
    down_grad = absolute(bulk, slice_hidden, slice_hidden)
    in_grad = [
        absolute(rest, 0, slice_channels),
        absolute(rest, slice_channels, slice_channels),
        absolute(bulk, 2 * slice_hidden, slice_channels),
    ]
    in_full = jnp.stack(in_grad).transpose(2, 0, 1)
    out_full = absolute(bulk, 2 * slice_hidden + slice_channels, slice_channels)
    kernel_grad = absolute(rest, 2 * slice_channels, filt_grad.shape[2]).reshape(own_channels, taps)

    gains = sum_all(jnp.stack([gain_first_grad, gain_second_grad]))
    return (
        block_out.astype(bf16)[None],
        grad_tokens[None],
        gains[0],
        in_full,
        kernel_grad,
        out_full,
        gains[1],
        up_grad,
        down_grad,
    )


def whole_call(kernel, outs, scratch=(), name=None, smem=0, count=0, room=6):
    return pl.pallas_call(
        kernel,
        out_shape=tuple(out if isinstance(out, pl.MemoryRef) else jax.ShapeDtypeStruct(*out) for out in outs),
        in_specs=[SM] * smem + [VM] * count,
        out_specs=tuple(VM for _ in outs),
        scratch_shapes=[pltpu.VMEM(shape, dtype) for shape, dtype in scratch],
        compiler_params=pltpu.CompilerParams(vmem_limit_bytes=room << 20),
        name=name,
    )


def relative_index(here, place, count):
    chip, core = place % (count // 2), place // (count // 2)
    return here ^ (2 * chip + core)


def filter_slices_kernel(
    here_ref, kernel_ref, pad_ref, high_ref, low_ref, twiddle_ref, spec_ref, filt, zh, zl, *, radix, channels, ways
):
    here = here_ref[0]
    rows = channels // ways
    taps = kernel_ref.shape[1]
    filt[...] = jnp.zeros_like(filt)
    spot = lax.broadcasted_iota(jnp.int32, (8, taps), 1)

    def step(tile, carry):
        place = tile // (rows // 8)
        start = relative_index(here, place, ways) * rows + (tile % (rows // 8)) * 8
        at = pl.ds(pl.multiple_of(start, 8), 8)
        raw = kernel_ref[at, :]
        shrunk = jnp.maximum(raw - thresh, 0.0) - jnp.maximum(-raw - thresh, 0.0)
        before = jnp.where(spot == 0, 0.0, pltpu.roll(shrunk, 1, 1))
        behind = jnp.where(spot == taps - 1, 0.0, pltpu.roll(shrunk, taps - 1, 1))
        pooled = (before + shrunk + behind) / 3.0
        filt[0, pl.ds(pl.multiple_of(tile * 8, 8), 8), :taps] = jnp.where(spot < taps - pad_ref[at, :], pooled, 0.0)
        return carry

    lax.fori_loop(0, channels // 8, step, 0)
    filter_kernel(filt, high_ref, low_ref, twiddle_ref, spec_ref, zh, zl, radix=radix, channels=channels)


def filter_slices(here, kernel, pad_len, tables, length, ways):
    high, low, twiddle = tables
    channels = kernel.shape[0]
    radix = length // BASE
    rows = radix * channels
    return whole_call(
        partial(filter_slices_kernel, radix=radix, channels=channels, ways=ways),
        [((rows, 2 * BASE), f32)],
        [((1, channels, length), f32), ((rows, 2 * BASE), bf16), ((rows, 2 * BASE), bf16)],
        name="filter_spectrum",
        smem=1,
        count=5,
        room=14,
    )(here, far(kernel), pad_len[:, None], far(high), far(low), far(twiddle))[0]


def nt(a, b):
    return dot(a, b, 1, 1)


def tn(a, b):
    return dot(a, b, 0, 0)


def first_norm_forward_kernel(x_ref, gain_ref, low_ref):
    unit, _ = norm(x_ref[...].astype(f32))
    low_ref[...] = (unit * gain_ref[...]).astype(bf16)


def project_kernel(level_ref, low_ref, *refs, rows, mesh_rows):
    groups, sends = (refs[:8], refs[8:16]), refs[16 : 16 + mesh_rows]
    v_ref, one_ref, two_ref, out_ref, weights, sems = refs[16 + mesh_rows :]
    step = pl.program_id(0)

    def weight_copy(group, source, slot):
        size = source.shape[0]
        start = group * groups[0][0].shape[0]
        return pltpu.make_async_copy(source, weights.at[slot, pl.ds(start, size), :], sems.at[group, slot])

    @pl.when(step == 0)
    def _():
        for chip in range(4):
            for core in range(2):
                for group, pieces in enumerate(groups):
                    weight_copy(group, pieces[core * 4 + chip], 2 * chip + core).start()

    for core in range(2):
        for group, pieces in enumerate(groups):
            weight_copy(group, pieces[0], 2 * step + core).wait()
    size = weights.shape[1]
    proj = nt(weights[pl.ds(2 * step, 2)].reshape(2 * size, weights.shape[2]), low_ref[...])
    for core in range(2):
        for i, send_ref in enumerate(sends):
            to = i ^ level_ref[0]
            at = 4 * i * rows
            start = core * size + at
            value, one, two = (proj[start + k * rows : start + (k + 1) * rows] for k in range(3))
            send_ref[core, 0] = (value * one).astype(bf16)
            v_ref[to, core, 0] = value
            one_ref[to, core, 0] = one
            two_ref[to, core, 0] = two
            out_ref[to, core, 0] = weights[2 * step + core, at + 3 * rows : at + 4 * rows, :]


def project(level, low, groups, mesh_rows):
    spots, width = low.shape
    size = sum(group[0].shape[0] for group in groups)
    rows = size // (4 * mesh_rows)
    block = lambda last: pl.BlockSpec((mesh_rows, 2, 1, rows, last), lambda j: (0, 0, j, 0, 0))
    shape = lambda last, dtype: pltpu.HBM((mesh_rows, 2, 4, rows, last), dtype)
    return pl.pallas_call(
        partial(project_kernel, rows=rows, mesh_rows=mesh_rows),
        grid=(4,),
        in_specs=[SM, VM] + [pl.BlockSpec(memory_space=pl.ANY)] * 16,
        out_specs=[pl.BlockSpec((2, 1, rows, spots), lambda j: (0, j, 0, 0))] * mesh_rows
        + [block(spots)] * 3
        + [block(width)],
        out_shape=[pltpu.HBM((2, 4, rows, spots), bf16)] * mesh_rows
        + [shape(spots, f32)] * 3
        + [shape(width, bf16)],
        scratch_shapes=[pltpu.VMEM((8, size, width), bf16), pltpu.SemaphoreType.DMA((2, 8))],
        compiler_params=pltpu.CompilerParams(vmem_limit_bytes=18 << 20),
        name="project",
    )(level, low, *groups[0], *groups[1])


def stack_kernel(*refs):
    for index, out_ref in enumerate(refs[len(refs) // 3 * 2 :]):
        out_ref[0] = refs[2 * index][...]
        out_ref[1] = refs[2 * index + 1][...]


def feed_kernel(*refs, mesh_rows):
    here_ref, x_ref, two_ref, out_weight_ref, gain_ref, grad_ref = refs[:6]
    sent, refs = refs[6 : 6 + mesh_rows], refs[6 + mesh_rows :]
    ups, downs, up_firsts, down_firsts = refs[:2], refs[2:4], refs[4:8], refs[8:12]
    mixer_ref, block_ref, mid_ref, mid_low_ref, gain_grad_ref, grad_two_ref = refs[12:18]
    sends, refs = refs[18 : 18 + mesh_rows], refs[18 + mesh_rows :]
    up_near, down_near, far_grads = refs[:3]
    residual, second, out_acc, norm_acc, conv, turned, weights, grads, sems, grad_sems = refs[3:]
    step = pl.program_id(0)
    size = weights.shape[2]
    pack = grads.shape[2] // size
    copies = []
    for side, (firsts, pairs) in enumerate(((up_firsts, ups), (down_firsts, downs))):
        for k in range(8):
            core, chip = divmod(k, 4)
            first = (0, 1) if side == 0 else (0, 2)
            if chip in first:
                source = firsts[2 * core + first.index(chip)]
            else:
                source = pairs[core].at[0 if chip == (2 if side == 0 else 1) else 1]
            copies.append(pltpu.make_async_copy(source, weights.at[side, k], sems.at[side, k]))

    @pl.when(step == 0)
    def _():
        for copy in copies:
            copy.start()
        for i, ref in enumerate(sent):
            conv[i ^ here_ref[0]] = ref[...]
        mixer_ref[...] = (two_ref[...] * conv[...].reshape(two_ref.shape).astype(f32)).astype(bf16)
        residual[...] = x_ref[...].astype(f32) + tn(mixer_ref[...], out_weight_ref[...])
        unit, _ = norm(residual[...])
        second[...] = (unit * gain_ref[...]).astype(bf16)
        out_acc[...] = residual[...]
        norm_acc[...] = jnp.zeros_like(norm_acc)

    for side in range(2):
        for k in range(pack):
            at = step * pack + k
            pltpu.make_async_copy(up_firsts[0], weights.at[side, at], sems.at[side, at]).wait()
    slot = step % 2

    @pl.when(step >= 2)
    def _():
        for side in range(2):
            pltpu.make_async_copy(
                grads.at[side, slot], up_near.at[pl.ds(0, pack * size), :], grad_sems.at[side, slot]
            ).wait()

    width = second.shape[1]
    up, down = (weights[side, pl.ds(step * pack, pack)].reshape(pack * size, width) for side in range(2))
    act, slope = gelu_both(nt(second[...], up))
    act_low = act.astype(bf16)
    grad_pre = (nt(grad_ref[...], down) * slope).astype(bf16)
    out_acc[...] += dot(act_low, down, 1, 0)
    norm_acc[...] += dot(grad_pre, up, 1, 0)
    grads[0, slot] = tn(grad_pre, second[...]).astype(bf16)
    grads[1, slot] = tn(act_low, grad_ref[...]).astype(bf16)
    steps = 4 // pack
    at = pl.ds(pl.multiple_of((step % steps) * pack * size, size), pack * size)
    for core, outs in enumerate(((up_near, down_near), (far_grads.at[0], far_grads.at[1]))):

        @pl.when(step // steps == core)
        def _():
            for side in range(2):
                pltpu.make_async_copy(
                    grads.at[side, slot], outs[side].at[at, :], grad_sems.at[side, slot]
                ).start()

    @pl.when(step == pl.num_programs(0) - 1)
    def _():
        unit, inverse = norm(residual[...])
        grad, gain_grad = norm_back(unit, inverse, gain_ref[...], norm_acc[...])
        gain_grad_ref[...] = gain_grad[None]
        mid = grad_ref[...].astype(f32) + grad
        mid_ref[...] = mid
        mid_low_ref[...] = mid.astype(bf16)
        block_ref[...] = out_acc[...].astype(bf16)
        grad_mixer = nt(out_weight_ref[...], mid_low_ref[...])
        flat = conv[...].reshape(two_ref.shape)
        grad_two_ref[...] = (grad_mixer * flat.astype(f32)).astype(bf16)
        turned[...] = (grad_mixer * two_ref[...]).astype(bf16).reshape(turned.shape)
        for i, ref in enumerate(sends):
            ref[...] = turned[i ^ here_ref[0]]
        for side in range(2):
            for last in range(2):
                pltpu.make_async_copy(
                    grads.at[side, last], up_near.at[pl.ds(0, pack * size), :], grad_sems.at[side, last]
                ).wait()


def feed_forward(here, wholes, conv, ups, downs, channels):
    mesh_rows = len(conv)
    size, width = ups[2].shape
    spots = wholes[0].shape[0]
    shape = jax.ShapeDtypeStruct
    tall = shape((channels, spots), bf16)
    piece = shape((channels // mesh_rows, spots), bf16)
    anywhere = pl.BlockSpec(memory_space=pl.ANY)
    return pl.pallas_call(
        partial(feed_kernel, mesh_rows=mesh_rows),
        grid=(8 // FEED_PACK,),
        in_specs=[SM] + [VM] * (len(wholes) + mesh_rows) + [anywhere] * 12,
        out_specs=[VM] * (6 + mesh_rows) + [anywhere] * 3,
        out_shape=[
            tall,
            pltpu.HBM((spots, width), bf16),
            pltpu.HBM((spots, width), f32),
            shape((spots, width), bf16),
            shape((1, width), f32),
            pltpu.HBM((channels, spots), bf16),
        ]
        + [piece] * mesh_rows
        + [shape((4 * size, width), bf16)] * 2
        + [shape((2, 4 * size, width), bf16)],
        scratch_shapes=[
            pltpu.VMEM((spots, width), f32),
            pltpu.VMEM((spots, width), bf16),
            pltpu.VMEM((spots, width), f32),
            pltpu.VMEM((spots, width), f32),
            pltpu.VMEM((mesh_rows, channels // mesh_rows, spots), bf16),
            pltpu.VMEM((mesh_rows, channels // mesh_rows, spots), bf16),
            pltpu.VMEM((2, 8, size, width), bf16),
            pltpu.VMEM((2, 2, FEED_PACK * size, width), bf16),
            pltpu.SemaphoreType.DMA((2, 8)),
            pltpu.SemaphoreType.DMA((2, 2)),
        ],
        compiler_params=pltpu.CompilerParams(vmem_limit_bytes=38 << 20),
        name="feed_forward",
    )(here, *wholes, *conv, *ups[:2], *downs[:2], *ups[2:], *downs[2:])


def put_slices(out_refs, rows_at, product, mesh_rows, rows):
    for i in range(mesh_rows):
        for core in range(2):
            for chip in range(4):
                start = ((i * 2 + core) * 4 + chip) * rows
                at = rows_at(i)
                out_refs[core][chip, at : at + rows, :] = product[start : start + rows, :].astype(bf16)


def late_kernel(grad_two_ref, low_ref, mixer_ref, mid_low_ref, near_ref, far_ref, product, *, mesh_rows, rows):
    for kind, pair in enumerate(((mixer_ref, mid_low_ref), (grad_two_ref, low_ref))):
        product[...] = dot(pair[0][...], pair[1][...], 1, 0)
        put_slices((near_ref, far_ref), lambda i: (2 * i + kind) * rows, product, mesh_rows, rows)


def rest_kernel(
    mixed_ref, value_ref, one_ref, low_ref, filt_ref, near_ref, far_ref, grad_value_ref, grad_one_ref, product,
    *, mesh_rows, rows,
):
    mixed = mixed_ref[...].astype(f32)
    grad_value_ref[...] = (mixed * one_ref[...]).astype(bf16)
    grad_one_ref[...] = (mixed * value_ref[...]).astype(bf16)
    for kind, grad_ref in enumerate((grad_value_ref, grad_one_ref)):
        product[...] = dot(grad_ref[...], low_ref[...], 1, 0)
        put_slices((near_ref, far_ref), lambda i: (2 * i + kind) * rows, product, mesh_rows, rows)
    base = 2 * mesh_rows * rows
    for part in range(filt_ref.shape[0]):
        for core, ref in enumerate((near_ref, far_ref)):
            for chip in range(4):
                start = (core * 4 + chip) * rows
                at = base + part * rows
                ref[chip, at : at + rows, :] = filt_ref[part, start : start + rows, :].astype(bf16)


def first_norm_kernel(level_ref, *refs, mesh_rows, rows):
    grads, groups = refs[:3], (refs[3:11], refs[11:19])
    x_ref, gain_ref, mid_ref, tokens_ref, gain_grad_ref, gathered, acc = refs[19:]
    split = groups[0][0].shape[0]
    for slot in range(8):
        for i in range(mesh_rows):
            start = slot * rows
            for k, grad_ref in enumerate(grads):
                at = (i * 4 + k) * rows
                gathered[at : at + rows, :] = grad_ref[i ^ level_ref[0], start : start + rows, :]
            at = (i * 4 + 3) * rows
            gathered[at : at + rows, :] = jnp.zeros((rows, gathered.shape[1]), bf16)
        term = tn(gathered[:split], groups[0][slot][...]) + tn(gathered[split:], groups[1][slot][...])
        acc[...] = term if slot == 0 else acc[...] + term
    unit, inverse = norm(x_ref[...].astype(f32))
    grad, gain_grad = norm_back(unit, inverse, gain_ref[...], acc[...])
    tokens_ref[...] = mid_ref[...] + grad
    gain_grad_ref[...] = gain_grad[None]


def add_low(*terms):
    return sum(term.astype(f32) for term in terms).astype(bf16)


def kept_kernel(
    up_ref, down_ref, far_in, late_ref, late_in, up_keep, up_send, down_keep, down_send, *, mesh_rows, hidden, rows
):
    for chip in range(4):
        for i in range(mesh_rows):
            at = slice((chip * mesh_rows + i) * hidden, (chip * mesh_rows + i + 1) * hidden)
            late = [slice((2 * i + kind) * rows, (2 * i + kind + 1) * rows) for kind in range(2)]
            out_ref, side = (up_send if chip & 1 else up_keep), chip >> 1
            out_ref[side, i, :hidden] = add_low(up_ref[at, :], far_in[0, at, :])
            out_ref[side, i, hidden:] = add_low(late_ref[chip, late[0], :], late_in[chip, late[0], :])
            out_ref, side = (down_send if chip >> 1 else down_keep), chip & 1
            out_ref[side, i, :hidden] = add_low(down_ref[at, :], far_in[1, at, :])
            out_ref[side, i, hidden:] = add_low(late_ref[chip, late[1], :], late_in[chip, late[1], :])


def window_call(kernel, windows, outs, name, room):
    def spec(x, lead):
        shape = (None,) * len(lead) + x.shape[len(lead) :]
        return pl.BlockSpec(shape, lambda n: tuple(lead) + (0,) * (len(x.shape) - len(lead)))

    return pl.pallas_call(
        kernel,
        grid=(1,),
        in_specs=[spec(x, lead) for x, lead in windows],
        out_specs=[VM] * len(outs),
        out_shape=list(outs),
        compiler_params=pltpu.CompilerParams(vmem_limit_bytes=room << 20),
        name=name,
    )(*(x for x, _ in windows))


def second_send_kernel(up_ref, up_in, down_ref, down_in, up_send, down_send):
    up_send[...] = add_low(up_ref[...], up_in[...])
    down_send[...] = add_low(down_ref[...], down_in[...])


def bulk_kernel(up_ref, up_in, up_last, down_ref, down_in, down_last, bulk_ref):
    mesh_rows, size = up_ref.shape[:2]
    for i in range(mesh_rows):
        bulk_ref[i, :size] = add_low(up_ref[i], up_in[i], up_last[i])
        bulk_ref[i, size:] = add_low(down_ref[i], down_in[i], down_last[i])


def split_kernel(near_ref, far_ref, *outs):
    for chip, out_ref in enumerate(outs):
        out_ref[...] = add_low(near_ref[chip], far_ref[chip])


def split_gain(gain):
    high = gain.astype(bf16)
    return high, (gain - high.astype(f32)).astype(bf16)


def rest_sum_kernel(
    here_ref, level_ref, p0, p1, p2, p3, kernel_ref, pad_ref, gain_one_ref, gain_two_ref, filt_ref, *sends, rows
):
    mesh_rows = len(sends)
    size, width = sends[0].shape
    size = size - 8
    pairs = [split_gain(ref[...]) for ref in (gain_one_ref, gain_two_ref)]
    gains = jnp.concatenate([pair[part].astype(f32) for part in range(2) for pair in pairs], axis=0)
    gains = jnp.concatenate([gains, jnp.zeros_like(gains)], axis=0).astype(bf16)
    for i, ref in enumerate(sends):
        at = pl.ds(pl.multiple_of((i ^ level_ref[0]) * size, 16), size)
        ref[:size] = add_low(*(part[at, :] for part in (p0, p1, p2, p3)))
        ref[size:] = gains
    taps = kernel_ref.shape[1]
    base = mesh_rows * size
    parts = filt_ref.shape[0] // rows
    grad = [
        sum(ref[base + part * rows : base + (part + 1) * rows, :].astype(f32) for ref in (p0, p1, p2, p3))
        for part in range(parts)
    ]
    grad = jnp.concatenate(grad, axis=1)[:, :taps]
    at = pl.ds(pl.multiple_of(here_ref[0] * rows, rows), rows)
    spot = lax.broadcasted_iota(jnp.int32, (rows, taps), 1)
    grad = jnp.where(spot < taps - pad_ref[at, :], grad, 0.0)
    before = jnp.where(spot == 0, 0.0, pltpu.roll(grad, 1, 1))
    behind = jnp.where(spot == taps - 1, 0.0, pltpu.roll(grad, taps - 1, 1))
    grad = jnp.where(jnp.abs(kernel_ref[at, :]) > thresh, (before + grad + behind) / 3.0, 0.0)
    for part in range(parts):
        size = min(width, taps - part * width)
        piece = grad[:, part * width : part * width + size].astype(bf16)
        filt_ref[part * rows : (part + 1) * rows, :size] = piece
        if size < width:
            filt_ref[part * rows : (part + 1) * rows, size:] = jnp.zeros((rows, width - size), bf16)


def mesh_sum_kernel(x_ref, out_ref):
    out_ref[...] = add_low(*(x_ref[i] for i in range(x_ref.shape[0])))


def tree_sum(terms):
    while len(terms) > 1:
        terms = [a + b for a, b in zip(terms[0::2], terms[1::2])]
    return terms[0]


def rest_mesh_sum_kernel(bulk_ref, filt_ref, *refs):
    sent, out_ref = refs[:-1], refs[-1]
    base = bulk_ref.shape[1]
    size = sent[0].shape[0] - 8
    filt = filt_ref.shape[0]
    mesh_sum_kernel(bulk_ref, out_ref.at[:base])
    out_ref[base : base + size] = add_low(*(ref[:size] for ref in sent))
    out_ref[base + size : base + size + filt] = filt_ref[...]
    gains = [ref[size:].astype(f32) for ref in sent]
    gains = tree_sum([gain[:2] + gain[2:4] for gain in gains])
    high, low = split_gain(gains)
    zeros = jnp.zeros((4, gains.shape[1]), f32)
    out_ref[base + size + filt :] = jnp.concatenate(
        [high.astype(f32), low.astype(f32), zeros], axis=0
    ).astype(bf16)


def slice_at(here, slot, rows):
    start = (here ^ (2 * (slot % 4) + slot // 4)) * rows
    return pl.ds(pl.multiple_of(start, 8), rows)


def unpack_kernel(here_ref, *refs, hidden, rows):
    pieces, outs, gain_refs = refs[:8], refs[8:13], refs[13:15]
    held, (turned, gains, sems) = refs[15:20], refs[20:]
    up, down, out, given, kernel = held
    copies = [pltpu.make_async_copy(source, to, sems.at[k]) for k, (source, to) in enumerate(zip(held, outs))]
    here = here_ref[0]
    width = given.shape[2]
    taps = kernel.shape[1]
    parts = -(-taps // width)
    for slot, ref in enumerate(pieces):
        start = hidden + rows
        down[slice_at(here, slot, hidden), :] = ref[start : start + hidden].astype(f32)
    copies[1].start()
    start = 2 * hidden + rows
    for slot, ref in enumerate(pieces):
        at = slice_at(here, slot, rows)
        out[at, :] = ref[hidden : hidden + rows].astype(f32)
        for place, gate in enumerate((2, 0, 1)):
            given[gate, at, :] = ref[start + place * rows : start + (place + 1) * rows].astype(f32)
    copies[2].start()
    copies[3].start()
    for slot, ref in enumerate(pieces):
        at = slice_at(here, slot, rows)
        for part in range(parts):
            size = min(width, taps - part * width)
            block = ref[start + (3 + part) * rows : start + (4 + part) * rows].astype(f32)
            kernel[at, part * width : part * width + size] = block[:, :size]
        gain = ref[start + (3 + parts) * rows :].astype(f32)
        gains[relative_index(here, slot, 8)] = gain[:2] + gain[2:4]
    copies[4].start()
    total = sum(gains[slot] for slot in range(8))
    for row, ref in enumerate(gain_refs):
        ref[...] = total[row]
    for slot, ref in enumerate(pieces):
        turned[slice_at(here, slot, hidden), :] = ref[:hidden].astype(f32)
    up[...] = turned[...].T
    copies[0].start()
    for copy in copies:
        copy.wait()


def chips_of(x, done=()):
    return [x] + [swap(x, "dp", 2 * chip, done) for chip in range(1, 4)]


def far(x):
    return pltpu.with_memory_space_constraint(x, pltpu.HBM)


def levels_of(pieces):
    return [pieces[0]] + [swap(pieces[i], "mp", i) for i in range(1, len(pieces))]


def stacked(*parts):
    shape = (len(parts),) + parts[0].shape
    (out,) = whole_call(stack_kernel, [(shape, bf16)], name="mixer_group", count=len(parts))(*parts)
    return out.reshape(-1, shape[-1])


def pair_of(pieces, done=()):
    return pieces + [swap(piece, "dp", 1, done) for piece in pieces]


def fast_body(
    tables,
    tokens,
    gain_first,
    input_weight,
    kernel,
    pad_len,
    output_weight,
    gain_second,
    up_weight,
    down_weight,
    cotangent,
):
    ways, mesh_rows = lax.axis_size("dp"), lax.axis_size("mp")
    here = lax.axis_index("dp")
    place = here.astype(jnp.int32)[None]
    level = lax.axis_index("mp").astype(jnp.int32)[None]
    x, grad_rows = tokens[0], cotangent[0]
    spots, width = x.shape
    length = spots * mesh_rows
    own_channels, taps = kernel.shape
    rows = own_channels // ways
    hidden = up_weight.shape[1] // ways
    channels = own_channels * mesh_rows
    sizes = dict(mesh_rows=mesh_rows, rows=rows)
    filt_parts = -(-taps // width)

    own_in = lax.dynamic_slice_in_dim(input_weight.transpose(1, 2, 0), here * rows, rows, 1)
    own_out = lax.dynamic_slice_in_dim(output_weight, here * rows, rows, 0)
    own_mixer = jnp.concatenate([own_in, own_out[None]]).reshape(-1, width)
    next_mixer = swap(own_mixer, "mp", 1)
    own_up = lax.dynamic_slice_in_dim(up_weight, here * hidden, hidden, 1).T
    own_down = lax.dynamic_slice_in_dim(down_weight, here * hidden, hidden, 0)
    own_feed = jnp.stack([own_up, own_down])
    own_feed = jnp.broadcast_to(own_feed, (mesh_rows,) + own_feed.shape)
    other_mixers = [swap(after(own_mixer, next_mixer), "mp", i) for i in range(2, mesh_rows)]
    (normed_low,) = whole_call(
        first_norm_forward_kernel, [((spots, width), bf16)], name="first_norm", count=2, room=10
    )(x, gain_first[None])
    first_group = chips_of(stacked(own_mixer, next_mixer))
    other_mixers = [after(part, *first_group[1:], normed_low, tables, own_feed) for part in other_mixers]
    second_group = chips_of(stacked(*other_mixers))
    feed_rows = turn(after(own_feed, *other_mixers))
    mixer = [[far(piece) for piece in pair_of(group)] for group in (first_group, second_group)]

    outs = project(level, normed_low, mixer, mesh_rows)
    mixed_in, (value, gate_one, gate_two, weight_out) = outs[:mesh_rows], outs[mesh_rows:]
    value, gate_one, gate_two = (part.reshape(channels, spots) for part in (value, gate_one, gate_two))
    weight_out = weight_out.reshape(channels, width)
    received = levels_of([part.reshape(own_channels, spots) for part in mixed_in])
    feed_rows = after(feed_rows, value)
    up, down = (feed_rows[:, side].reshape(-1, width) for side in range(2))
    up_x, down_y = swap(up, "dp", 2), swap(down, "dp", 4)
    fspec = filter_slices(place, after(kernel, gate_two), pad_len, tables, length, ways)
    up_x, down_y = after(up_x, *received[1:], fspec), after(down_y, *received[1:], fspec)
    quarter = ((2, mesh_rows * hidden, width), bf16)
    up_pair, down_pair = whole_call(stack_kernel, [quarter] * 2, name="feed_pairs", count=4, room=8)(
        up, up_x, down, down_y
    )
    up_pair, down_pair = swap(up_pair, "dp", 4), swap(down_pair, "dp", 2)
    received = [received[0]] + [after(piece, fspec) for piece in received[1:]]
    *conv_out, uspec = conv_forward(level, received, fspec, tables)
    conv = levels_of(conv_out)
    ups = [after(up_pair, *conv[1:]), up, up_x]
    downs = [after(down_pair, *conv[1:]), down, down_y]
    ups, downs = (
        [pair, swap(pair, "dp", 1), one, two, swap(one, "dp", 1), swap(two, "dp", 1)]
        for pair, one, two in (ups, downs)
    )

    wide, tall = ((spots, width), f32), ((channels, spots), bf16)
    outs = feed_forward(
        level,
        (far(x), far(gate_two), far(weight_out), gain_second[None], far(grad_rows)),
        conv,
        ups,
        downs,
        channels,
    )
    mixer_low, block_out, grad_mid, mid_low, gain_second_grad, grad_two = outs[:6]
    grad_conv, (up_near, down_near, far_grads) = outs[6 : 6 + mesh_rows], outs[6 + mesh_rows :]
    received = levels_of(grad_conv)
    late_shape = ((4, 2 * mesh_rows * rows, width), bf16)
    late_near, late_far = whole_call(
        partial(late_kernel, **sizes), [late_shape] * 2, [((channels, width), f32)], name="late_grads", count=4
    )(far(grad_two), far(normed_low), mixer_low, mid_low)
    half = ((2, mesh_rows, hidden + rows, width), bf16)
    up_keep, up_send, down_keep, down_send = whole_call(
        partial(kept_kernel, hidden=hidden, **sizes), [pltpu.HBM(*half), half] * 2, name="kept", count=5, room=20
    )(up_near, down_near, swap(far_grads, "dp", 1), late_near, swap(late_far, "dp", 1))
    up_in, down_in = swap(up_send, "dp", 2), swap(down_send, "dp", 4)

    received = [received[0]] + [after(piece, up_keep) for piece in received[1:]]
    mixed_out, gspec = conv_mixed(level, received, fspec, tables)
    mixed = turn(mixed_out).reshape(channels, spots)
    filt_grad = conv_filt(gspec, uspec, tables, taps, width, length)
    up_in, down_in = after(up_in, mixed_out), after(down_in, mixed_out)
    up_send, down_send = window_call(
        second_send_kernel,
        [(far(up_keep), (1,)), (up_in, (1,)), (far(down_keep), (1,)), (down_in, (1,))],
        [jax.ShapeDtypeStruct(half[0][1:], bf16)] * 2,
        "second_send",
        12,
    )
    up_last, down_last = swap(up_send, "dp", 4), swap(down_send, "dp", 2)
    rest_rows = (2 * mesh_rows + filt_parts) * rows
    rest_near, rest_far, grad_value, grad_one = whole_call(
        partial(rest_kernel, **sizes),
        [pltpu.HBM((4, rest_rows, width), bf16)] * 2 + [pltpu.HBM(*tall)] * 2,
        [((channels, width), f32)],
        name="rest_grads",
        count=5,
        room=12,
    )(mixed, far(value), far(gate_one), far(normed_low), filt_grad)
    rest = whole_call(split_kernel, [((rest_rows, width), bf16)] * 4, name="rest_kept", count=2)(
        far(rest_near), swap(rest_far, "dp", 1)
    )
    (bulk,) = window_call(
        bulk_kernel,
        [(far(up_keep), (0,)), (up_in, (0,)), (after(up_last, rest_near), ())]
        + [(far(down_keep), (0,)), (down_in, (0,)), (after(down_last, rest_near), ())],
        [pltpu.HBM((mesh_rows, 2 * (hidden + rows), width), bf16)],
        "bulk_sum",
        16,
    )
    bulk = turn(bulk)
    rest = [rest[0]] + [swap(rest[chip], "dp", 2 * chip) for chip in range(1, 4)]
    grad_tokens, gain_first_grad = whole_call(
        partial(first_norm_kernel, **sizes),
        [wide, ((1, width), f32)],
        [((4 * mesh_rows * rows, spots), bf16), wide],
        name="first_norm_back",
        smem=1,
        count=22,
        room=20,
    )(
        level,
        *(far(part.reshape(mesh_rows, own_channels, spots)) for part in (grad_value, grad_one, grad_two)),
        *mixer[0],
        *mixer[1],
        far(x),
        gain_first[None],
        far(grad_mid),
    )
    rest = [rest[0]] + [after(piece, grad_tokens) for piece in rest[1:]]
    own_filt, *rest = whole_call(
        partial(rest_sum_kernel, rows=rows),
        [((filt_parts * rows, width), bf16)] + [((2 * rows + 8, width), bf16)] * mesh_rows,
        name="rest_sum",
        smem=2,
        count=8,
    )(place, level, *rest, kernel, pad_len[:, None], gain_first_grad, gain_second_grad)
    rest = levels_of(rest)
    (mine,) = whole_call(
        rest_mesh_sum_kernel,
        [((bulk.shape[1] + (2 + filt_parts) * rows + 8, width), bf16)],
        name="mesh_sum",
        count=2 + mesh_rows,
        room=8,
    )(after(bulk, *rest[1:]), own_filt, *rest)
    shapes = [up_weight.shape, down_weight.shape, (own_channels, width), (3, own_channels, width), kernel.shape]
    up_grad, down_grad, out_grad, in_grad, kernel_grad, gain_one, gain_two = pl.pallas_call(
        partial(unpack_kernel, hidden=hidden, rows=rows),
        out_shape=[jax.ShapeDtypeStruct(shape, f32) for shape in shapes + [(width,)] * 2],
        in_specs=[SM] + [VM] * 8,
        out_specs=[pl.BlockSpec(memory_space=pl.ANY)] * 5 + [VM] * 2,
        scratch_shapes=[pltpu.VMEM(shape, f32) for shape in shapes + [down_weight.shape, (8, 2, width)]]
        + [pltpu.SemaphoreType.DMA((5,))],
        compiler_params=pltpu.CompilerParams(vmem_limit_bytes=24 << 20),
        name="unpack",
    )(place, *pair_of(chips_of(mine)))
    return (
        block_out[None],
        grad_tokens[None],
        gain_one,
        in_grad.transpose(2, 0, 1),
        kernel_grad,
        out_grad,
        gain_two,
        up_grad,
        down_grad,
    )


def body(tables, *arrays):
    ways = lax.axis_size("dp")
    whole_tiles = arrays[3].shape[0] % (8 * ways) == 0 and arrays[7].shape[1] % (32 * ways) == 0
    assert arrays[0].shape[0] == 1
    return (fast_body if ways == 8 and whole_tiles else plain_body)(tables, *arrays)


def solution(mesh):
    in_specs = (
        P("dp", "mp", None),
        P(),
        P(None, None, "mp"),
        P("mp", None),
        P("mp"),
        P("mp", None),
        P(),
        P(None, "mp"),
        P("mp", None),
        P("dp", "mp", None),
    )
    out_specs = (
        P("dp", "mp", None),
        P("dp", "mp", None),
        P(),
        P(None, None, "mp"),
        P("mp", None),
        P("mp", None),
        P(),
        P(None, "mp"),
        P("mp", None),
    )

    def program(tokens, *rest):
        tables = dft_tables(tokens.shape[1])
        inner = jax.shard_map(
            body, mesh=mesh, in_specs=((P(), P(), P()),) + in_specs, out_specs=out_specs, check_vma=False
        )
        return inner(tables, tokens, *rest)

    return program
```

```python
import math
from functools import partial

import jax
import jax.numpy as jnp
import numpy as np
from jax import lax
from jax.experimental import pallas as pl
from jax.experimental.pallas import tpu as pltpu
from jax.sharding import PartitionSpec as P

LANES = 128
FEED_PACK = 2
ROWS = 16
BASE = 256
f32 = jnp.float32
bf16 = jnp.bfloat16


def dft_tables(length):
    radix = length // BASE
    spot = lax.iota(jnp.int32, BASE)
    angle = (spot[:, None] * spot[None] % BASE).astype(f32) * (2 * math.pi / BASE)
    cos, sin = jnp.cos(angle), jnp.sin(angle)
    matrix = jnp.concatenate(
        [jnp.concatenate([cos, -sin], axis=1), jnp.concatenate([sin, cos], axis=1)], axis=0
    )
    high = matrix.astype(bf16)
    low = (matrix - high.astype(f32)).astype(bf16)
    turn = 2 * np.pi * np.outer(np.arange(radix) + 0.25, np.arange(BASE)) / length
    twiddle = np.stack([np.cos(turn), np.sin(turn)]).astype(np.float32)
    return high, low, jnp.asarray(twiddle)


def times(re, im, angle):
    c, s = math.cos(angle), math.sin(angle)
    if abs(s) < 1e-12:
        return (re, im) if c > 0 else (-re, -im)
    if abs(c) < 1e-12:
        return (-im, re) if s > 0 else (im, -re)
    if abs(abs(c) - abs(s)) < 1e-12:
        a = abs(c)
        sc, ss = (a if c > 0 else -a), (1.0 if (s > 0) == (c > 0) else -1.0)
        if ss > 0:
            return (re - im) * sc, (re + im) * sc
        return (re + im) * sc, (im - re) * sc
    return re * c - im * s, re * s + im * c


def radix_dft(re, im, sign):
    n = len(re)
    if n == 1:
        return re, im
    er, ei = radix_dft(re[0::2], im[0::2], sign)
    odr, odi = radix_dft(re[1::2], im[1::2], sign)
    lo_r, lo_i, hi_r, hi_i = [], [], [], []
    for k in range(n // 2):
        tr, ti = times(odr[k], odi[k], sign * 2 * math.pi * k / n)
        lo_r.append(er[k] + tr)
        lo_i.append(ei[k] + ti)
        hi_r.append(er[k] - tr)
        hi_i.append(ei[k] - ti)
    return lo_r + hi_r, lo_i + hi_i


def split_in(load, twiddle_ref, store, radix, channels):
    def step(tile, carry):
        rows = pl.ds(pl.multiple_of(tile * ROWS, ROWS), ROWS)
        for half in range(BASE // LANES):
            lanes = slice(half * LANES, (half + 1) * LANES)
            re, im = [], []
            for block in range(radix):
                x = load(rows, block, half)
                angle = -2 * math.pi * block * 0.25 / radix
                re.append(x * math.cos(angle))
                im.append(x * math.sin(angle))
            re, im = radix_dft(re, im, -1)
            for k in range(radix):
                c = twiddle_ref[0, k : k + 1, lanes]
                s = twiddle_ref[1, k : k + 1, lanes]
                store(rows, k, half, re[k] * c + im[k] * s, im[k] * c - re[k] * s)
        return carry

    lax.fori_loop(0, channels // ROWS, step, 0)


def split_out(load, twiddle_ref, store, radix, channels, length):
    def step(tile, carry):
        rows = pl.ds(pl.multiple_of(tile * ROWS, ROWS), ROWS)
        for half in range(BASE // LANES):
            lanes = slice(half * LANES, (half + 1) * LANES)
            re, im = [], []
            for k in range(radix):
                vr, vi = load(rows, k, half)
                c = twiddle_ref[0, k : k + 1, lanes]
                s = twiddle_ref[1, k : k + 1, lanes]
                re.append(vr * c - vi * s)
                im.append(vr * s + vi * c)
            re, im = radix_dft(re, im, 1)
            for block in range(radix):
                angle = 2 * math.pi * block * 0.25 / radix
                store(
                    rows,
                    block,
                    half,
                    re[block] * (math.cos(angle) / length) - im[block] * (math.sin(angle) / length),
                )
        return carry

    lax.fori_loop(0, channels // ROWS, step, 0)


def forward_dot(z, matrix):
    return jnp.dot(z, matrix, preferred_element_type=f32)


def inverse_dot(y, matrix):
    return lax.dot_general(y, matrix, (((1,), (1,)), ((), ())), preferred_element_type=f32)


def product_loop(a_load, b_load, store, total_rows, conj):
    def step(tile, carry):
        rows = pl.ds(pl.multiple_of(tile * ROWS, ROWS), ROWS)
        for half in range(BASE // LANES):
            cr = slice(half * LANES, (half + 1) * LANES)
            ci = slice(BASE + half * LANES, BASE + (half + 1) * LANES)
            ar, ai = a_load(rows, cr), a_load(rows, ci)
            br, bi = b_load(rows, cr), b_load(rows, ci)
            if conj:
                store(rows, cr, ar * br + ai * bi)
                store(rows, ci, ai * br - ar * bi)
            else:
                store(rows, cr, ar * br - ai * bi)
                store(rows, ci, ai * br + ar * bi)
        return carry

    lax.fori_loop(0, total_rows // ROWS, step, 0)


def cut(ref, here, rows, block, half):
    width = ref.shape[-1]
    start = block * BASE + half * LANES
    return ref[(start // width) ^ here, rows, start % width : start % width + LANES].astype(f32)


def put(ref, here, rows, block, half, value):
    width = ref.shape[-1]
    start = block * BASE + half * LANES
    ref[(start // width) ^ here, rows, start % width : start % width + LANES] = value.astype(ref.dtype)


def rowshift(rows, k, channels):
    return pl.ds(pl.multiple_of(rows.start + k * channels, ROWS), ROWS)


def into_scratch(ref, channels):
    def store(rows, k, half, re, im):
        at = rowshift(rows, k, channels)
        ref[at, half * LANES : (half + 1) * LANES] = re.astype(ref.dtype)
        ref[at, BASE + half * LANES : BASE + (half + 1) * LANES] = im.astype(ref.dtype)

    return store


def from_scratch(ref, channels):
    def load(rows, k, half):
        at = rowshift(rows, k, channels)
        return (
            ref[at, half * LANES : (half + 1) * LANES].astype(f32),
            ref[at, BASE + half * LANES : BASE + (half + 1) * LANES].astype(f32),
        )

    return load


def filter_kernel(f_ref, high_ref, low_ref, twiddle_ref, spec_ref, zh, zl, *, radix, channels):
    def store(rows, k, half, re, im):
        at = rowshift(rows, k, channels)
        for value, base in ((re, 0), (im, BASE)):
            lanes = slice(base + half * LANES, base + (half + 1) * LANES)
            top = value.astype(bf16)
            zh[at, lanes] = top
            zl[at, lanes] = (value - top.astype(f32)).astype(bf16)

    split_in(partial(cut, f_ref, 0), twiddle_ref, store, radix, channels)
    spec_ref[...] = (
        forward_dot(zh[...], high_ref[...])
        + forward_dot(zl[...], high_ref[...])
        + forward_dot(zh[...], low_ref[...])
    )


def tile_load(ref):
    return lambda rows, lanes: ref[rows, lanes].astype(f32)


def tile_store(ref):
    def store(rows, lanes, value):
        ref[rows, lanes] = value.astype(ref.dtype)

    return store


def conv_kernel(here_ref, *refs, parts, radix, channels, length):
    sent, (fspec_ref, high_ref, twiddle_ref) = refs[:parts], refs[parts : parts + 3]
    outs, (uspec_ref, z, y, big, turned) = refs[parts + 3 : 2 * parts + 3], refs[2 * parts + 3 :]
    here = here_ref[0]
    for i, ref in enumerate(sent):
        turned[i ^ here] = ref[...]
    split_in(partial(cut, turned, 0), twiddle_ref, into_scratch(z, channels), radix, channels)
    big[...] = forward_dot(z[...], high_ref[...])
    uspec_ref[...] = big[...].astype(uspec_ref.dtype)
    product_loop(tile_load(big), tile_load(fspec_ref), tile_store(y), radix * channels, False)
    big[...] = inverse_dot(y[...], high_ref[...])
    split_out(from_scratch(big, channels), twiddle_ref, partial(put, turned, 0), radix, channels, length)
    for i, ref in enumerate(outs):
        ref[...] = turned[i ^ here]


def conv_mixed_kernel(here_ref, *refs, parts, radix, channels, length):
    sent, (fspec_ref, high_ref, twiddle_ref) = refs[:parts], refs[parts : parts + 3]
    mixed_ref, spec_ref, z, y, big, turned = refs[parts + 3 :]
    here = here_ref[0]
    for i, ref in enumerate(sent):
        turned[i ^ here] = ref[...]
    split_in(partial(cut, turned, 0), twiddle_ref, into_scratch(z, channels), radix, channels)
    big[...] = forward_dot(z[...], high_ref[...])
    spec_ref[...] = big[...].astype(bf16)
    product_loop(tile_load(big), tile_load(fspec_ref), tile_store(y), radix * channels, True)
    big[...] = inverse_dot(y[...], high_ref[...])
    split_out(from_scratch(big, channels), twiddle_ref, partial(put, mixed_ref, 0), radix, channels, length)


def conv_filt_kernel(
    gspec_ref, uspec_ref, high_ref, twiddle_ref, filt_ref, y, big, *, radix, channels, length, taps
):
    product_loop(tile_load(gspec_ref), tile_load(uspec_ref), tile_store(y), radix * channels, True)
    big[...] = inverse_dot(y[...], high_ref[...])
    filt_ref[filt_ref.shape[0] - 1] = jnp.zeros(filt_ref.shape[1:], filt_ref.dtype)

    def store(rows, block, half, value):
        if block * BASE + half * LANES < taps:
            put(filt_ref, 0, rows, block, half, value)

    split_out(from_scratch(big, channels), twiddle_ref, store, radix, channels, length)


VM = pl.BlockSpec(memory_space=pltpu.VMEM)
SM = pl.BlockSpec(memory_space=pltpu.SMEM)


def filter_spectrum(filt, tables):
    high, low, twiddle = tables
    channels, length = filt.shape[1], filt.shape[0] * filt.shape[2]
    radix = length // BASE
    rows = radix * channels
    return pl.pallas_call(
        partial(filter_kernel, radix=radix, channels=channels),
        out_shape=jax.ShapeDtypeStruct((rows, 2 * BASE), f32),
        in_specs=[VM] * 4,
        out_specs=VM,
        scratch_shapes=[pltpu.VMEM((rows, 2 * BASE), bf16)] * 2,
        name="filter_spectrum",
    )(filt, high, low, twiddle)


def conv_forward(here, pieces, fspec, tables):
    high, _, twiddle = tables
    parts = len(pieces)
    channels, width = pieces[0].shape
    length = parts * width
    radix = length // BASE
    rows = radix * channels
    return pl.pallas_call(
        partial(conv_kernel, parts=parts, radix=radix, channels=channels, length=length),
        out_shape=[jax.ShapeDtypeStruct((channels, width), bf16)] * parts + [pltpu.HBM((rows, 2 * BASE), bf16)],
        in_specs=[SM] + [VM] * (parts + 3),
        out_specs=[VM] * (parts + 1),
        scratch_shapes=[pltpu.VMEM((rows, 2 * BASE), bf16)] * 2
        + [pltpu.VMEM((rows, 2 * BASE), f32), pltpu.VMEM((parts, channels, width), bf16)],
        compiler_params=pltpu.CompilerParams(vmem_limit_bytes=16 << 20),
        name="conv_forward",
    )(here, *pieces, fspec, high, twiddle)


def conv_mixed(here, pieces, fspec, tables):
    high, _, twiddle = tables
    parts = len(pieces)
    channels, width = pieces[0].shape
    length = parts * width
    radix = length // BASE
    rows = radix * channels
    return pl.pallas_call(
        partial(conv_mixed_kernel, parts=parts, radix=radix, channels=channels, length=length),
        out_shape=(
            pltpu.HBM((parts, channels, width), bf16),
            pltpu.HBM((rows, 2 * BASE), bf16),
        ),
        in_specs=[SM] + [VM] * (parts + 3),
        out_specs=(VM, VM),
        scratch_shapes=[pltpu.VMEM((rows, 2 * BASE), bf16)] * 2
        + [pltpu.VMEM((rows, 2 * BASE), f32), pltpu.VMEM((parts, channels, width), bf16)],
        compiler_params=pltpu.CompilerParams(vmem_limit_bytes=16 << 20),
        name="conv_mixed",
    )(here, *pieces, fspec, high, twiddle)


def conv_filt(gspec, uspec, tables, taps, width, length):
    high, _, twiddle = tables
    rows = gspec.shape[0]
    radix = length // BASE
    channels = rows // radix
    return pl.pallas_call(
        partial(conv_filt_kernel, radix=radix, channels=channels, length=length, taps=taps),
        out_shape=jax.ShapeDtypeStruct((-(-taps // width), channels, width), f32),
        in_specs=[VM] * 4,
        out_specs=VM,
        scratch_shapes=[pltpu.VMEM((rows, 2 * BASE), bf16), pltpu.VMEM((rows, 2 * BASE), f32)],
        compiler_params=pltpu.CompilerParams(vmem_limit_bytes=16 << 20),
        name="conv_filt",
    )(gspec, uspec, high, twiddle)


thresh = 0.003
epsilon = 1e-05
gelu_scale = math.sqrt(2 / math.pi)
gelu_cube = 0.044715


def norm(values):
    centered = values - jnp.mean(values, axis=-1, keepdims=True)
    inverse = lax.rsqrt(jnp.mean(centered * centered, axis=-1, keepdims=True) + epsilon)
    return centered * inverse, inverse


def norm_back(unit, inverse, gain, grad):
    scaled = grad * gain
    mean = jnp.mean(scaled, axis=-1, keepdims=True)
    along = jnp.mean(scaled * unit, axis=-1, keepdims=True)
    return inverse * (scaled - mean - unit * along), jnp.sum(grad * unit, axis=0)


def shrink_pool(kernel, pad_len):
    shrunk = jax.nn.relu(kernel - thresh) - jax.nn.relu(-kernel - thresh)
    padded = jnp.pad(shrunk, ((0, 0), (1, 1)))
    pooled = (padded[:, :-2] + padded[:, 1:-1] + padded[:, 2:]) / 3.0
    positions = lax.broadcasted_iota(jnp.int32, pooled.shape, 1)
    return jnp.where(positions < (pooled.shape[1] - pad_len)[:, None], pooled, 0.0)


def gelu_both(values):
    cubic = gelu_cube * values * values
    turn = jnp.tanh(gelu_scale * (values + cubic * values))
    half = 0.5 * (1 + turn)
    slope = half + 0.5 * values * (1 - turn * turn) * (gelu_scale * (1 + 3 * cubic))
    return values * half, slope


def dot(a, b, over_a, over_b):
    return lax.dot_general(a, b, (((over_a,), (over_b,)), ((), ())), preferred_element_type=f32)


def after(x, *waits):
    return lax.optimization_barrier((x, waits))[0] if waits else x


def swap(x, axis, bit, done=()):
    return after(lax.ppermute(x, axis, [(i, i ^ bit) for i in range(lax.axis_size(axis))]), *done)


def gather(x, axis, stride=1, done=()):
    return jnp.stack([x] + [swap(x, axis, i, done) for i in range(stride, lax.axis_size(axis), stride)])


def scatter(x, axis, stride=1, done=()):
    terms = [x[0]] + [swap(x[i], axis, i * stride, done) for i in range(1, x.shape[0])]
    return sum(term.astype(f32) for term in terms)


class Gather:
    def __init__(self, x, bits):
        self.x, self.held, self.left = x, [], list(bits)

    def step(self, count=1, done=()):
        for bit in self.left[:count]:
            place = sum(other > bit for other in self.held)
            self.x = jnp.stack([self.x, swap(self.x, "dp", 1 << bit, done)], axis=place)
            self.held.append(bit)
        self.left = self.left[count:]
        return self

    def finish(self, done=()):
        self.step(len(self.left), done)
        return self.x.reshape((-1,) + self.x.shape[len(self.held) :])


def narrow_sum(*terms):
    return sum(term.astype(f32) for term in terms).astype(bf16)


class Reduction:
    def __init__(self, x, bits):
        self.x = x.reshape((2,) * len(bits) + x.shape[1:])
        self.held, self.left = sorted(bits, reverse=True), list(bits)

    def step(self, count=1, done=()):
        for bit in self.left[:count]:
            place = self.held.index(bit)
            self.held.remove(bit)
            keep, send = (lax.index_in_dim(self.x, side, place, keepdims=False) for side in (0, 1))
            self.x = narrow_sum(keep, swap(send, "dp", 1 << bit, done))
        self.left = self.left[count:]
        return self

    def finish(self, done=()):
        return self.step(len(self.left), done).x


def sum_all(x):
    for axis in ("dp", "mp"):
        bit = 1
        while bit < lax.axis_size(axis):
            x = x + swap(x, axis, bit)
            bit *= 2
    return x


def parts_of(x, axis, stride=1):
    return [x] + [swap(x, axis, i) for i in range(stride, lax.axis_size(axis), stride)]


def parts_for(x, axis):
    return [x[0]] + [swap(x[i], axis, i) for i in range(1, x.shape[0])]


def turn(x):
    return lax.all_to_all(x, "mp", 0, 0)


def exchange(x, done=()):
    return jnp.stack([x[0]] + [swap(x[i], "mp", i, done) for i in range(1, x.shape[0])])


def spread(x, *orders):
    x = x.astype(bf16)
    if orders:
        half = x.shape[0] // 16 * 8
        x = [Gather(part, bits).finish() for part, bits in zip((x[:half], x[half:]), orders)]
        x = jnp.concatenate(x, axis=1)
    else:
        x = gather(x, "dp", 2)
    return jnp.concatenate([x, swap(x, "dp", 1)])


class Spread:
    def __init__(self, x, *orders):
        half = x.shape[0] // 16 * 8
        self.parts = [Gather(part, bits) for part, bits in zip((x[:half], x[half:]), orders)]

    @property
    def x(self):
        return [part.x for part in self.parts]

    def step(self, done=()):
        for part in self.parts:
            part.step(done=done)

    def finish(self, done=()):
        x = jnp.concatenate([part.finish(done=done) for part in self.parts], axis=1)
        return jnp.concatenate([x, swap(x, "dp", 1)])


class Doubling:
    def __init__(self, x):
        self.x = x
        self.left = [
            (axis, 1 << bit) for axis in ("dp", "mp") for bit in range(lax.axis_size(axis).bit_length() - 1)
        ]

    def step(self):
        if self.left:
            self.x = self.x + swap(self.x, *self.left.pop(0))

    def finish(self):
        while self.left:
            self.step()


def absolute(x, start, rows):
    here = lax.axis_index("dp")
    count = x.shape[0]
    picks = []
    for index in range(count):
        relative = here ^ index
        at = (relative & 1) * (count // 2) + (relative >> 1)
        picks.append(lax.dynamic_slice(x, (at, start, 0), (1, rows, x.shape[2]))[0])
    return jnp.concatenate(picks).astype(f32)


def plain_body(
    tables,
    tokens,
    gain_first,
    input_weight,
    kernel,
    pad_len,
    output_weight,
    gain_second,
    up_weight,
    down_weight,
    cotangent,
):
    ways, rows_mp = lax.axis_size("dp"), lax.axis_size("mp")
    here_dp, here_mp = lax.axis_index("dp"), lax.axis_index("mp")
    chips = list(range(1, ways.bit_length() - 1))
    first_bits, second_bits = chips, chips[::-1]
    here = here_mp.astype(jnp.int32)[None]
    spots, width = tokens.shape[1:]
    length = spots * rows_mp
    own_channels = kernel.shape[0]
    slice_channels = own_channels // ways
    slice_hidden = up_weight.shape[1] // ways
    channels = own_channels * rows_mp

    own_in = lax.dynamic_slice_in_dim(input_weight, here_dp * slice_channels, slice_channels, 2)
    own_out = lax.dynamic_slice_in_dim(output_weight, here_dp * slice_channels, slice_channels, 0)
    mixer_rows = gather(jnp.concatenate([own_in.transpose(1, 2, 0), own_out[None]]), "mp")
    start_rows = tokens[0].astype(f32)
    unit_one, inverse_one = norm(start_rows)
    normed_low = (unit_one * gain_first).astype(bf16)
    own_up = lax.dynamic_slice_in_dim(up_weight, here_dp * slice_hidden, slice_hidden, 1).T
    own_down = lax.dynamic_slice_in_dim(down_weight, here_dp * slice_hidden, slice_hidden, 0)
    own_feed = jnp.stack([own_up, own_down])

    picks = []
    for core in range(2):
        for chip in range(ways // 2):
            at = (here_dp ^ (2 * chip + core)) * slice_channels
            picks.append(at)
    kernel_rel = jnp.concatenate([lax.dynamic_slice_in_dim(kernel, at, slice_channels, 0) for at in picks])
    pad_rel = jnp.concatenate([lax.dynamic_slice_in_dim(pad_len, at, slice_channels, 0) for at in picks])
    filt = shrink_pool(kernel_rel, pad_rel)
    fspec = filter_spectrum(jnp.pad(filt, ((0, 0), (0, length - filt.shape[1])))[None], tables)

    feed_rows = gather(after(own_feed, mixer_rows), "mp")
    mixer_rows = gather(after(mixer_rows, fspec, normed_low, own_feed), "dp", 2)
    feeds = [
        Gather(after(feed_rows[:, side], mixer_rows), bits).step()
        for side, bits in ((0, first_bits), (1, second_bits))
    ]
    mixer_rows = jnp.stack([mixer_rows, swap(mixer_rows, "dp", 1)])
    mixer_weights = mixer_rows.transpose(3, 2, 0, 1, 4, 5)
    weight_in = mixer_weights[:3].reshape(3 * channels, width)
    weight_out = mixer_weights[3].reshape(channels, width)

    proj = dot(weight_in, normed_low, 1, 1).reshape(3, channels, spots)
    value, gate_one, gate_two = proj[0], proj[1], proj[2]
    mixed_in = (value * gate_one).astype(bf16).reshape(rows_mp, own_channels, spots)
    for feed in feeds:
        feed.x = after(feed.x, mixed_in)
        feed.finish()
    *conv_out, uspec = conv_forward(here, list(exchange(mixed_in)), fspec, tables)
    conv_out = jnp.stack(conv_out)
    feeds = [after(feed.x, conv_out).reshape(-1, width) for feed in feeds]
    conv = exchange(conv_out).reshape(channels, spots).astype(f32)
    mixer_low = (gate_two * conv).astype(bf16)
    residual_one = start_rows + dot(mixer_low, weight_out, 0, 0)

    unit_two, inverse_two = norm(residual_one)
    second_low = (unit_two * gain_second).astype(bf16)
    grad_rows = cotangent[0]
    feeds = [[feed, swap(feed, "dp", 1)] for feed in feeds]
    block_out, grad_norm_two = residual_one, 0.0
    up_grads, down_grads = [], []
    for up, down in zip(*feeds):
        act, slope = gelu_both(dot(second_low, up, 1, 1))
        act_low = act.astype(bf16)
        grad_pre = (dot(grad_rows, down, 1, 1) * slope).astype(bf16)
        block_out = block_out + dot(act_low, down, 1, 0)
        grad_norm_two = grad_norm_two + dot(grad_pre, up, 1, 0)
        up_grads.append(dot(grad_pre, second_low, 0, 0).astype(bf16))
        down_grads.append(dot(act_low, grad_rows, 0, 0).astype(bf16))
    grad_mid_norm, gain_second_grad = norm_back(unit_two, inverse_two, gain_second, grad_norm_two)
    grad_mid = grad_rows.astype(f32) + grad_mid_norm
    mid_low = grad_mid.astype(bf16)

    chips_count = ways // 2

    def hidden_sum(parts, bits):
        kept = narrow_sum(parts[0], swap(parts[1], "dp", 1))
        return Reduction(kept.reshape(chips_count, rows_mp, slice_hidden, width), bits)

    down_sum = hidden_sum(down_grads, second_bits)
    up_sum = hidden_sum(up_grads, first_bits)

    def by_slice(parts):
        parts = [part.astype(bf16).reshape(rows_mp, 2, chips_count, slice_channels, width) for part in parts]
        return jnp.concatenate(parts, axis=3).transpose(1, 2, 0, 3, 4)

    grad_mixer = dot(weight_out, mid_low, 1, 1)
    grad_conv = (grad_mixer * gate_two).astype(bf16).reshape(rows_mp, own_channels, spots)
    grad_conv = exchange(grad_conv)
    grad_gate_two = (grad_mixer * conv).astype(bf16)
    out_grad = dot(mixer_low, mid_low, 1, 0)
    late = by_slice([dot(grad_gate_two, normed_low, 1, 0), out_grad])
    late = narrow_sum(late[0], swap(late[1], "dp", 1))
    grad_conv = after(grad_conv, down_sum.x, up_sum.x, late)
    mixed_out, gspec = conv_mixed(here, list(grad_conv), fspec, tables)
    filt_grad = conv_filt(gspec, uspec, tables, length, length, length)
    mixed_out = jnp.take(mixed_out, lax.iota(jnp.int32, rows_mp) ^ here_mp, axis=0)
    down_sum.step()
    up_sum.step()
    late = scatter(late, "dp", 2).astype(bf16)
    grad_mixed = exchange(mixed_out).reshape(channels, spots).astype(f32)
    grad_mixed = after(grad_mixed, down_sum.x, up_sum.x, late)
    grad_value = (grad_mixed * gate_one).astype(bf16)
    grad_gate_one = (grad_mixed * value).astype(bf16)
    rest = by_slice([dot(grad, normed_low, 1, 0) for grad in (grad_value, grad_gate_one)])
    grad_norm_one = dot(jnp.concatenate([grad_value, grad_gate_one, grad_gate_two]), weight_in, 0, 0)
    grad_start, gain_first_grad = norm_back(unit_one, inverse_one, gain_first, grad_norm_one)
    grad_tokens = grad_mid + grad_start

    taps = kernel.shape[1]
    filt_grad = filt_grad[0, :, :taps].astype(bf16).reshape(2, chips_count, -1, width)
    rest = jnp.concatenate([rest.reshape(2, chips_count, -1, width), filt_grad], axis=2)
    rest = scatter(narrow_sum(rest[0], swap(rest[1], "dp", 1)), "dp", 2)
    split = rest.shape[0] - filt_grad.shape[2]
    own_kernel = lax.dynamic_slice_in_dim(kernel, here_dp * slice_channels, slice_channels, 0)
    own_pad = lax.dynamic_slice_in_dim(pad_len, here_dp * slice_channels, slice_channels, 0)
    _, filter_back = jax.vjp(partial(shrink_pool, pad_len=own_pad), own_kernel)
    (own_filt,) = filter_back(rest[split:].reshape(slice_channels, taps))
    rest = scatter(rest[:split].astype(bf16).reshape(rows_mp, 2 * slice_channels, width), "mp")
    rest = spread(jnp.concatenate([rest, own_filt.reshape(-1, width)]))
    bulk = jnp.concatenate([up_sum.finish(), down_sum.finish(), late], axis=1)
    bulk = spread(scatter(bulk, "mp"))

    up_grad = absolute(bulk, 0, slice_hidden).T
    down_grad = absolute(bulk, slice_hidden, slice_hidden)
    in_grad = [
        absolute(rest, 0, slice_channels),
        absolute(rest, slice_channels, slice_channels),
        absolute(bulk, 2 * slice_hidden, slice_channels),
    ]
    in_full = jnp.stack(in_grad).transpose(2, 0, 1)
    out_full = absolute(bulk, 2 * slice_hidden + slice_channels, slice_channels)
    kernel_grad = absolute(rest, 2 * slice_channels, filt_grad.shape[2]).reshape(own_channels, taps)

    gains = sum_all(jnp.stack([gain_first_grad, gain_second_grad]))
    return (
        block_out.astype(bf16)[None],
        grad_tokens[None],
        gains[0],
        in_full,
        kernel_grad,
        out_full,
        gains[1],
        up_grad,
        down_grad,
    )


def whole_call(kernel, outs, scratch=(), name=None, smem=0, count=0, room=6):
    return pl.pallas_call(
        kernel,
        out_shape=tuple(out if isinstance(out, pl.MemoryRef) else jax.ShapeDtypeStruct(*out) for out in outs),
        in_specs=[SM] * smem + [VM] * count,
        out_specs=tuple(VM for _ in outs),
        scratch_shapes=[pltpu.VMEM(shape, dtype) for shape, dtype in scratch],
        compiler_params=pltpu.CompilerParams(vmem_limit_bytes=room << 20),
        name=name,
    )


def relative_index(here, place, count):
    chip, core = place % (count // 2), place // (count // 2)
    return here ^ (2 * chip + core)


def filter_slices_kernel(
    here_ref, kernel_ref, pad_ref, high_ref, low_ref, twiddle_ref, spec_ref, filt, zh, zl, *, radix, channels, ways
):
    here = here_ref[0]
    rows = channels // ways
    taps = kernel_ref.shape[1]
    filt[...] = jnp.zeros_like(filt)
    spot = lax.broadcasted_iota(jnp.int32, (8, taps), 1)

    def step(tile, carry):
        place = tile // (rows // 8)
        start = relative_index(here, place, ways) * rows + (tile % (rows // 8)) * 8
        at = pl.ds(pl.multiple_of(start, 8), 8)
        raw = kernel_ref[at, :]
        shrunk = jnp.maximum(raw - thresh, 0.0) - jnp.maximum(-raw - thresh, 0.0)
        before = jnp.where(spot == 0, 0.0, pltpu.roll(shrunk, 1, 1))
        behind = jnp.where(spot == taps - 1, 0.0, pltpu.roll(shrunk, taps - 1, 1))
        pooled = (before + shrunk + behind) / 3.0
        filt[0, pl.ds(pl.multiple_of(tile * 8, 8), 8), :taps] = jnp.where(spot < taps - pad_ref[at, :], pooled, 0.0)
        return carry

    lax.fori_loop(0, channels // 8, step, 0)
    filter_kernel(filt, high_ref, low_ref, twiddle_ref, spec_ref, zh, zl, radix=radix, channels=channels)


def filter_slices(here, kernel, pad_len, tables, length, ways):
    high, low, twiddle = tables
    channels = kernel.shape[0]
    radix = length // BASE
    rows = radix * channels
    return whole_call(
        partial(filter_slices_kernel, radix=radix, channels=channels, ways=ways),
        [((rows, 2 * BASE), f32)],
        [((1, channels, length), f32), ((rows, 2 * BASE), bf16), ((rows, 2 * BASE), bf16)],
        name="filter_spectrum",
        smem=1,
        count=5,
        room=14,
    )(here, far(kernel), pad_len[:, None], far(high), far(low), far(twiddle))[0]


def nt(a, b):
    return dot(a, b, 1, 1)


def tn(a, b):
    return dot(a, b, 0, 0)


def first_norm_forward_kernel(x_ref, gain_ref, low_ref):
    unit, _ = norm(x_ref[...].astype(f32))
    low_ref[...] = (unit * gain_ref[...]).astype(bf16)


def project_kernel(level_ref, low_ref, *refs, rows, mesh_rows):
    groups, sends = (refs[:8], refs[8:16]), refs[16 : 16 + mesh_rows]
    v_ref, one_ref, two_ref, out_ref, weights, sems = refs[16 + mesh_rows :]
    step = pl.program_id(0)

    def weight_copy(group, source, slot):
        size = source.shape[0]
        start = group * groups[0][0].shape[0]
        return pltpu.make_async_copy(source, weights.at[slot, pl.ds(start, size), :], sems.at[group, slot])

    @pl.when(step == 0)
    def _():
        for chip in range(4):
            for core in range(2):
                for group, pieces in enumerate(groups):
                    weight_copy(group, pieces[core * 4 + chip], 2 * chip + core).start()

    for core in range(2):
        for group, pieces in enumerate(groups):
            weight_copy(group, pieces[0], 2 * step + core).wait()
    size = weights.shape[1]
    proj = nt(weights[pl.ds(2 * step, 2)].reshape(2 * size, weights.shape[2]), low_ref[...])
    for core in range(2):
        for i, send_ref in enumerate(sends):
            to = i ^ level_ref[0]
            at = 4 * i * rows
            start = core * size + at
            value, one, two = (proj[start + k * rows : start + (k + 1) * rows] for k in range(3))
            send_ref[core, 0] = (value * one).astype(bf16)
            v_ref[to, core, 0] = value
            one_ref[to, core, 0] = one
            two_ref[to, core, 0] = two
            out_ref[to, core, 0] = weights[2 * step + core, at + 3 * rows : at + 4 * rows, :]


def project(level, low, groups, mesh_rows):
    spots, width = low.shape
    size = sum(group[0].shape[0] for group in groups)
    rows = size // (4 * mesh_rows)
    block = lambda last: pl.BlockSpec((mesh_rows, 2, 1, rows, last), lambda j: (0, 0, j, 0, 0))
    shape = lambda last, dtype: pltpu.HBM((mesh_rows, 2, 4, rows, last), dtype)
    return pl.pallas_call(
        partial(project_kernel, rows=rows, mesh_rows=mesh_rows),
        grid=(4,),
        in_specs=[SM, VM] + [pl.BlockSpec(memory_space=pl.ANY)] * 16,
        out_specs=[pl.BlockSpec((2, 1, rows, spots), lambda j: (0, j, 0, 0))] * mesh_rows
        + [block(spots)] * 3
        + [block(width)],
        out_shape=[pltpu.HBM((2, 4, rows, spots), bf16)] * mesh_rows
        + [shape(spots, f32)] * 3
        + [shape(width, bf16)],
        scratch_shapes=[pltpu.VMEM((8, size, width), bf16), pltpu.SemaphoreType.DMA((2, 8))],
        compiler_params=pltpu.CompilerParams(vmem_limit_bytes=18 << 20),
        name="project",
    )(level, low, *groups[0], *groups[1])


def stack_kernel(*refs):
    for index, out_ref in enumerate(refs[len(refs) // 3 * 2 :]):
        out_ref[0] = refs[2 * index][...]
        out_ref[1] = refs[2 * index + 1][...]


def feed_kernel(*refs, mesh_rows):
    here_ref, x_ref, two_ref, out_weight_ref, gain_ref, grad_ref = refs[:6]
    sent, refs = refs[6 : 6 + mesh_rows], refs[6 + mesh_rows :]
    ups, downs, up_firsts, down_firsts = refs[:2], refs[2:4], refs[4:8], refs[8:12]
    mixer_ref, block_ref, mid_ref, mid_low_ref, gain_grad_ref, grad_two_ref = refs[12:18]
    sends, refs = refs[18 : 18 + mesh_rows], refs[18 + mesh_rows :]
    up_near, down_near, far_grads = refs[:3]
    residual, second, out_acc, norm_acc, conv, turned, weights, grads, sems, grad_sems = refs[3:]
    step = pl.program_id(0)
    size = weights.shape[2]
    pack = grads.shape[2] // size
    copies = []
    for side, (firsts, pairs) in enumerate(((up_firsts, ups), (down_firsts, downs))):
        for k in range(8):
            core, chip = divmod(k, 4)
            first = (0, 1) if side == 0 else (0, 2)
            if chip in first:
                source = firsts[2 * core + first.index(chip)]
            else:
                source = pairs[core].at[0 if chip == (2 if side == 0 else 1) else 1]
            copies.append(pltpu.make_async_copy(source, weights.at[side, k], sems.at[side, k]))

    @pl.when(step == 0)
    def _():
        for copy in copies:
            copy.start()
        for i, ref in enumerate(sent):
            conv[i ^ here_ref[0]] = ref[...]
        mixer_ref[...] = (two_ref[...] * conv[...].reshape(two_ref.shape).astype(f32)).astype(bf16)
        residual[...] = x_ref[...].astype(f32) + tn(mixer_ref[...], out_weight_ref[...])
        unit, _ = norm(residual[...])
        second[...] = (unit * gain_ref[...]).astype(bf16)
        out_acc[...] = residual[...]
        norm_acc[...] = jnp.zeros_like(norm_acc)

    for side in range(2):
        for k in range(pack):
            at = step * pack + k
            pltpu.make_async_copy(up_firsts[0], weights.at[side, at], sems.at[side, at]).wait()
    slot = step % 2

    @pl.when(step >= 2)
    def _():
        for side in range(2):
            pltpu.make_async_copy(
                grads.at[side, slot], up_near.at[pl.ds(0, pack * size), :], grad_sems.at[side, slot]
            ).wait()

    width = second.shape[1]
    up, down = (weights[side, pl.ds(step * pack, pack)].reshape(pack * size, width) for side in range(2))
    act, slope = gelu_both(nt(second[...], up))
    act_low = act.astype(bf16)
    grad_pre = (nt(grad_ref[...], down) * slope).astype(bf16)
    out_acc[...] += dot(act_low, down, 1, 0)
    norm_acc[...] += dot(grad_pre, up, 1, 0)
    grads[0, slot] = tn(grad_pre, second[...]).astype(bf16)
    grads[1, slot] = tn(act_low, grad_ref[...]).astype(bf16)
    steps = 4 // pack
    at = pl.ds(pl.multiple_of((step % steps) * pack * size, size), pack * size)
    for core, outs in enumerate(((up_near, down_near), (far_grads.at[0], far_grads.at[1]))):

        @pl.when(step // steps == core)
        def _():
            for side in range(2):
                pltpu.make_async_copy(
                    grads.at[side, slot], outs[side].at[at, :], grad_sems.at[side, slot]
                ).start()

    @pl.when(step == pl.num_programs(0) - 1)
    def _():
        unit, inverse = norm(residual[...])
        grad, gain_grad = norm_back(unit, inverse, gain_ref[...], norm_acc[...])
        gain_grad_ref[...] = gain_grad[None]
        mid = grad_ref[...].astype(f32) + grad
        mid_ref[...] = mid
        mid_low_ref[...] = mid.astype(bf16)
        block_ref[...] = out_acc[...].astype(bf16)
        grad_mixer = nt(out_weight_ref[...], mid_low_ref[...])
        flat = conv[...].reshape(two_ref.shape)
        grad_two_ref[...] = (grad_mixer * flat.astype(f32)).astype(bf16)
        turned[...] = (grad_mixer * two_ref[...]).astype(bf16).reshape(turned.shape)
        for i, ref in enumerate(sends):
            ref[...] = turned[i ^ here_ref[0]]
        for side in range(2):
            for last in range(2):
                pltpu.make_async_copy(
                    grads.at[side, last], up_near.at[pl.ds(0, pack * size), :], grad_sems.at[side, last]
                ).wait()


def feed_forward(here, wholes, conv, ups, downs, channels):
    mesh_rows = len(conv)
    size, width = ups[2].shape
    spots = wholes[0].shape[0]
    shape = jax.ShapeDtypeStruct
    tall = shape((channels, spots), bf16)
    piece = shape((channels // mesh_rows, spots), bf16)
    anywhere = pl.BlockSpec(memory_space=pl.ANY)
    return pl.pallas_call(
        partial(feed_kernel, mesh_rows=mesh_rows),
        grid=(8 // FEED_PACK,),
        in_specs=[SM] + [VM] * (len(wholes) + mesh_rows) + [anywhere] * 12,
        out_specs=[VM] * (6 + mesh_rows) + [anywhere] * 3,
        out_shape=[
            tall,
            pltpu.HBM((spots, width), bf16),
            pltpu.HBM((spots, width), f32),
            shape((spots, width), bf16),
            shape((1, width), f32),
            pltpu.HBM((channels, spots), bf16),
        ]
        + [piece] * mesh_rows
        + [shape((4 * size, width), bf16)] * 2
        + [shape((2, 4 * size, width), bf16)],
        scratch_shapes=[
            pltpu.VMEM((spots, width), f32),
            pltpu.VMEM((spots, width), bf16),
            pltpu.VMEM((spots, width), f32),
            pltpu.VMEM((spots, width), f32),
            pltpu.VMEM((mesh_rows, channels // mesh_rows, spots), bf16),
            pltpu.VMEM((mesh_rows, channels // mesh_rows, spots), bf16),
            pltpu.VMEM((2, 8, size, width), bf16),
            pltpu.VMEM((2, 2, FEED_PACK * size, width), bf16),
            pltpu.SemaphoreType.DMA((2, 8)),
            pltpu.SemaphoreType.DMA((2, 2)),
        ],
        compiler_params=pltpu.CompilerParams(vmem_limit_bytes=38 << 20),
        name="feed_forward",
    )(here, *wholes, *conv, *ups[:2], *downs[:2], *ups[2:], *downs[2:])


def put_slices(out_refs, rows_at, product, mesh_rows, rows):
    for i in range(mesh_rows):
        for core in range(2):
            for chip in range(4):
                start = ((i * 2 + core) * 4 + chip) * rows
                at = rows_at(i)
                out_refs[core][chip, at : at + rows, :] = product[start : start + rows, :].astype(bf16)


def late_kernel(grad_two_ref, low_ref, mixer_ref, mid_low_ref, near_ref, far_ref, product, *, mesh_rows, rows):
    for kind, pair in enumerate(((mixer_ref, mid_low_ref), (grad_two_ref, low_ref))):
        product[...] = dot(pair[0][...], pair[1][...], 1, 0)
        put_slices((near_ref, far_ref), lambda i: (2 * i + kind) * rows, product, mesh_rows, rows)


def rest_kernel(
    mixed_ref, value_ref, one_ref, low_ref, filt_ref, near_ref, far_ref, grad_value_ref, grad_one_ref, product,
    *, mesh_rows, rows,
):
    mixed = mixed_ref[...].astype(f32)
    grad_value_ref[...] = (mixed * one_ref[...]).astype(bf16)
    grad_one_ref[...] = (mixed * value_ref[...]).astype(bf16)
    for kind, grad_ref in enumerate((grad_value_ref, grad_one_ref)):
        product[...] = dot(grad_ref[...], low_ref[...], 1, 0)
        put_slices((near_ref, far_ref), lambda i: (2 * i + kind) * rows, product, mesh_rows, rows)
    base = 2 * mesh_rows * rows
    for part in range(filt_ref.shape[0]):
        for core, ref in enumerate((near_ref, far_ref)):
            for chip in range(4):
                start = (core * 4 + chip) * rows
                at = base + part * rows
                ref[chip, at : at + rows, :] = filt_ref[part, start : start + rows, :].astype(bf16)


def first_norm_kernel(level_ref, *refs, mesh_rows, rows):
    grads, groups = refs[:3], (refs[3:11], refs[11:19])
    x_ref, gain_ref, mid_ref, tokens_ref, gain_grad_ref, gathered, acc = refs[19:]
    split = groups[0][0].shape[0]
    for slot in range(8):
        for i in range(mesh_rows):
            start = slot * rows
            for k, grad_ref in enumerate(grads):
                at = (i * 4 + k) * rows
                gathered[at : at + rows, :] = grad_ref[i ^ level_ref[0], start : start + rows, :]
            at = (i * 4 + 3) * rows
            gathered[at : at + rows, :] = jnp.zeros((rows, gathered.shape[1]), bf16)
        term = tn(gathered[:split], groups[0][slot][...]) + tn(gathered[split:], groups[1][slot][...])
        acc[...] = term if slot == 0 else acc[...] + term
    unit, inverse = norm(x_ref[...].astype(f32))
    grad, gain_grad = norm_back(unit, inverse, gain_ref[...], acc[...])
    tokens_ref[...] = mid_ref[...] + grad
    gain_grad_ref[...] = gain_grad[None]


def add_low(*terms):
    return sum(term.astype(f32) for term in terms).astype(bf16)


def kept_kernel(
    up_ref, down_ref, far_in, late_ref, late_in, up_keep, up_send, down_keep, down_send, *, mesh_rows, hidden, rows
):
    for chip in range(4):
        for i in range(mesh_rows):
            at = slice((chip * mesh_rows + i) * hidden, (chip * mesh_rows + i + 1) * hidden)
            late = [slice((2 * i + kind) * rows, (2 * i + kind + 1) * rows) for kind in range(2)]
            out_ref, side = (up_send if chip & 1 else up_keep), chip >> 1
            out_ref[side, i, :hidden] = add_low(up_ref[at, :], far_in[0, at, :])
            out_ref[side, i, hidden:] = add_low(late_ref[chip, late[0], :], late_in[chip, late[0], :])
            out_ref, side = (down_send if chip >> 1 else down_keep), chip & 1
            out_ref[side, i, :hidden] = add_low(down_ref[at, :], far_in[1, at, :])
            out_ref[side, i, hidden:] = add_low(late_ref[chip, late[1], :], late_in[chip, late[1], :])


def window_call(kernel, windows, outs, name, room):
    def spec(x, lead):
        shape = (None,) * len(lead) + x.shape[len(lead) :]
        return pl.BlockSpec(shape, lambda n: tuple(lead) + (0,) * (len(x.shape) - len(lead)))

    return pl.pallas_call(
        kernel,
        grid=(1,),
        in_specs=[spec(x, lead) for x, lead in windows],
        out_specs=[VM] * len(outs),
        out_shape=list(outs),
        compiler_params=pltpu.CompilerParams(vmem_limit_bytes=room << 20),
        name=name,
    )(*(x for x, _ in windows))


def second_send_kernel(up_ref, up_in, down_ref, down_in, up_send, down_send):
    up_send[...] = add_low(up_ref[...], up_in[...])
    down_send[...] = add_low(down_ref[...], down_in[...])


def bulk_kernel(up_ref, up_in, up_last, down_ref, down_in, down_last, bulk_ref):
    mesh_rows, size = up_ref.shape[:2]
    for i in range(mesh_rows):
        bulk_ref[i, :size] = add_low(up_ref[i], up_in[i], up_last[i])
        bulk_ref[i, size:] = add_low(down_ref[i], down_in[i], down_last[i])


def split_kernel(near_ref, far_ref, *outs):
    for chip, out_ref in enumerate(outs):
        out_ref[...] = add_low(near_ref[chip], far_ref[chip])


def split_gain(gain):
    high = gain.astype(bf16)
    return high, (gain - high.astype(f32)).astype(bf16)


def rest_sum_kernel(
    here_ref, level_ref, p0, p1, p2, p3, kernel_ref, pad_ref, gain_one_ref, gain_two_ref, filt_ref, *sends, rows
):
    mesh_rows = len(sends)
    size, width = sends[0].shape
    size = size - 8
    pairs = [split_gain(ref[...]) for ref in (gain_one_ref, gain_two_ref)]
    gains = jnp.concatenate([pair[part].astype(f32) for part in range(2) for pair in pairs], axis=0)
    gains = jnp.concatenate([gains, jnp.zeros_like(gains)], axis=0).astype(bf16)
    for i, ref in enumerate(sends):
        at = pl.ds(pl.multiple_of((i ^ level_ref[0]) * size, 16), size)
        ref[:size] = add_low(*(part[at, :] for part in (p0, p1, p2, p3)))
        ref[size:] = gains
    taps = kernel_ref.shape[1]
    base = mesh_rows * size
    parts = filt_ref.shape[0] // rows
    grad = [
        sum(ref[base + part * rows : base + (part + 1) * rows, :].astype(f32) for ref in (p0, p1, p2, p3))
        for part in range(parts)
    ]
    grad = jnp.concatenate(grad, axis=1)[:, :taps]
    at = pl.ds(pl.multiple_of(here_ref[0] * rows, rows), rows)
    spot = lax.broadcasted_iota(jnp.int32, (rows, taps), 1)
    grad = jnp.where(spot < taps - pad_ref[at, :], grad, 0.0)
    before = jnp.where(spot == 0, 0.0, pltpu.roll(grad, 1, 1))
    behind = jnp.where(spot == taps - 1, 0.0, pltpu.roll(grad, taps - 1, 1))
    grad = jnp.where(jnp.abs(kernel_ref[at, :]) > thresh, (before + grad + behind) / 3.0, 0.0)
    for part in range(parts):
        size = min(width, taps - part * width)
        piece = grad[:, part * width : part * width + size].astype(bf16)
        filt_ref[part * rows : (part + 1) * rows, :size] = piece
        if size < width:
            filt_ref[part * rows : (part + 1) * rows, size:] = jnp.zeros((rows, width - size), bf16)


def mesh_sum_kernel(x_ref, out_ref):
    out_ref[...] = add_low(*(x_ref[i] for i in range(x_ref.shape[0])))


def tree_sum(terms):
    while len(terms) > 1:
        terms = [a + b for a, b in zip(terms[0::2], terms[1::2])]
    return terms[0]


def rest_mesh_sum_kernel(bulk_ref, filt_ref, *refs):
    sent, out_ref = refs[:-1], refs[-1]
    base = bulk_ref.shape[1]
    size = sent[0].shape[0] - 8
    filt = filt_ref.shape[0]
    mesh_sum_kernel(bulk_ref, out_ref.at[:base])
    out_ref[base : base + size] = add_low(*(ref[:size] for ref in sent))
    out_ref[base + size : base + size + filt] = filt_ref[...]
    gains = [ref[size:].astype(f32) for ref in sent]
    gains = tree_sum([gain[:2] + gain[2:4] for gain in gains])
    high, low = split_gain(gains)
    zeros = jnp.zeros((4, gains.shape[1]), f32)
    out_ref[base + size + filt :] = jnp.concatenate(
        [high.astype(f32), low.astype(f32), zeros], axis=0
    ).astype(bf16)


def slice_at(here, slot, rows):
    start = (here ^ (2 * (slot % 4) + slot // 4)) * rows
    return pl.ds(pl.multiple_of(start, 8), rows)


def unpack_kernel(here_ref, *refs, hidden, rows):
    pieces, outs, gain_refs = refs[:8], refs[8:13], refs[13:15]
    held, (turned, gains, sems) = refs[15:20], refs[20:]
    up, down, out, given, kernel = held
    copies = [pltpu.make_async_copy(source, to, sems.at[k]) for k, (source, to) in enumerate(zip(held, outs))]
    here = here_ref[0]
    width = given.shape[2]
    taps = kernel.shape[1]
    parts = -(-taps // width)
    for slot, ref in enumerate(pieces):
        turned[slice_at(here, slot, hidden), :] = ref[:hidden].astype(f32)
    up[...] = turned[...].T
    copies[0].start()
    for slot, ref in enumerate(pieces):
        start = hidden + rows
        down[slice_at(here, slot, hidden), :] = ref[start : start + hidden].astype(f32)
    copies[1].start()
    start = 2 * hidden + rows
    for slot, ref in enumerate(pieces):
        at = slice_at(here, slot, rows)
        out[at, :] = ref[hidden : hidden + rows].astype(f32)
        for place, gate in enumerate((2, 0, 1)):
            given[gate, at, :] = ref[start + place * rows : start + (place + 1) * rows].astype(f32)
    copies[2].start()
    copies[3].start()
    for slot, ref in enumerate(pieces):
        at = slice_at(here, slot, rows)
        for part in range(parts):
            size = min(width, taps - part * width)
            block = ref[start + (3 + part) * rows : start + (4 + part) * rows].astype(f32)
            kernel[at, part * width : part * width + size] = block[:, :size]
        gain = ref[start + (3 + parts) * rows :].astype(f32)
        gains[relative_index(here, slot, 8)] = gain[:2] + gain[2:4]
    copies[4].start()
    total = sum(gains[slot] for slot in range(8))
    for row, ref in enumerate(gain_refs):
        ref[...] = total[row]
    for copy in copies:
        copy.wait()


def chips_of(x, done=()):
    return [x] + [swap(x, "dp", 2 * chip, done) for chip in range(1, 4)]


def far(x):
    return pltpu.with_memory_space_constraint(x, pltpu.HBM)


def levels_of(pieces):
    return [pieces[0]] + [swap(pieces[i], "mp", i) for i in range(1, len(pieces))]


def stacked(*parts):
    shape = (len(parts),) + parts[0].shape
    (out,) = whole_call(stack_kernel, [(shape, bf16)], name="mixer_group", count=len(parts))(*parts)
    return out.reshape(-1, shape[-1])


def pair_of(pieces, done=()):
    return pieces + [swap(piece, "dp", 1, done) for piece in pieces]


def fast_body(
    tables,
    tokens,
    gain_first,
    input_weight,
    kernel,
    pad_len,
    output_weight,
    gain_second,
    up_weight,
    down_weight,
    cotangent,
):
    ways, mesh_rows = lax.axis_size("dp"), lax.axis_size("mp")
    here = lax.axis_index("dp")
    place = here.astype(jnp.int32)[None]
    level = lax.axis_index("mp").astype(jnp.int32)[None]
    x, grad_rows = tokens[0], cotangent[0]
    spots, width = x.shape
    length = spots * mesh_rows
    own_channels, taps = kernel.shape
    rows = own_channels // ways
    hidden = up_weight.shape[1] // ways
    channels = own_channels * mesh_rows
    sizes = dict(mesh_rows=mesh_rows, rows=rows)
    filt_parts = -(-taps // width)

    own_in = lax.dynamic_slice_in_dim(input_weight.transpose(1, 2, 0), here * rows, rows, 1)
    own_out = lax.dynamic_slice_in_dim(output_weight, here * rows, rows, 0)
    own_mixer = jnp.concatenate([own_in, own_out[None]]).reshape(-1, width)
    next_mixer = swap(own_mixer, "mp", 1)
    own_up = lax.dynamic_slice_in_dim(up_weight, here * hidden, hidden, 1).T
    own_down = lax.dynamic_slice_in_dim(down_weight, here * hidden, hidden, 0)
    own_feed = jnp.stack([own_up, own_down])
    own_feed = jnp.broadcast_to(own_feed, (mesh_rows,) + own_feed.shape)
    other_mixers = [swap(after(own_mixer, next_mixer), "mp", i) for i in range(2, mesh_rows)]
    (normed_low,) = whole_call(
        first_norm_forward_kernel, [((spots, width), bf16)], name="first_norm", count=2, room=10
    )(x, gain_first[None])
    first_group = chips_of(stacked(own_mixer, next_mixer))
    other_mixers = [after(part, *first_group[1:], normed_low, tables, own_feed) for part in other_mixers]
    second_group = chips_of(stacked(*other_mixers))
    feed_rows = turn(after(own_feed, *other_mixers))
    mixer = [[far(piece) for piece in pair_of(group)] for group in (first_group, second_group)]

    outs = project(level, normed_low, mixer, mesh_rows)
    mixed_in, (value, gate_one, gate_two, weight_out) = outs[:mesh_rows], outs[mesh_rows:]
    value, gate_one, gate_two = (part.reshape(channels, spots) for part in (value, gate_one, gate_two))
    weight_out = weight_out.reshape(channels, width)
    received = levels_of([part.reshape(own_channels, spots) for part in mixed_in])
    feed_rows = after(feed_rows, value)
    up, down = (feed_rows[:, side].reshape(-1, width) for side in range(2))
    up_x, down_y = swap(up, "dp", 2), swap(down, "dp", 4)
    fspec = filter_slices(place, after(kernel, gate_two), pad_len, tables, length, ways)
    up_x, down_y = after(up_x, *received[1:], fspec), after(down_y, *received[1:], fspec)
    quarter = ((2, mesh_rows * hidden, width), bf16)
    up_pair, down_pair = whole_call(stack_kernel, [quarter] * 2, name="feed_pairs", count=4, room=8)(
        up, up_x, down, down_y
    )
    up_pair, down_pair = swap(up_pair, "dp", 4), swap(down_pair, "dp", 2)
    received = [received[0]] + [after(piece, fspec) for piece in received[1:]]
    *conv_out, uspec = conv_forward(level, received, fspec, tables)
    conv = levels_of(conv_out)
    ups = [after(up_pair, *conv[1:]), up, up_x]
    downs = [after(down_pair, *conv[1:]), down, down_y]
    ups, downs = (
        [pair, swap(pair, "dp", 1), one, two, swap(one, "dp", 1), swap(two, "dp", 1)]
        for pair, one, two in (ups, downs)
    )

    wide, tall = ((spots, width), f32), ((channels, spots), bf16)
    outs = feed_forward(
        level,
        (far(x), far(gate_two), far(weight_out), gain_second[None], far(grad_rows)),
        conv,
        ups,
        downs,
        channels,
    )
    mixer_low, block_out, grad_mid, mid_low, gain_second_grad, grad_two = outs[:6]
    grad_conv, (up_near, down_near, far_grads) = outs[6 : 6 + mesh_rows], outs[6 + mesh_rows :]
    received = levels_of(grad_conv)
    late_shape = ((4, 2 * mesh_rows * rows, width), bf16)
    late_near, late_far = whole_call(
        partial(late_kernel, **sizes), [late_shape] * 2, [((channels, width), f32)], name="late_grads", count=4
    )(far(grad_two), far(normed_low), mixer_low, mid_low)
    half = ((2, mesh_rows, hidden + rows, width), bf16)
    up_keep, up_send, down_keep, down_send = whole_call(
        partial(kept_kernel, hidden=hidden, **sizes), [pltpu.HBM(*half), half] * 2, name="kept", count=5, room=20
    )(up_near, down_near, swap(far_grads, "dp", 1), late_near, swap(late_far, "dp", 1))
    up_in, down_in = swap(up_send, "dp", 2), swap(down_send, "dp", 4)

    received = [received[0]] + [after(piece, up_keep) for piece in received[1:]]
    mixed_out, gspec = conv_mixed(level, received, fspec, tables)
    mixed = turn(mixed_out).reshape(channels, spots)
    filt_grad = conv_filt(gspec, uspec, tables, taps, width, length)
    up_in, down_in = after(up_in, mixed_out), after(down_in, mixed_out)
    up_send, down_send = window_call(
        second_send_kernel,
        [(far(up_keep), (1,)), (up_in, (1,)), (far(down_keep), (1,)), (down_in, (1,))],
        [jax.ShapeDtypeStruct(half[0][1:], bf16)] * 2,
        "second_send",
        12,
    )
    up_last, down_last = swap(up_send, "dp", 4), swap(down_send, "dp", 2)
    rest_rows = (2 * mesh_rows + filt_parts) * rows
    rest_near, rest_far, grad_value, grad_one = whole_call(
        partial(rest_kernel, **sizes),
        [pltpu.HBM((4, rest_rows, width), bf16)] * 2 + [pltpu.HBM(*tall)] * 2,
        [((channels, width), f32)],
        name="rest_grads",
        count=5,
        room=12,
    )(mixed, far(value), far(gate_one), far(normed_low), filt_grad)
    rest = whole_call(split_kernel, [((rest_rows, width), bf16)] * 4, name="rest_kept", count=2)(
        far(rest_near), swap(rest_far, "dp", 1)
    )
    (bulk,) = window_call(
        bulk_kernel,
        [(far(up_keep), (0,)), (up_in, (0,)), (after(up_last, rest_near), ())]
        + [(far(down_keep), (0,)), (down_in, (0,)), (after(down_last, rest_near), ())],
        [pltpu.HBM((mesh_rows, 2 * (hidden + rows), width), bf16)],
        "bulk_sum",
        16,
    )
    bulk = turn(bulk)
    rest = [rest[0]] + [swap(rest[chip], "dp", 2 * chip) for chip in range(1, 4)]
    grad_tokens, gain_first_grad = whole_call(
        partial(first_norm_kernel, **sizes),
        [wide, ((1, width), f32)],
        [((4 * mesh_rows * rows, spots), bf16), wide],
        name="first_norm_back",
        smem=1,
        count=22,
        room=20,
    )(
        level,
        *(far(part.reshape(mesh_rows, own_channels, spots)) for part in (grad_value, grad_one, grad_two)),
        *mixer[0],
        *mixer[1],
        far(x),
        gain_first[None],
        far(grad_mid),
    )
    rest = [rest[0]] + [after(piece, grad_tokens) for piece in rest[1:]]
    own_filt, *rest = whole_call(
        partial(rest_sum_kernel, rows=rows),
        [((filt_parts * rows, width), bf16)] + [((2 * rows + 8, width), bf16)] * mesh_rows,
        name="rest_sum",
        smem=2,
        count=8,
    )(place, level, *rest, kernel, pad_len[:, None], gain_first_grad, gain_second_grad)
    rest = levels_of(rest)
    (mine,) = whole_call(
        rest_mesh_sum_kernel,
        [((bulk.shape[1] + (2 + filt_parts) * rows + 8, width), bf16)],
        name="mesh_sum",
        count=2 + mesh_rows,
        room=8,
    )(after(bulk, *rest[1:]), own_filt, *rest)
    shapes = [up_weight.shape, down_weight.shape, (own_channels, width), (3, own_channels, width), kernel.shape]
    up_grad, down_grad, out_grad, in_grad, kernel_grad, gain_one, gain_two = pl.pallas_call(
        partial(unpack_kernel, hidden=hidden, rows=rows),
        out_shape=[jax.ShapeDtypeStruct(shape, f32) for shape in shapes + [(width,)] * 2],
        in_specs=[SM] + [VM] * 8,
        out_specs=[pl.BlockSpec(memory_space=pl.ANY)] * 5 + [VM] * 2,
        scratch_shapes=[pltpu.VMEM(shape, f32) for shape in shapes + [down_weight.shape, (8, 2, width)]]
        + [pltpu.SemaphoreType.DMA((5,))],
        compiler_params=pltpu.CompilerParams(vmem_limit_bytes=24 << 20),
        name="unpack",
    )(place, *pair_of(chips_of(mine)))
    return (
        block_out[None],
        grad_tokens[None],
        gain_one,
        in_grad.transpose(2, 0, 1),
        kernel_grad,
        out_grad,
        gain_two,
        up_grad,
        down_grad,
    )


def body(tables, *arrays):
    ways = lax.axis_size("dp")
    whole_tiles = arrays[3].shape[0] % (8 * ways) == 0 and arrays[7].shape[1] % (32 * ways) == 0
    assert arrays[0].shape[0] == 1
    return (fast_body if ways == 8 and whole_tiles else plain_body)(tables, *arrays)


def solution(mesh):
    in_specs = (
        P("dp", "mp", None),
        P(),
        P(None, None, "mp"),
        P("mp", None),
        P("mp"),
        P("mp", None),
        P(),
        P(None, "mp"),
        P("mp", None),
        P("dp", "mp", None),
    )
    out_specs = (
        P("dp", "mp", None),
        P("dp", "mp", None),
        P(),
        P(None, None, "mp"),
        P("mp", None),
        P("mp", None),
        P(),
        P(None, "mp"),
        P("mp", None),
    )

    def program(tokens, *rest):
        tables = dft_tables(tokens.shape[1])
        inner = jax.shard_map(
            body, mesh=mesh, in_specs=((P(), P(), P()),) + in_specs, out_specs=out_specs, check_vma=False
        )
        return inner(tables, tokens, *rest)

    return program
```
